32 devices in a mesh: res: 8 (over z, y), mp: 4 (over x, core).
Axes of the slice: x: 2, y: 2, z: 4, core: 2. Of those that a mesh axis runs over, the one named last changes fastest.
Arguments:
- nodes: float32 [1536, 512], P('res'), may hold values from -6 to 6
- edges: float32 [1536, 6912], P('res'), may hold values from -6 to 6
- neighbours: int32 [1536, 36], P('res'), may hold values from 0 to 1535, as said below
- edge_mask: int32 [1536, 36], P('res'), may hold values from 0 to 1, as said below
- msg_in: bfloat16 [1216, 512], P(None, 'mp'), may hold values from -0.15625 to 0.15625
- msg_out: bfloat16 [512, 512], P('mp'), may hold values from -0.25 to 0.25
- gain_a: float32 [512], replicated, may hold values from 0.5 to 1.5
- ffn_in: bfloat16 [512, 2048], P(None, 'mp'), may hold values from -0.25 to 0.25
- ffn_out: bfloat16 [2048, 512], P('mp'), may hold values from -0.125 to 0.125
- gain_b: float32 [512], replicated, may hold values from 0.5 to 1.5
- edge_in: bfloat16 [1216, 768], P(None, 'mp'), may hold values from -0.15625 to 0.15625
- edge_out: bfloat16 [768, 192], P('mp'), may hold values from -0.21875 to 0.21875
- gain_c: float32 [192], replicated, may hold values from 0.5 to 1.5
- node_cot: float32 [1536, 512], P('res'), may hold values from -6 to 6
- edge_cot: float32 [1536, 6912], P('res'), may hold values from -6 to 6
Outputs:
- new_nodes: float32 [1536, 512], P('res')
- new_edges: float32 [1536, 6912], P('res')
- node_grad: float32 [1536, 512], P(('res', 'mp'))
- edge_grad: float32 [1536, 6912], P(('res', 'mp'))
- msg_in_grad: float32 [1216, 512], P(None, 'mp')
- msg_out_grad: float32 [512, 512], P('mp')
- gain_a_grad: float32 [512], replicated
- ffn_in_grad: float32 [512, 2048], P(None, 'mp')
- ffn_out_grad: float32 [2048, 512], P('mp')
- gain_b_grad: float32 [512], replicated
- edge_in_grad: float32 [1216, 768], P(None, 'mp')
- edge_out_grad: float32 [768, 192], P('mp')
- gain_c_grad: float32 [192], replicated
The draws below stay inside these ranges and needn't reach their ends.
Inputs may be any that keep to these rules, and one draw needn't show every extreme that they name: `neighbours`: each edge of residue i leads to a residue at most 192 places from i, clamped to the residues that exist. `edge_mask`: some residues have all their edges 0.
All inputs are finite; a program needn't handle non-finite values.
Results may differ from the reference program's by a relative error of at most 0.024.
Values may be sent and summed in bfloat16 or wider, within the bound.
A program may use at most 128 MiB of HBM per device.

```python
import jax
import jax.numpy as jnp
from jax import lax

D = 512
DE = 192
FF = 2048
HM = 512
HE = 768
K = 36
RD = 192
R = 1536


def draw_neighbours(key, part):
    offsets = jnp.concatenate([jnp.arange(-RD, 0), jnp.arange(1, RD + 1)]).astype(jnp.int32)
    scores = jax.random.randint(jax.random.fold_in(key, 11), (R, 2 * RD), 0, 1 << 20) * (2 * RD) + jnp.arange(2 * RD, dtype=jnp.int32)[None, :]
    ranking = jnp.argsort(scores, axis=1)[:, :K]
    picked = jnp.arange(R, dtype=jnp.int32)[:, None] + offsets[ranking]
    return jnp.clip(picked, 0, R - 1).astype(jnp.int32)


def draw_edge_mask(key, part):
    first_key, second_key = jax.random.split(jax.random.fold_in(key, 7))
    missing = jax.random.randint(first_key, (R, 1), 0, 16) == 0
    live_edges = jax.random.randint(second_key, (R, K), 0, 8) != 0
    return jnp.where(missing, 0, live_edges.astype(jnp.int32)).astype(jnp.int32)


def levels(stream_key, extent, cuts, low, top_value):
    level = 1.0
    for dim, parts in cuts:
        steps = jax.random.uniform(jax.random.fold_in(jax.random.fold_in(stream_key, 6), dim), (parts,), jnp.float32, low / len(cuts), top_value / len(cuts))
        level = level * jnp.repeat(jnp.exp(steps), extent[dim] // parts).reshape((-1,) + (1,) * (len(extent) - 1 - dim))
    return level


def noise(stream_key, dims, deviation, reach, cuts=(), held_as=jnp.bfloat16):
    loudness = levels(stream_key, dims, cuts, -0.22, 0.18) if cuts else 1.0
    array = jax.random.normal(stream_key, dims, jnp.float32) * deviation * loudness
    return jnp.minimum(jnp.maximum(array, -reach), reach).astype(held_as)


def setup_inputs(seed: int = 0) -> dict:
    key_of = jax.random.split(jax.random.key(seed), 16)
    return {
        "nodes": noise(key_of[0], (R, D), 1.0, 6.0, ((0, 8),), jnp.float32),
        "edges": noise(key_of[1], (R, K * DE), 1.0, 6.0, ((0, 8),), jnp.float32),
        "neighbours": draw_neighbours(jax.random.fold_in(key_of[15], 71), 0),
        "edge_mask": draw_edge_mask(jax.random.fold_in(key_of[15], 71), 0),
        "msg_in": noise(key_of[4], (2 * D + DE, HM), (2 * D + DE) ** -0.5, 0.15625, ((1, 4),)),
        "msg_out": noise(key_of[5], (HM, D), HM ** -0.5, 0.25, ((0, 4),)),
        "gain_a": jnp.clip(1.0 + 0.1 * jax.random.normal(key_of[6], (D,), jnp.float32), 0.5, 1.5),
        "ffn_in": noise(key_of[7], (D, FF), D ** -0.5, 0.25, ((1, 4),)),
        "ffn_out": noise(key_of[8], (FF, D), FF ** -0.5, 0.125, ((0, 4),)),
        "gain_b": jnp.clip(1.0 + 0.1 * jax.random.normal(key_of[9], (D,), jnp.float32), 0.5, 1.5),
        "edge_in": noise(key_of[10], (2 * D + DE, HE), (2 * D + DE) ** -0.5, 0.15625, ((1, 4),)),
        "edge_out": noise(key_of[11], (HE, DE), HE ** -0.5, 0.21875, ((0, 4),)),
        "gain_c": jnp.clip(1.0 + 0.1 * jax.random.normal(key_of[12], (DE,), jnp.float32), 0.5, 1.5),
        "node_cot": noise(key_of[13], (R, D), 1.0, 6.0, ((0, 8),), jnp.float32),
        "edge_cot": noise(key_of[14], (R, K * DE), 1.0, 6.0, ((0, 8),), jnp.float32),
    }


@jax.custom_vjp
def low(v):
    return lax.optimization_barrier(v.astype(jnp.bfloat16)).astype(jnp.float32)

@jax.custom_vjp
def low_back(v):
    return v

def low_keep(v):
    return (low(v), None)

def low_pass(kept, grad):
    return (grad,)

def back_keep(v):
    return (v, None)

def back_low(kept, grad):
    return (low(grad),)
low.defvjp(low_keep, low_pass)
low_back.defvjp(back_keep, back_low)
EPSILON = 1e-05

def matmul(left_side, right_side):
    return jnp.dot(left_side, right_side, precision=lax.Precision.HIGHEST, preferred_element_type=jnp.float32)

def layer_norm(values, norm_gain):
    centred = values - lax.optimization_barrier(jnp.mean(values, axis=-1, keepdims=True))
    return centred * lax.rsqrt(lax.optimization_barrier(jnp.mean(centred * centred, axis=-1, keepdims=True)) + EPSILON) * norm_gain

def smooth(values):
    return jax.nn.gelu(values, approximate=False)

def node_pass(states, edge_states, neighbours, weights_mean, params):
    msg_in, msg_out, gain_a, ffn_in, ffn_out, gain_b = params
    node_width = states.shape[1]
    residues = edge_states.shape[0]
    degree = edge_states.shape[1]
    low_states = low(states)
    self_term = low_back(matmul(low_states, msg_in[:node_width]))
    other_term = low_back(matmul(low_states, msg_in[node_width:2 * node_width]))
    edge_term = matmul(low(edge_states.reshape(residues * degree, -1)), msg_in[2 * node_width:]).reshape(residues, degree, -1)
    before = low_back(self_term[:, None, :] + other_term[neighbours] + edge_term)
    averaged = lax.optimization_barrier(jnp.sum(smooth(before) * weights_mean[:, :, None], axis=1))
    gathered = low_back(matmul(low(averaged), msg_out))
    middle = layer_norm(states + gathered, gain_a)
    hidden = low_back(matmul(low(middle), ffn_in))
    update = low_back(matmul(low(smooth(hidden)), ffn_out))
    return layer_norm(middle + update, gain_b)

def edge_pass(states, edge_states, neighbours, params):
    edge_in, edge_out, gain_c = params
    node_width = states.shape[1]
    residues = edge_states.shape[0]
    degree = edge_states.shape[1]
    low_states = low(states)
    self_term = low_back(matmul(low_states, edge_in[:node_width]))
    other_term = low_back(matmul(low_states, edge_in[node_width:2 * node_width]))
    edge_term = matmul(low(edge_states.reshape(residues * degree, -1)), edge_in[2 * node_width:]).reshape(residues, degree, -1)
    before = low_back(self_term[:, None, :] + other_term[neighbours] + edge_term)
    activity = smooth(before).reshape(residues * degree, -1)
    update = low_back(matmul(low(activity), edge_out)).reshape(residues, degree, -1)
    return layer_norm(edge_states + update, gain_c)

def reference(nodes, edges, neighbours, edge_mask, msg_in, msg_out, gain_a, ffn_in, ffn_out, gain_b, edge_in, edge_out, gain_c, node_cot, edge_cot):
    residues = nodes.shape[0]
    degree = neighbours.shape[1]
    edge_states = edges.reshape(residues, degree, -1)
    live_edges = edge_mask.astype(jnp.float32)
    weights_mean = live_edges / jnp.maximum(lax.optimization_barrier(jnp.sum(live_edges, axis=1, keepdims=True)), 1.0)
    params = (msg_in.astype(jnp.float32), msg_out.astype(jnp.float32), gain_a, ffn_in.astype(jnp.float32), ffn_out.astype(jnp.float32), gain_b, edge_in.astype(jnp.float32), edge_out.astype(jnp.float32), gain_c)
    predicted = node_pass(nodes, edge_states, neighbours, weights_mean, params[:6])
    settled = node_pass(0.5 * (nodes + predicted), edge_states, neighbours, weights_mean, params[:6])
    guess = edge_pass(settled, edge_states, neighbours, params[6:])

    def forward(node_input, edge_input, *weights):
        new_states = node_pass(0.5 * (node_input + predicted), edge_input, neighbours, weights_mean, weights[:6])
        new_edge_states = edge_pass(new_states, 0.5 * (edge_input + guess), neighbours, weights[6:])
        return (new_states, new_edge_states)
    outputs, pullback = jax.vjp(forward, nodes, edge_states, *params)
    gradients = pullback((node_cot, edge_cot.reshape(residues, degree, -1)))
    return (outputs[0], outputs[1].reshape(residues, -1), gradients[0], gradients[1].reshape(residues, -1), gradients[2], gradients[3], gradients[4], gradients[5], gradients[6], gradients[7], gradients[8], gradients[9], gradients[10])
```

```python
import functools
import math
from types import SimpleNamespace

import jax
import jax.numpy as jnp
from jax import lax
from jax.experimental import pallas as pl
from jax.experimental.pallas import tpu as pltpu
from jax.sharding import PartitionSpec as P

EPSILON = 1e-05
F32 = jnp.float32
BF16 = jnp.bfloat16
MESH = pl.DeviceIdType.MESH
ROOT_TWO_PI = 0.3989422804014327
SCALE = 0.3275911 * 0.7071067811865476
TAIL = (0.127414796, -0.142248368, 0.7107068705, -0.7265760135, 0.5307027145)
ANY = pl.BlockSpec(memory_space=pl.ANY)
VMEM = pl.BlockSpec(memory_space=pltpu.VMEM)


def dot(left, right):
    return jnp.dot(left, right, preferred_element_type=F32)


def dot_bt(left, right):
    return lax.dot_general(left, right, (((1,), (1,)), ((), ())), preferred_element_type=F32)


def dot_at(left, right):
    return lax.dot_general(left, right, (((0,), (0,)), ((), ())), preferred_element_type=F32)


def bell(v):
    t = 1.0 / (1.0 + SCALE * jnp.abs(v))
    fall = jnp.exp(-0.5 * (v * v))
    poly = TAIL[4]
    for c in (TAIL[3], TAIL[2], TAIL[1], TAIL[0]):
        poly = c + t * poly
    tail = t * poly * fall
    return jnp.where(v >= 0.0, 1.0 - tail, tail), fall


def norm_parts(values, width):
    scale = 1.0 / width
    centred = values - jnp.sum(values, axis=-1, keepdims=True) * scale
    inverse = lax.rsqrt(jnp.sum(centred * centred, axis=-1, keepdims=True) * scale + EPSILON)
    return centred * inverse, inverse


def norm_back(upstream, normed, inverse, gain, width):
    scale = 1.0 / width
    scaled = upstream * gain
    mean = jnp.sum(scaled, axis=-1, keepdims=True) * scale
    along = jnp.sum(scaled * normed, axis=-1, keepdims=True) * scale
    return inverse * (scaled - mean - normed * along)


def up(rows, step):
    return -(-rows // step) * step


class Net:
    def __init__(self, send, recv, local):
        self.send, self.recv, self.local = send, recv, local
        self.remote_count = 0
        self.local_count = 0

    def remote(self, src, dst, side="", **where):
        i = self.remote_count
        self.remote_count += 1
        return pltpu.make_async_remote_copy(
            src_ref=src,
            dst_ref=dst,
            send_sem=self.send.at[i],
            recv_sem=self.recv.at[i],
            device_id=where,
            device_id_type=MESH,
        )

    def reserve(self, count):
        i = self.remote_count
        self.remote_count += count
        return i

    def at(self, i, src, dst, **where):
        return pltpu.make_async_remote_copy(
            src_ref=src,
            dst_ref=dst,
            send_sem=self.send.at[i],
            recv_sem=self.recv.at[i],
            device_id=where,
            device_id_type=MESH,
        )

    def opened(self, i, src, dst, **where):
        return self.at(i, src, dst, **where)

    def copy(self, src, dst):
        i = self.local_count
        self.local_count += 1
        c = pltpu.make_async_copy(src, dst, self.local.at[i])
        c.start()
        return c


def kernel_body(S, in_names, out_names, scratch_names, *refs):
    names = in_names + out_names + scratch_names
    A = SimpleNamespace(**dict(zip(names, refs, strict=True)))
    net = Net(A.send, A.recv, A.local)
    RB, RQ, K, D, DE, HM, HE, FL = S.RB, S.RQ, S.K, S.D, S.DE, S.HM, S.HE, S.FL
    E = RQ * K
    W = 3 * RB
    EC = 6 * RQ
    res = lax.axis_index("res")
    mp = lax.axis_index("mp")
    has_l = res > 0
    has_r = res < S.n_res - 1
    pair = mp + 1 - 2 * (mp % 2)
    cross = (mp + 2) % 4
    third = (pair + 2) % 4

    def peer(d):
        return (mp + d) % 4

    def rows_at(start, size, step=16):
        return pl.ds(pl.multiple_of(start, step), size)

    def quarter(q, base=0):
        return rows_at(base + RQ * q, RQ)

    load_nodes = net.copy(A.nodes, A.nodes_v)
    load_nbr = net.copy(A.neighbours, A.nbr_v)
    load_mask = net.copy(A.edge_mask, A.mask_v)
    load_edges = net.copy(A.edges.at[quarter(mp)], A.e_v)
    own_msg_in = A.Wm.at[:, pl.ds(pl.multiple_of(mp * 128, 128), 128)]
    load_msg_in = net.copy(A.msg_in, own_msg_in)
    own_msg_out = A.Wo.at[rows_at(mp * 128, 128)]
    load_msg_out = net.copy(A.msg_out, own_msg_out)
    load_ffn_in = net.copy(A.ffn_in, A.fi_v)
    load_ffn_out = net.copy(A.ffn_out, A.fo_v)
    big, small = HE // 4 // 3 * 2, HE // 4 // 3

    def main_rows(ref):
        return lambda q: ref.at[rows_at(big * q, big)]

    def rest_rows(ref):
        return lambda q: ref.at[rows_at(4 * big + small * q, small)]

    first, rest = pl.ds(0, big), pl.ds(big, small)
    edge_parts = (
        (A.edge_in.at[first], main_rows(A.We)),
        (A.edge_out.at[first], main_rows(A.Eo)),
        (A.edge_in.at[rest], rest_rows(A.We)),
        (A.edge_out.at[rest], rest_rows(A.Eo)),
    )
    load_edge_weights = [net.copy(src, place(mp)) for src, place in edge_parts]
    load_node_cot = net.copy(A.node_cot.at[quarter(mp)], A.nc_v)
    load_edge_cot = net.copy(A.edge_cot.at[quarter(mp)], A.ec_v)

    barrier = pltpu.get_barrier_semaphore()

    def greet(**where):
        pl.semaphore_signal(barrier, inc=1, device_id=where, device_id_type=MESH)

    def across(s):
        return res + (1 << s) * (1 - 2 * ((res // (1 << s)) % 2))

    for d in (1, 2, 3):
        greet(mp=peer(d))
    for s in range(S.bits):
        greet(res=across(s))

    @pl.when(has_l)
    def _():
        greet(res=res - 1)

    @pl.when(has_r)
    def _():
        greet(res=res + 1)

    sides = (res + S.n_res - 1) // S.n_res + 1 - (res + 1) // S.n_res
    pl.semaphore_wait(barrier, 3 + S.bits + sides)

    class Spread:
        def __init__(self, src, place):
            own = place(mp)
            self.first = [net.remote(src, own, mp=pair), net.remote(src, own, mp=cross)]
            self.then = net.remote(place(cross), place(cross), mp=pair)

        def start(self):
            for c in self.first:
                c.start()

        def forward(self):
            self.first[1].wait_recv()
            self.then.start()

        def wait(self):
            self.first[0].wait_recv()
            self.then.wait_recv()

        def sent(self):
            for c in self.first:
                c.wait_send()
            self.then.wait_send()

    spread_msg_in = Spread(
        A.msg_in, lambda q: A.Wm.at[:, pl.ds(pl.multiple_of(q * 128, 128), 128)]
    )
    spread_msg_out = Spread(A.msg_out, lambda q: A.Wo.at[rows_at(q * 128, 128)])
    spread_edge = [Spread(src, place) for src, place in edge_parts]

    def clear_sides(win):
        @pl.when(jnp.logical_not(has_l))
        def _():
            win[0:RB] = jnp.zeros((RB, D), BF16)

        @pl.when(jnp.logical_not(has_r))
        def _():
            win[2 * RB : 3 * RB] = jnp.zeros((RB, D), BF16)

    half = RB // 2

    class Halo:
        def __init__(self, win):
            h = mp % 2
            own = win.at[rows_at(RB + half * h, half)]
            left = win.at[rows_at(half * h, half)]
            right = win.at[rows_at(2 * RB + half * h, half)]
            self.to_l = net.remote(own, right, side="l", res=res - 1)
            self.to_r = net.remote(own, left, side="r", res=res + 1)
            self.on_l = net.remote(left, left, mp=pair)
            self.on_r = net.remote(right, right, mp=pair)

        def start(self):
            pl.when(has_l)(self.to_l.start)
            pl.when(has_r)(self.to_r.start)

        def forward(self):
            @pl.when(has_l)
            def _():
                self.to_r.wait_recv()
                self.on_l.start()

            @pl.when(has_r)
            def _():
                self.to_l.wait_recv()
                self.on_r.start()

        def wait(self):
            pl.when(has_l)(self.on_l.wait_recv)
            pl.when(has_r)(self.on_r.wait_recv)

        def sent(self):
            @pl.when(has_l)
            def _():
                self.to_l.wait_send()
                self.on_l.wait_send()

            @pl.when(has_r)
            def _():
                self.to_r.wait_send()
                self.on_r.wait_send()

    class Window:
        def __init__(self, win):
            own = win.at[quarter(mp, RB)]
            left = win.at[quarter(mp)]
            right = win.at[quarter(mp, 2 * RB)]
            self.to_l = net.remote(own, right, side="l", res=res - 1)
            self.to_r = net.remote(own, left, side="r", res=res + 1)
            self.mine = [net.remote(own, own, mp=peer(d)) for d in (1, 2, 3)]
            self.on_l = [net.remote(left, left, mp=peer(d)) for d in (1, 2, 3)]
            self.on_r = [net.remote(right, right, mp=peer(d)) for d in (1, 2, 3)]

        def start(self):
            pl.when(has_l)(self.to_l.start)
            pl.when(has_r)(self.to_r.start)
            for c in self.mine:
                c.start()

        def forward(self):
            @pl.when(has_l)
            def _():
                self.to_r.wait_recv()
                for c in self.on_l:
                    c.start()

            @pl.when(has_r)
            def _():
                self.to_l.wait_recv()
                for c in self.on_r:
                    c.start()

        def wait_own(self):
            for c in self.mine:
                c.wait_recv()

        def wait(self):
            @pl.when(has_l)
            def _():
                for c in self.on_l:
                    c.wait_recv()

            @pl.when(has_r)
            def _():
                for c in self.on_r:
                    c.wait_recv()

        def sent(self):
            for c in self.mine:
                c.wait_send()

            @pl.when(has_l)
            def _():
                self.to_l.wait_send()
                for c in self.on_l:
                    c.wait_send()

            @pl.when(has_r)
            def _():
                self.to_r.wait_send()
                for c in self.on_r:
                    c.wait_send()

    def gather_rows(buf):
        own = buf.at[quarter(mp)]
        copies = [net.remote(own, own, mp=peer(d)) for d in (1, 2, 3)]
        for c in copies:
            c.start()
        return copies

    def scatter_sum_start(buf, into):
        copies = [
            net.remote(buf.at[quarter(peer(d))], into.at[d - 1], mp=peer(d)) for d in (1, 2, 3)
        ]
        for c in copies:
            c.start()
        return copies

    def landed(copies):
        for c in copies:
            c.wait_recv()

    late = []

    def return_rows(product, send, recv, side_send, side_recv, fill, between):
        for blk in range(3):
            part = product(blk)
            for q in range(4):
                send[q, blk] = part[RQ * q : RQ * q + RQ].astype(BF16)
        copies = [net.remote(send.at[peer(d)], recv.at[d - 1], mp=peer(d)) for d in (1, 2, 3)]
        for c in copies:
            c.start()
        fill()
        landed(copies)
        late.extend(copies)

        def total(blk):
            out = send[mp, blk].astype(F32)
            for d in range(3):
                out = out + recv[d, blk].astype(F32)
            return out

        side_send[0] = total(0).astype(BF16)
        side_send[1] = total(2).astype(BF16)
        to_l = net.remote(side_send.at[0], side_recv.at[1], side="l", res=res - 1)
        to_r = net.remote(side_send.at[1], side_recv.at[0], side="r", res=res + 1)
        pl.when(has_l)(to_l.start)
        pl.when(has_r)(to_r.start)
        mid = total(1)
        between()
        pl.when(has_l)(to_r.wait_recv)
        pl.when(has_r)(to_l.wait_recv)
        pl.when(has_l)(to_l.wait_send)
        pl.when(has_r)(to_r.wait_send)
        return mid + side_recv[0].astype(F32) + side_recv[1].astype(F32)

    spread_msg_in.start()
    spread_msg_out.start()
    load_nodes.wait()

    @pl.loop(0, RB // 16)
    def _(i):
        A.win1[rows_at(RB + 16 * i, 16)] = A.nodes_v[rows_at(16 * i, 16)].astype(BF16)

    halo = Halo(A.win1)
    halo.start()
    for win in (A.win1, A.win2, A.win3):
        clear_sides(win)
    for ref in (A.back_side_a, A.back_side_b):
        ref[...] = jnp.zeros_like(ref)

    load_nbr.wait()
    load_mask.wait()
    load_edges.wait()
    stack = jnp.concatenate(
        [A.nbr_v[...].astype(F32), A.mask_v[...].astype(F32), jnp.zeros((128 - 2 * K, RB), F32)],
        axis=0,
    )
    stack = jnp.concatenate([stack, jnp.zeros((128, 256 - RB), F32)], axis=1)
    A.columns[...] = jnp.transpose(stack)[0:RB]
    columns = A.columns[rows_at(RQ * mp, RQ)]
    local = columns[:, 0:K].astype(jnp.int32) - (res - 1) * RB + DE
    live = columns[:, K : 2 * K]
    mean_weight = live / jnp.maximum(jnp.sum(live, axis=1, keepdims=True), 1.0)
    lane256 = lax.broadcasted_iota(jnp.int32, (RQ, 256), 1)
    lane512 = lax.broadcasted_iota(jnp.int32, (RQ, 512), 1) + 256
    is_edge = lane256 < DE

    def pair_load(buf, base):
        even = buf[:, pl.ds(base, 256)]
        odd = pltpu.roll(buf[:, pl.ds(base + 128, 256)], 192, 1)
        return jnp.where(is_edge, even, 0.0), jnp.where(is_edge, odd, 0.0)

    def pair_store(buf, base, even, odd, sub=slice(None)):
        back = pltpu.roll(odd, 64, 1)
        buf[sub, pl.ds(base, 128)] = even[:, :128].astype(buf.dtype)
        buf[sub, pl.ds(base + 128, 128)] = (even[:, 128:] + back[:, :128]).astype(buf.dtype)
        buf[sub, pl.ds(base + 256, 128)] = back[:, 128:].astype(buf.dtype)

    for j in range(K // 2):
        both = pair_load(A.e_v, 384 * j)
        for p in range(2):
            k = 2 * j + p
            column = local[:, k : k + 1]
            hot = jnp.where(column == lane256, 1.0, 0.0)
            A.XE[RQ * k : RQ * k + RQ] = jnp.where(is_edge, both[p], hot).astype(BF16)
            A.XO[RQ * k : RQ * k + RQ] = jnp.where(column == lane512, 1.0, 0.0).astype(BF16)
            A.WB[RQ * k : RQ * k + RQ] = jnp.broadcast_to(mean_weight[:, k : k + 1], (RQ, 128))

    halo.forward()

    full = E // 128

    @pl.loop(0, full)
    def _(c):
        at = pl.ds(pl.multiple_of(128 * c, 128), 128)
        A.XT[0:256, at] = A.XE[at].T
        A.XT[256:768, at] = A.XO[at].T

    if E % 128:
        at = slice(full * 128, E)
        A.XT[0:256, at] = A.XE[at].T
        A.XT[256:768, at] = A.XO[at].T

    spread_msg_in.forward()
    spread_msg_out.forward()
    halo.wait()

    gain_a = A.gain_a[...]
    gain_b = A.gain_b[...]
    load_msg_in.wait()
    load_msg_out.wait()

    def node_table(win):
        for blk in (1, 0, 2):
            part = dot(win[RB * blk : RB * blk + RB], A.Wm[D : 2 * D])
            A.T[DE + RB * blk : DE + RB * blk + RB] = part.astype(BF16)

    def message_mean(win, keep):
        A.selfs[...] = dot(win[quarter(mp, RB)], A.Wm[0:D])
        A.total[...] = jnp.zeros((RQ, HM), F32)

        @pl.loop(0, E // EC)
        def _(c):
            rows = rows_at(EC * c, EC)
            left = jnp.concatenate([A.XE[rows], A.XO[rows]], axis=1)
            A.base[:, 0:HM] = dot(left, A.T[...])

            @pl.loop(0, RQ // 16)
            def _(sub):
                own = rows_at(16 * sub, 16)
                mine = A.selfs[own]
                total = A.total[own]
                for k in range(6):
                    v = A.base[rows_at(RQ * k + 16 * sub, 16), 0:HM] + mine
                    at = rows_at(EC * c + RQ * k + 16 * sub, 16)
                    w = jnp.concatenate([A.WB[at]] * (HM // 128), axis=1)
                    phi, fall = bell(v)
                    if keep:
                        A.slope[at] = (w * (phi + v * fall * ROOT_TWO_PI)).astype(BF16)
                    total = total + w * (v * phi)
                A.total[own] = total

        A.avg[...] = A.total[...].astype(BF16)

    def node_tail(states, ug, part_b, part_r, keep):
        normed_a, inverse_a = norm_parts(states + dot(A.avg[...], A.Wo[...]), D)
        middle = normed_a * gain_a
        ug[quarter(mp)] = middle.astype(BF16)
        moved = gather_rows(ug)
        landed(moved)
        late.extend(moved)
        A.hid[...] = dot(ug[...], A.fi_v[...])

        @pl.loop(0, RB // 16)
        def _(i):
            rows = rows_at(16 * i, 16)
            v = A.hid[rows]
            phi, fall = bell(v)
            A.smooth[rows] = (v * phi).astype(BF16)
            if keep:
                A.hslope[rows] = phi + v * fall * ROOT_TWO_PI

        A.part[...] = dot(A.smooth[...], A.fo_v[...])
        part_b[...] = A.part[...].astype(BF16)
        moved = scatter_sum_start(part_b, part_r)
        total = middle + A.part[quarter(mp)]
        landed(moved)
        late.extend(moved)
        for d in range(3):
            total = total + part_r[d].astype(F32)
        normed_b, inverse_b = norm_parts(total, D)
        if keep:
            A.normed_a[...] = normed_a
            A.inverse_a[...] = jnp.broadcast_to(inverse_a, (RQ, 128))
            A.normed_b[...] = normed_b
            A.inverse_b[...] = jnp.broadcast_to(inverse_b, (RQ, 128))
        return normed_b * gain_b

    spread_msg_in.wait()
    spread_edge[0].start()
    spread_edge[1].start()
    A.T[0:DE] = A.Wm[2 * D : 2 * D + DE]
    node_table(A.win1)
    message_mean(A.win1, False)
    spread_msg_out.wait()
    load_ffn_in.wait()
    load_ffn_out.wait()
    own_nodes = A.nodes_v[quarter(mp)]
    predicted = node_tail(own_nodes, A.ug1, A.pb1, A.pr1, False)
    A.mixed[...] = 0.5 * (own_nodes + predicted)
    A.win2[quarter(mp, RB)] = A.mixed[...].astype(BF16)
    window2 = Window(A.win2)
    window2.start()
    window2.forward()
    window2.wait_own()
    window2.wait()
    spread_edge[2].start()
    spread_edge[3].start()
    spread_edge[0].forward()
    spread_edge[1].forward()
    node_table(A.win2)
    message_mean(A.win2, True)
    spread_edge[2].forward()
    spread_edge[3].forward()
    settled = node_tail(A.mixed[...], A.ug2, A.pb2, A.pr2, True)
    A.win3[quarter(mp, RB)] = settled.astype(BF16)
    window3 = Window(A.win3)
    window3.start()
    window3.forward()

    for c in (*spread_edge, *load_edge_weights):
        c.wait()
    A.Eop[...] = jnp.concatenate([A.Eo[...], jnp.zeros((HE, 64), BF16)], axis=1)
    A.Te[0:DE] = A.We[:, 2 * D : 2 * D + DE].T
    window3.wait_own()
    window3.wait()
    store = [net.copy(A.win3.at[RB : 2 * RB], A.out_nodes)]

    for blk in (1, 0, 2):
        part = dot_bt(A.win3[RB * blk : RB * blk + RB], A.We[:, D : 2 * D])
        A.Te[DE + RB * blk : DE + RB * blk + RB] = part.astype(BF16)
    A.selfe[...] = dot_bt(A.win3[quarter(mp, RB)], A.We[:, 0:D])
    A.dself[...] = jnp.zeros((RQ, HE), F32)
    load_edge_cot.wait()
    gain_c = jnp.concatenate([A.gain_c[...], jnp.zeros((1, 256 - DE), F32)], axis=1)

    def norm_parts_e(values):
        scale = 1.0 / DE
        mean = jnp.sum(values, axis=-1, keepdims=True) * scale
        centred = jnp.where(is_edge, values - mean, 0.0)
        inverse = lax.rsqrt(jnp.sum(centred * centred, axis=-1, keepdims=True) * scale + EPSILON)
        return centred * inverse, inverse

    chunks = E // EC
    stream = net.reserve(3 * chunks)

    def new_part(q, c):
        return A.new_edges.at[quarter(q), pl.ds(pl.multiple_of(6 * DE * c, 128), 6 * DE)]

    def stream_copies(make, c):
        return (
            make(stream + c, new_part(mp, c), new_part(mp, c), mp=pair),
            make(stream + chunks + c, new_part(mp, c), new_part(mp, c), mp=cross),
            make(stream + 2 * chunks + c, new_part(cross, c), new_part(cross, c), mp=pair),
        )

    def edge_chunk(c, gain_total):
        rows = rows_at(EC * c, EC)
        A.base[...] = dot(A.XO[rows], A.Te[256:768])
        A.pre2[...] = dot(A.XE[rows], A.Te[0:256])

        @pl.loop(0, EC // 16)
        def _(b):
            at = rows_at(16 * b, 16)
            base = A.base[at] + A.selfe[rows_at(16 * (b % (RQ // 16)), 16)]
            A.base[at] = base
            v = base + A.pre2[at]
            phi, _ = bell(v)
            A.G[at] = (v * phi).astype(BF16)

        A.upd[...] = dot(A.G[...], A.Eop[...])
        for j in range(3):
            both = pair_load(A.e_v, pl.multiple_of(1152 * c + 384 * j, 128))
            for p in range(2):
                k = 2 * j + p
                mine = slice(RQ * k, RQ * k + RQ)
                at = rows_at(EC * c + RQ * k, RQ)
                normed, _ = norm_parts_e(both[p] + A.upd[mine])
                mixed = 0.5 * (both[p] + normed * gain_c)
                A.emix[mine] = mixed
                A.XM[at] = jnp.where(is_edge, mixed, A.XE[at].astype(F32)).astype(BF16)

        A.pre2[...] = dot(A.XM[rows], A.Te[0:256])

        @pl.loop(0, EC // 16)
        def _(b):
            at = rows_at(16 * b, 16)
            v = A.base[at] + A.pre2[at]
            phi, fall = bell(v)
            A.G2[rows_at(EC * c + 16 * b, 16)] = (v * phi).astype(BF16)
            A.base[at] = phi + v * fall * ROOT_TWO_PI

        A.upd[...] = dot(A.G2[rows], A.Eop[...])
        for j in range(3):
            lanes = pl.multiple_of(1152 * c + 384 * j, 128)
            cots = pair_load(A.ec_v, lanes)
            news = []
            for p in range(2):
                k = 2 * j + p
                mine = slice(RQ * k, RQ * k + RQ)
                normed, inverse = norm_parts_e(A.emix[mine] + A.upd[mine])
                news.append(normed * gain_c)
                gain_total = gain_total + jnp.sum(
                    (cots[p] * normed).reshape(RQ // 8, 8, 256), axis=0
                )
                d_sum = jnp.where(is_edge, norm_back(cots[p], normed, inverse, gain_c, DE), 0.0)
                A.emix[mine] = d_sum
                A.DO[rows_at(EC * c + RQ * k, RQ)] = d_sum.astype(BF16)
            pair_store(A.new_edges, lanes, news[0], news[1], quarter(mp))

        to_pair, to_cross, _ = stream_copies(net.at, c)
        to_cross.start()
        to_pair.start()

        @pl.when(c > 0)
        def _():
            _, arrived, on = stream_copies(net.at, c - 1)
            arrived.wait_recv()
            on.start()


        A.pre2[...] = dot_bt(A.DO[rows], A.Eop[...])

        @pl.loop(0, EC // 16)
        def _(b):
            at = rows_at(16 * b, 16)
            own = rows_at(16 * (b % (RQ // 16)), 16)
            d = (A.pre2[at] * A.base[at]).astype(BF16)
            A.DP2[rows_at(EC * c + 16 * b, 16)] = d
            A.dself[own] = A.dself[own] + d.astype(F32)

        A.EG[rows] = 0.5 * (A.emix[...] + dot_bt(A.DP2[rows], A.Te[0:256]))
        return gain_total

    gain_total = lax.fori_loop(0, E // EC, edge_chunk, jnp.zeros((8, 256), F32))
    A.gains[...] = jnp.zeros_like(A.gains)
    A.gains[2:3, 0:256] = jnp.sum(gain_total, axis=0, keepdims=True)

    streams = [stream_copies(net.opened, c) for c in range(chunks - 1)]
    last_pair, last_cross, _ = stream_copies(net.opened, chunks - 1)
    on_last = net.remote(new_part(cross, chunks - 1), new_part(cross, chunks - 1), mp=pair)

    A.dself_low[...] = A.dself[...].astype(BF16)
    for blk in range(3):
        at = slice(RB * blk, RB * blk + RB)
        A.dq[at] = dot(A.XT[DE + RB * blk : DE + RB * blk + RB], A.DP2[...]).astype(BF16)

    load_node_cot.wait()

    def emit_edge(tile, value):
        for q in range(4):
            at = DE * tile
            A.ge[q, at : at + big] = value[big * q : big * q + big].astype(BF16)
            more = 4 * big + small * q
            A.ge[q, at + big : at + DE] = value[more : more + small].astype(BF16)

    def emit_msg(row, value):
        n = value.shape[0]
        for q in range(4):
            A.gm[q, row : row + n] = value[:, 128 * q : 128 * q + 128].astype(BF16)

    def edge_weight_gradients():
        by_in = dot_at(A.XM[...], A.DP2[...])
        by_out = dot_at(A.DO[...], A.G2[...])
        emit_edge(8, jnp.transpose(by_in[0:128]))
        emit_edge(10, jnp.transpose(by_out[0:128]))
        emit_edge(
            9, jnp.transpose(jnp.concatenate([by_in[128:DE], by_out[128:DE]], axis=0))
        )
        own = A.win3[quarter(mp, RB)]
        for t in range(4):
            at = slice(128 * t, 128 * t + 128)
            emit_edge(t, jnp.transpose(dot_at(own[:, at], A.dself_low[...])))
            emit_edge(4 + t, jnp.transpose(dot_at(A.win3[:, at], A.dq[...])))
        pump(sum_edge)

    def message_weight_gradients():
        own = A.win2[quarter(mp, RB)]
        for t in range(4):
            at = slice(128 * t, 128 * t + 128)
            emit_msg(128 * t, dot_at(own[:, at], A.dmsg_low[...]))
            emit_msg(D + 128 * t, dot_at(A.win2[:, at], A.dq1[...]))
            value = dot_at(A.avg[:, at], A.dg1[...])
            for u in range(4):
                row = 2 * D + DE + 128 * u
                A.gm[t, row : row + 128] = value[:, 128 * u : 128 * u + 128].astype(BF16)
        emit_msg(2 * D, dot(A.XT[0:DE], A.DP[...]))

    for ref, used in ((A.ge, 11 * DE), (A.gm, 3 * D + DE)):
        if ref.shape[1] > used:
            for q in range(4):
                ref[q, used:] = jnp.zeros((ref.shape[1] - used, 128), BF16)

    def reduce_mp(g, got, cuts):
        rows = g.shape[1]
        a1 = net.remote(g.at[pair], got.at[0], mp=pair)
        a2 = net.remote(g.at[third], got.at[1], mp=pair)
        a2.start()
        a1.start()
        yield
        a2.wait_recv()

        @pl.loop(0, rows // 32)
        def _(i):
            at = rows_at(32 * i, 32)
            got[1, at] = (g[cross, at].astype(F32) + got[1, at].astype(F32)).astype(BF16)

        step = rows // cuts
        pieces = []
        for i in range(cuts):
            at = pl.ds(step * i, step)
            b = net.remote(got.at[1, at], got.at[2, at], mp=cross)
            b.start()
            pieces.append(b)
            yield
        for c in (a1, *pieces):
            c.wait_recv()

        @pl.loop(0, rows // 32)
        def _(i):
            at = rows_at(32 * i, 32)
            total = g[mp, at].astype(F32) + got[0, at].astype(F32) + got[2, at].astype(F32)
            got[0, at] = total.astype(BF16)

        for c in (a1, a2, *pieces):
            c.wait_send()

    def reduce_res(work, got, out, result, order):
        size = work.shape[0]
        low = 0
        used = 0
        for s in order:
            bit = (res // (1 << s)) % 2
            size = size // 2
            keep = low + bit * size
            give = low + (1 - bit) * size
            c = net.remote(
                work.at[rows_at(give, size, S.grain)], got.at[pl.ds(used, size)], res=across(s)
            )
            c.start()
            yield
            c.wait()
            into = out if s == order[-1] else work

            @pl.loop(0, size // S.grain)
            def _(i, keep=keep, used=used, into=into):
                at = rows_at(keep + S.grain * i, S.grain, S.grain)
                there = rows_at(used + S.grain * i, S.grain, S.grain)
                into[at] = (work[at].astype(F32) + got[there].astype(F32)).astype(BF16)

            used += size
            low = keep
        for s in reversed(order):
            bit = (res // (1 << s)) % 2
            here = out.at[rows_at(low, size, S.grain)]
            c = net.remote(here, here, res=across(s))
            c.start()
            yield
            c.wait()
            low = low - bit * size
            size = 2 * size
        store.append(net.copy(out, result))

    def reduce_gains():
        copies = [net.remote(A.gains, A.gains_r.at[d - 1], mp=peer(d)) for d in (1, 2, 3)]
        for c in copies:
            c.start()
        yield
        for c in copies:
            c.wait()
        A.gains_t[0] = A.gains[...] + A.gains_r[0] + A.gains_r[1] + A.gains_r[2]
        for s in range(S.bits):
            c = net.remote(A.gains_t.at[s], A.gains_r.at[3 + s], res=across(s))
            c.start()
            yield
            c.wait()
            A.gains_t[s + 1] = A.gains_t[s] + A.gains_r[3 + s]
        store.append(net.copy(A.gains_t.at[S.bits], A.out_gains))

    def chain(*parts):
        for part in parts:
            yield from part

    def pump(*sums):
        for g in sums:
            next(g, None)

    order = list(range(S.bits))
    sum_edge = chain(
        reduce_mp(A.ge, A.ge_r, 2), reduce_res(A.ge_r.at[0], A.sum_er, A.sum_e, A.pack_e, order)
    )
    sum_in = reduce_res(A.grad_i, A.sum_ir, A.sum_i, A.pack_i, order)
    sum_out = reduce_res(A.grad_o, A.sum_or, A.sum_o, A.pack_o, order)
    sum_msg = chain(
        reduce_mp(A.gm, A.gm_r, 1), reduce_res(A.gm_r.at[0], A.sum_mr, A.sum_m, A.pack_m, order)
    )
    sum_gains = reduce_gains()

    def between_a():
        last_cross.wait_recv()
        on_last.start()
        pump(sum_edge)

    d_settled = A.nc_v[...] + dot(A.dself_low[...], A.We[:, 0:D])
    d_settled = d_settled + return_rows(
        lambda blk: dot(A.dq[RB * blk : RB * blk + RB], A.We[:, D : 2 * D]),
        A.back_send_a,
        A.back_recv_a,
        A.back_side_send_a,
        A.back_side_a,
        edge_weight_gradients,
        between_a,
    )

    normed_b = A.normed_b[...]
    d_sum_b = norm_back(d_settled, normed_b, A.inverse_b[:, 0:1], gain_b, D)
    A.gains[1:2] = jnp.sum(d_settled * normed_b, axis=0, keepdims=True)
    A.dF[quarter(mp)] = d_sum_b.astype(BF16)
    moved = gather_rows(A.dF)
    landed(moved)
    late.extend(moved)
    A.hid[...] = dot_bt(A.dF[...], A.fo_v[...])

    @pl.loop(0, RB // 16)
    def _(i):
        rows = rows_at(16 * i, 16)
        A.dT[rows] = (A.hid[rows] * A.hslope[rows]).astype(BF16)

    A.part[...] = dot_bt(A.dT[...], A.fi_v[...])
    A.pb3[...] = A.part[...].astype(BF16)
    moved = scatter_sum_start(A.pb3, A.pr3)
    pump(sum_edge)
    A.grad_i[...] = dot_at(A.ug2[...], A.dT[...]).astype(BF16)
    pump(sum_in)
    A.grad_o[...] = dot_at(A.smooth[...], A.dF[...]).astype(BF16)
    pump(sum_out)
    d_middle = d_sum_b + A.part[quarter(mp)]
    landed(moved)
    late.extend(moved)
    for d in range(3):
        d_middle = d_middle + A.pr3[d].astype(F32)
    normed_a = A.normed_a[...]
    d_sum_a = norm_back(d_middle, normed_a, A.inverse_a[:, 0:1], gain_a, D)
    A.gains[0:1] = jnp.sum(d_middle * normed_a, axis=0, keepdims=True)
    pump(sum_gains)
    A.dsa[...] = d_sum_a
    A.dg1[...] = d_sum_a.astype(BF16)
    A.davg[...] = dot_bt(A.dg1[...], A.Wo[...])

    for sub in range(RQ // 16):
        mine = A.davg[16 * sub : 16 * sub + 16]

        def back_step(k, total, sub=sub, mine=mine):
            rows = rows_at(RQ * k + 16 * sub, 16)
            d = (mine * A.slope[rows].astype(F32)).astype(BF16)
            A.DP[rows] = d
            return total + d.astype(F32)

        total = lax.fori_loop(0, K, back_step, jnp.zeros((16, HM), F32))
        A.dmsg_low[16 * sub : 16 * sub + 16] = total.astype(BF16)

    for blk in range(3):
        at = slice(RB * blk, RB * blk + RB)
        A.dq1[at] = dot(A.XT[DE + RB * blk : DE + RB * blk + RB], A.DP[...]).astype(BF16)

    message_weight_gradients()
    pump(sum_msg, sum_edge, sum_in, sum_out, sum_gains)

    def edge_gradient():
        @pl.loop(0, E // EC)
        def _(c):
            rows = rows_at(EC * c, EC)
            A.EG[rows] = A.EG[rows] + dot_bt(A.DP[rows], A.T[0:256])
            for j in range(3):
                lanes = pl.multiple_of(1152 * c + 384 * j, 128)
                ends = [
                    jnp.where(is_edge, A.EG[rows_at(EC * c + RQ * (2 * j + p), RQ)], 0.0)
                    for p in range(2)
                ]
                pair_store(A.ec_v, lanes, ends[0], ends[1])

        store.append(net.copy(A.ec_v, A.out_edge_grad))
        for a, b, c in streams:
            a.wait()
            b.wait_send()
            c.wait()
        last_pair.wait()
        last_cross.wait_send()
        on_last.wait()
        store.append(net.copy(A.new_edges, A.out_edges))

    def fill_b():
        pump(sum_msg)
        edge_gradient()

    back = return_rows(
        lambda blk: dot_bt(A.dq1[RB * blk : RB * blk + RB], A.Wm[D : 2 * D]),
        A.back_send_b,
        A.back_recv_b,
        A.back_side_send_b,
        A.back_side_b,
        fill_b,
        lambda: pump(sum_in, sum_out, sum_edge, sum_msg, sum_gains),
    )
    A.node_grad_v[...] = 0.5 * (A.dsa[...] + dot_bt(A.dmsg_low[...], A.Wm[0:D]) + back)
    store.append(net.copy(A.node_grad_v, A.out_node_grad))

    work = [sum_in, sum_out, sum_edge, sum_msg, sum_gains]
    while work:
        for g in list(work):
            try:
                next(g)
            except StopIteration:
                work.remove(g)
    for c in store:
        c.wait()
    for s in (spread_msg_in, spread_msg_out, *spread_edge, halo, window2, window3):
        s.sent()
    for c in late:
        c.wait_send()
    assert net.remote_count <= S.remote and net.local_count <= S.local


def build(S):
    E = S.RQ * S.K
    W = 3 * S.RB
    EC = 6 * S.RQ
    grain = S.grain * S.n_res
    rows_e = up(11 * S.DE, grain)
    rows_m = up(3 * S.D + S.DE, grain)
    in_names = ["nodes", "edges", "neighbours", "edge_mask", "msg_in", "msg_out", "gain_a"]
    in_names += ["ffn_in", "ffn_out", "gain_b", "edge_in", "edge_out", "gain_c"]
    in_names += ["node_cot", "edge_cot"]
    outs = dict(
        out_nodes=((S.RB, S.D), BF16),
        out_edges=((S.RB, S.K * S.DE), BF16),
        out_node_grad=((S.RQ, S.D), F32),
        out_edge_grad=((S.RQ, S.K * S.DE), F32),
        pack_e=((rows_e, 128), BF16),
        pack_i=((S.D, S.FL), BF16),
        pack_o=((S.FL, S.D), BF16),
        pack_m=((rows_m, 128), BF16),
        out_gains=((8, S.D), F32),
    )
    scratch = dict(
        nodes_v=((S.RB, S.D), F32),
        nbr_v=((S.K, S.RB), jnp.int32),
        mask_v=((S.K, S.RB), jnp.int32),
        columns=((S.RB, 128), F32),
        new_edges=((S.RB, S.K * S.DE), BF16),
        node_grad_v=((S.RQ, S.D), F32),
        e_v=((S.RQ, S.K * S.DE), F32),
        ec_v=((S.RQ, S.K * S.DE), F32),
        nc_v=((S.RQ, S.D), F32),
        Wm=((2 * S.D + S.DE, S.HM), BF16),
        Wo=((S.HM, S.D), BF16),
        fi_v=((S.D, S.FL), BF16),
        fo_v=((S.FL, S.D), BF16),
        We=((S.HE, 2 * S.D + S.DE), BF16),
        Eo=((S.HE, S.DE), BF16),
        Eop=((S.HE, 256), BF16),
        win1=((W, S.D), BF16),
        win2=((W, S.D), BF16),
        win3=((W, S.D), BF16),
        XE=((E, 256), BF16),
        XM=((E, 256), BF16),
        XO=((E, 512), BF16),
        XT=((768, E), BF16),
        WB=((E, 128), F32),
        T=((768, S.HM), BF16),
        Te=((768, S.HE), BF16),
        selfs=((S.RQ, S.HM), F32),
        selfe=((S.RQ, S.HE), F32),
        total=((S.RQ, S.HM), F32),
        slope=((E, S.HM), BF16),
        avg=((S.RQ, S.HM), BF16),
        ug1=((S.RB, S.D), BF16),
        ug2=((S.RB, S.D), BF16),
        hid=((S.RB, S.FL), F32),
        smooth=((S.RB, S.FL), BF16),
        hslope=((S.RB, S.FL), F32),
        part=((S.RB, S.D), F32),
        pb1=((S.RB, S.D), BF16),
        pb2=((S.RB, S.D), BF16),
        pb3=((S.RB, S.D), BF16),
        pr1=((3, S.RQ, S.D), BF16),
        pr2=((3, S.RQ, S.D), BF16),
        pr3=((3, S.RQ, S.D), BF16),
        normed_a=((S.RQ, S.D), F32),
        normed_b=((S.RQ, S.D), F32),
        inverse_a=((S.RQ, 128), F32),
        inverse_b=((S.RQ, 128), F32),
        mixed=((S.RQ, S.D), F32),
        base=((EC, S.HE), F32),
        pre2=((EC, S.HE), F32),
        G=((EC, S.HE), BF16),
        upd=((EC, 256), F32),
        emix=((EC, 256), F32),
        G2=((E, S.HE), BF16),
        DO=((E, 256), BF16),
        DP2=((E, S.HE), BF16),
        EG=((E, 256), F32),
        dself=((S.RQ, S.HE), F32),
        dself_low=((S.RQ, S.HE), BF16),
        dq=((W, S.HE), BF16),
        gains=((8, S.D), F32),
        gains_r=((3 + S.bits, 8, S.D), F32),
        gains_t=((1 + S.bits, 8, S.D), F32),
        back_send_a=((4, 3, S.RQ, S.D), BF16),
        back_recv_a=((3, 3, S.RQ, S.D), BF16),
        back_side_send_a=((2, S.RQ, S.D), BF16),
        back_side_a=((2, S.RQ, S.D), BF16),
        back_send_b=((4, 3, S.RQ, S.D), BF16),
        back_recv_b=((3, 3, S.RQ, S.D), BF16),
        back_side_send_b=((2, S.RQ, S.D), BF16),
        back_side_b=((2, S.RQ, S.D), BF16),
        dF=((S.RB, S.D), BF16),
        dT=((S.RB, S.FL), BF16),
        dsa=((S.RQ, S.D), F32),
        dg1=((S.RQ, S.D), BF16),
        davg=((S.RQ, S.HM), F32),
        DP=((E, S.HM), BF16),
        dmsg_low=((S.RQ, S.HM), BF16),
        dq1=((W, S.HM), BF16),
        ge=((4, rows_e, 128), BF16),
        ge_r=((3, rows_e, 128), BF16),
        sum_er=((rows_e, 128), BF16),
        sum_e=((rows_e, 128), BF16),
        grad_i=((S.D, S.FL), BF16),
        sum_ir=((S.D, S.FL), BF16),
        sum_i=((S.D, S.FL), BF16),
        grad_o=((S.FL, S.D), BF16),
        sum_or=((S.FL, S.D), BF16),
        sum_o=((S.FL, S.D), BF16),
        gm=((4, rows_m, 128), BF16),
        gm_r=((3, rows_m, 128), BF16),
        sum_mr=((rows_m, 128), BF16),
        sum_m=((rows_m, 128), BF16),
    )
    names = list(scratch) + ["send", "recv", "local"]
    shapes = [pltpu.VMEM(*v) for v in scratch.values()] + [
        pltpu.SemaphoreType.DMA((S.remote,)),
        pltpu.SemaphoreType.DMA((S.remote,)),
        pltpu.SemaphoreType.DMA((S.local,)),
    ]
    body = functools.partial(kernel_body, S, in_names, list(outs), names)
    body.__name__ = "layer"
    gains = ("gain_a", "gain_b", "gain_c")
    return pl.pallas_call(
        body,
        name="layer",
        out_shape=[jax.ShapeDtypeStruct(*v) for v in outs.values()],
        in_specs=[VMEM if n in gains else ANY for n in in_names],
        out_specs=[ANY] * len(outs),
        scratch_shapes=shapes,
        compiler_params=pltpu.CompilerParams(
            collective_id=0, has_side_effects=True, vmem_limit_bytes=62 * 1024 * 1024
        ),
    )


def unpack_body(S, names, *refs):
    A = SimpleNamespace(**dict(zip(names, refs, strict=True)))
    D, DE, RB = S.D, S.DE, S.RB
    count = [0]

    def copy(src, dst):
        c = pltpu.make_async_copy(src, dst, A.sems.at[count[0]])
        count[0] += 1
        c.start()
        return c

    part = RB // 4
    edge_loads = [
        copy(A.in_edges.at[pl.ds(part * i, part)], A.edges_l.at[pl.ds(part * i, part)])
        for i in range(4)
    ]
    pairs = (
        (A.in_e, A.e_l),
        (A.in_i, A.i_l),
        (A.in_o, A.o_l),
        (A.in_m, A.m_l),
        (A.in_nodes, A.nodes_l),
        (A.in_gains, A.gains_l),
    )
    loads = [copy(*p) for p in pairs]
    stores = [copy(A.in_node_grad, A.o2), copy(A.in_edge_grad, A.o3)]
    for i in range(4):
        edge_loads[i].wait()

        @pl.loop(0, part // 16)
        def _(k, i=i):
            at = pl.ds(pl.multiple_of(part * i + 16 * k, 16), 16)
            A.edges_f[at] = A.edges_l[at].astype(F32)

        at = pl.ds(part * i, part)
        stores.append(copy(A.edges_f.at[at], A.o1.at[at]))
    for c in loads:
        c.wait()

    def widen(src, dst, out, rows):
        @pl.loop(0, rows // 16)
        def _(k):
            at = pl.ds(pl.multiple_of(16 * k, 16), 16)
            dst[at] = src[at].astype(F32)

        stores.append(copy(dst, out))

    widen(A.i_l, A.i_f, A.o7, D)
    widen(A.o_l, A.o_f, A.o8, S.FL)
    widen(A.nodes_l, A.nodes_f, A.o0, RB)
    widen(A.m_l, A.m_f, A.o4, 2 * D + DE)
    for u in range(4):
        row = 2 * D + DE + 128 * u
        A.mo_f[:, 128 * u : 128 * u + 128] = A.m_l[row : row + 128].astype(F32)
    stores.append(copy(A.mo_f, A.o5))
    mixed = A.e_l[9 * DE : 10 * DE].astype(F32)
    for t in range(9):
        A.ei_f[:, 128 * t : 128 * t + 128] = A.e_l[DE * t : DE * t + DE].astype(F32)
    A.ei_f[:, 1152 : 1152 + 64] = mixed[:, 0:64]
    stores.append(copy(A.ei_f, A.o10))
    A.eo_f[:, 0:128] = A.e_l[10 * DE : 11 * DE].astype(F32)
    A.eo_f[:, 128:DE] = pltpu.roll(mixed, 64, 1)[:, 0:64]
    stores.append(copy(A.eo_f, A.o11))
    A.ga_f[...] = A.gains_l[0:1]
    A.gb_f[...] = A.gains_l[1:2]
    A.gc_f[...] = A.gains_l[2:3, 0:DE]
    for src, out in ((A.ga_f, A.o6), (A.gb_f, A.o9), (A.gc_f, A.o12)):
        stores.append(copy(src, out))
    for c in stores:
        c.wait()


def unpack(S, values):
    D, DE, RB, RQ, K, FL = S.D, S.DE, S.RB, S.RQ, S.K, S.FL
    ins = ["in_nodes", "in_edges", "in_node_grad", "in_edge_grad"]
    ins += ["in_e", "in_i", "in_o", "in_m", "in_gains"]
    shapes = [
        (RB, D),
        (RB, K * DE),
        (RQ, D),
        (RQ, K * DE),
        (2 * D + DE, S.HM // 4),
        (S.HM // 4, D),
        (1, D),
        (D, FL),
        (FL, D),
        (1, D),
        (S.HE // 4, 2 * D + DE),
        (S.HE // 4, DE),
        (1, DE),
    ]
    outs = ["o%d" % i for i in range(13)]
    scratch = dict(
        edges_l=((RB, K * DE), BF16),
        edges_f=((RB, K * DE), F32),
        e_l=(values[4].shape, BF16),
        i_l=((D, FL), BF16),
        o_l=((FL, D), BF16),
        m_l=(values[7].shape, BF16),
        nodes_l=((RB, D), BF16),
        gains_l=((8, D), F32),
        i_f=((D, FL), F32),
        o_f=((FL, D), F32),
        nodes_f=((RB, D), F32),
        m_f=(shapes[4], F32),
        mo_f=(shapes[5], F32),
        ei_f=(shapes[10], F32),
        eo_f=(shapes[11], F32),
        ga_f=(shapes[6], F32),
        gb_f=(shapes[9], F32),
        gc_f=(shapes[12], F32),
    )
    names = ins + outs + list(scratch) + ["sems"]
    body = functools.partial(unpack_body, S, names)
    return list(
        pl.pallas_call(
            body,
            name="unpack",
            out_shape=[jax.ShapeDtypeStruct(x, F32) for x in shapes],
            in_specs=[ANY] * len(ins),
            out_specs=[ANY] * len(outs),
            scratch_shapes=[pltpu.VMEM(*v) for v in scratch.values()]
            + [pltpu.SemaphoreType.DMA((32,))],
            compiler_params=pltpu.CompilerParams(vmem_limit_bytes=62 * 1024 * 1024),
        )(*values)
    )


STOP = 0


def on_device(n_res, *args):
    nodes, edges, neighbours, _, _, _, _, ffn_in = args[:8]
    height = nodes.shape[0]
    degree = neighbours.shape[1]
    S = SimpleNamespace(
        n_res=n_res,
        bits=int(math.log2(n_res)),
        RB=height,
        RQ=height // 4,
        K=degree,
        D=nodes.shape[1],
        DE=edges.shape[1] // degree,
        HM=args[4].shape[1] * 4,
        HE=args[10].shape[1] * 4,
        FL=ffn_in.shape[1],
        grain=16 if n_res <= 16 else 8,
        remote=160,
        local=32,
        stop=STOP,
    )
    fixed = [a.reshape(1, -1) if a.ndim == 1 else a for a in args]
    for i in (2, 3, 10):
        fixed[i] = fixed[i].T
    out = unpack(S, build(S)(*fixed))
    for i in (6, 9, 12):
        out[i] = out[i].reshape(-1)
    out[10] = out[10].T
    return tuple(out)


def solution(mesh):
    in_specs = (
        P("res", None),
        P("res", None),
        P("res", None),
        P("res", None),
        P(None, "mp"),
        P("mp", None),
        P(),
        P(None, "mp"),
        P("mp", None),
        P(),
        P(None, "mp"),
        P("mp", None),
        P(),
        P("res", None),
        P("res", None),
    )
    out_specs = (
        P("res", None),
        P("res", None),
        P(("res", "mp"), None),
        P(("res", "mp"), None),
        P(None, "mp"),
        P("mp", None),
        P(),
        P(None, "mp"),
        P("mp", None),
        P(),
        P(None, "mp"),
        P("mp", None),
        P(),
    )
    return jax.shard_map(
        functools.partial(on_device, mesh.shape["res"]),
        mesh=mesh,
        in_specs=in_specs,
        out_specs=out_specs,
        check_vma=False,
    )
```

```python
import functools
import math
from types import SimpleNamespace

import jax
import jax.numpy as jnp
from jax import lax
from jax.experimental import pallas as pl
from jax.experimental.pallas import tpu as pltpu
from jax.sharding import PartitionSpec as P

EPSILON = 1e-05
F32 = jnp.float32
BF16 = jnp.bfloat16
MESH = pl.DeviceIdType.MESH
ROOT_TWO_PI = 0.3989422804014327
ROOT_HALF = 0.7071067811865476
ANY = pl.BlockSpec(memory_space=pl.ANY)
VMEM = pl.BlockSpec(memory_space=pltpu.VMEM)


def dot(left, right):
    return jnp.dot(left, right, preferred_element_type=F32)


def dot_bt(left, right):
    return lax.dot_general(left, right, (((1,), (1,)), ((), ())), preferred_element_type=F32)


def dot_at(left, right):
    return lax.dot_general(left, right, (((0,), (0,)), ((), ())), preferred_element_type=F32)


def bell(v):
    return 0.5 + 0.5 * lax.erf(v * ROOT_HALF)


def bell_slope(phi, v):
    return phi + v * (jnp.exp(-0.5 * (v * v)) * ROOT_TWO_PI)


def norm_parts(values, width):
    scale = 1.0 / width
    centred = values - jnp.sum(values, axis=-1, keepdims=True) * scale
    inverse = lax.rsqrt(jnp.sum(centred * centred, axis=-1, keepdims=True) * scale + EPSILON)
    return centred * inverse, inverse


def norm_back(upstream, normed, inverse, gain, width):
    scale = 1.0 / width
    scaled = upstream * gain
    mean = jnp.sum(scaled, axis=-1, keepdims=True) * scale
    along = jnp.sum(scaled * normed, axis=-1, keepdims=True) * scale
    return inverse * (scaled - mean - normed * along)


def up(rows, step):
    return -(-rows // step) * step


class Net:
    def __init__(self, send, recv, local):
        self.send, self.recv, self.local = send, recv, local
        self.remote_count = 0
        self.local_count = 0

    def remote(self, src, dst, side="", **where):
        i = self.remote_count
        self.remote_count += 1
        return pltpu.make_async_remote_copy(
            src_ref=src,
            dst_ref=dst,
            send_sem=self.send.at[i],
            recv_sem=self.recv.at[i],
            device_id=where,
            device_id_type=MESH,
        )

    def reserve(self, count):
        i = self.remote_count
        self.remote_count += count
        return i

    def at(self, i, src, dst, **where):
        return pltpu.make_async_remote_copy(
            src_ref=src,
            dst_ref=dst,
            send_sem=self.send.at[i],
            recv_sem=self.recv.at[i],
            device_id=where,
            device_id_type=MESH,
        )

    def opened(self, i, src, dst, **where):
        return self.at(i, src, dst, **where)

    def copy(self, src, dst):
        i = self.local_count
        self.local_count += 1
        c = pltpu.make_async_copy(src, dst, self.local.at[i])
        c.start()
        return c


def kernel_body(S, in_names, out_names, scratch_names, *refs):
    names = in_names + out_names + scratch_names
    A = SimpleNamespace(**dict(zip(names, refs, strict=True)))
    net = Net(A.send, A.recv, A.local)
    RB, RQ, K, D, DE, HM, HE, FL = S.RB, S.RQ, S.K, S.D, S.DE, S.HM, S.HE, S.FL
    E = RQ * K
    W = 3 * RB
    EC = 6 * RQ
    res = lax.axis_index("res")
    mp = lax.axis_index("mp")
    has_l = res > 0
    has_r = res < S.n_res - 1
    pair = mp + 1 - 2 * (mp % 2)
    cross = (mp + 2) % 4
    third = (pair + 2) % 4

    def peer(d):
        return (mp + d) % 4

    def rows_at(start, size, step=16):
        return pl.ds(pl.multiple_of(start, step), size)

    def quarter(q, base=0):
        return rows_at(base + RQ * q, RQ)

    load_nodes = net.copy(A.nodes, A.nodes_v)
    load_nbr = net.copy(A.neighbours, A.nbr_v)
    load_mask = net.copy(A.edge_mask, A.mask_v)
    load_edges = net.copy(A.edges.at[quarter(mp)], A.e_v)
    own_msg_in = A.Wm.at[:, pl.ds(pl.multiple_of(mp * 128, 128), 128)]
    load_msg_in = net.copy(A.msg_in, own_msg_in)
    own_msg_out = A.Wo.at[rows_at(mp * 128, 128)]
    load_msg_out = net.copy(A.msg_out, own_msg_out)
    load_ffn_in = net.copy(A.ffn_in, A.fi_v)
    load_ffn_out = net.copy(A.ffn_out, A.fo_v)
    big, small = HE // 4 // 3 * 2, HE // 4 // 3

    def main_rows(ref):
        return lambda q: ref.at[rows_at(big * q, big)]

    def rest_rows(ref):
        return lambda q: ref.at[rows_at(4 * big + small * q, small)]

    first, rest = pl.ds(0, big), pl.ds(big, small)
    edge_parts = (
        (A.edge_in.at[first], main_rows(A.We)),
        (A.edge_out.at[first], main_rows(A.Eo)),
        (A.edge_in.at[rest], rest_rows(A.We)),
        (A.edge_out.at[rest], rest_rows(A.Eo)),
    )
    load_edge_weights = [net.copy(src, place(mp)) for src, place in edge_parts]
    load_node_cot = net.copy(A.node_cot.at[quarter(mp)], A.nc_v)
    load_edge_cot = net.copy(A.edge_cot.at[quarter(mp)], A.ec_v)

    barrier = pltpu.get_barrier_semaphore()

    def greet(**where):
        pl.semaphore_signal(barrier, inc=1, device_id=where, device_id_type=MESH)

    def across(s):
        return res + (1 << s) * (1 - 2 * ((res // (1 << s)) % 2))

    for d in (1, 2, 3):
        greet(mp=peer(d))
    for s in range(S.bits - 2):
        greet(res=across(s))
    stride = S.n_res // 4
    for d in (1, 2, 3):
        greet(res=res + ((res // stride + d) % 4 - res // stride) * stride)

    @pl.when(has_l)
    def _():
        greet(res=res - 1)

    @pl.when(has_r)
    def _():
        greet(res=res + 1)

    sides = (res + S.n_res - 1) // S.n_res + 1 - (res + 1) // S.n_res
    pl.semaphore_wait(barrier, 6 + S.bits - 2 + sides)

    class Spread:
        def __init__(self, src, place):
            own = place(mp)
            self.first = [net.remote(src, own, mp=pair), net.remote(src, own, mp=cross)]
            self.then = net.remote(place(cross), place(cross), mp=pair)

        def start(self):
            for c in self.first:
                c.start()

        def forward(self):
            self.first[1].wait_recv()
            self.then.start()

        def wait(self):
            self.first[0].wait_recv()
            self.then.wait_recv()

        def sent(self):
            for c in self.first:
                c.wait_send()
            self.then.wait_send()

    spread_msg_in = Spread(
        A.msg_in, lambda q: A.Wm.at[:, pl.ds(pl.multiple_of(q * 128, 128), 128)]
    )
    spread_msg_out = Spread(A.msg_out, lambda q: A.Wo.at[rows_at(q * 128, 128)])
    spread_edge = [Spread(src, place) for src, place in edge_parts]

    def clear_sides(win):
        @pl.when(jnp.logical_not(has_l))
        def _():
            win[0:RB] = jnp.zeros((RB, D), BF16)

        @pl.when(jnp.logical_not(has_r))
        def _():
            win[2 * RB : 3 * RB] = jnp.zeros((RB, D), BF16)

    half = RB // 2

    class Halo:
        def __init__(self, win):
            h = mp % 2
            own = win.at[rows_at(RB + half * h, half)]
            left = win.at[rows_at(half * h, half)]
            right = win.at[rows_at(2 * RB + half * h, half)]
            self.to_l = net.remote(own, right, side="l", res=res - 1)
            self.to_r = net.remote(own, left, side="r", res=res + 1)
            self.on_l = net.remote(left, left, mp=pair)
            self.on_r = net.remote(right, right, mp=pair)

        def start(self):
            pl.when(has_l)(self.to_l.start)
            pl.when(has_r)(self.to_r.start)

        def forward(self):
            @pl.when(has_l)
            def _():
                self.to_r.wait_recv()
                self.on_l.start()

            @pl.when(has_r)
            def _():
                self.to_l.wait_recv()
                self.on_r.start()

        def wait(self):
            pl.when(has_l)(self.on_l.wait_recv)
            pl.when(has_r)(self.on_r.wait_recv)

        def sent(self):
            @pl.when(has_l)
            def _():
                self.to_l.wait_send()
                self.on_l.wait_send()

            @pl.when(has_r)
            def _():
                self.to_r.wait_send()
                self.on_r.wait_send()

    class Window:
        def __init__(self, win):
            own = win.at[quarter(mp, RB)]
            left = win.at[quarter(mp)]
            right = win.at[quarter(mp, 2 * RB)]
            self.to_l = net.remote(own, right, side="l", res=res - 1)
            self.to_r = net.remote(own, left, side="r", res=res + 1)
            self.mine = [net.remote(own, own, mp=peer(d)) for d in (1, 2, 3)]
            self.on_l = [net.remote(left, left, mp=peer(d)) for d in (1, 2, 3)]
            self.on_r = [net.remote(right, right, mp=peer(d)) for d in (1, 2, 3)]

        def start(self):
            pl.when(has_l)(self.to_l.start)
            pl.when(has_r)(self.to_r.start)
            for c in self.mine:
                c.start()

        def forward(self):
            @pl.when(has_l)
            def _():
                self.to_r.wait_recv()
                for c in self.on_l:
                    c.start()

            @pl.when(has_r)
            def _():
                self.to_l.wait_recv()
                for c in self.on_r:
                    c.start()

        def wait_own(self):
            for c in self.mine:
                c.wait_recv()

        def wait(self):
            @pl.when(has_l)
            def _():
                for c in self.on_l:
                    c.wait_recv()

            @pl.when(has_r)
            def _():
                for c in self.on_r:
                    c.wait_recv()

        def sent(self):
            for c in self.mine:
                c.wait_send()

            @pl.when(has_l)
            def _():
                self.to_l.wait_send()
                for c in self.on_l:
                    c.wait_send()

            @pl.when(has_r)
            def _():
                self.to_r.wait_send()
                for c in self.on_r:
                    c.wait_send()

    def gather_rows(buf):
        own = buf.at[quarter(mp)]
        copies = [net.remote(own, own, mp=peer(d)) for d in (1, 2, 3)]
        for c in copies:
            c.start()
        return copies

    def scatter_sum_start(buf, into):
        copies = [
            net.remote(buf.at[quarter(peer(d))], into.at[d - 1], mp=peer(d)) for d in (1, 2, 3)
        ]
        for c in copies:
            c.start()
        return copies

    def landed(copies):
        for c in copies:
            c.wait_recv()

    late = []

    def lanes_at(q):
        return pl.ds(pl.multiple_of(128 * q, 128), 128)

    def spread_columns(src, dst):
        copies = [
            net.remote(src.at[:, lanes_at(peer(d))], dst.at[quarter(mp)], mp=peer(d))
            for d in (1, 2, 3)
        ]
        for c in copies:
            c.start()
        late.extend(copies)
        dst[quarter(mp)] = src[:, lanes_at(mp)]
        return copies

    def return_rows(product, send, recv, side_send, side_recv, fill, between):
        for blk in range(3):
            part = product(blk)
            for q in range(4):
                send[q, blk] = part[RQ * q : RQ * q + RQ].astype(BF16)
        copies = [net.remote(send.at[peer(d)], recv.at[d - 1], mp=peer(d)) for d in (1, 2, 3)]
        for c in copies:
            c.start()
        fill()
        landed(copies)
        late.extend(copies)

        def total(blk):
            out = send[mp, blk].astype(F32)
            for d in range(3):
                out = out + recv[d, blk].astype(F32)
            return out

        side_send[0] = total(0).astype(BF16)
        side_send[1] = total(2).astype(BF16)
        to_l = net.remote(side_send.at[0], side_recv.at[1], side="l", res=res - 1)
        to_r = net.remote(side_send.at[1], side_recv.at[0], side="r", res=res + 1)
        pl.when(has_l)(to_l.start)
        pl.when(has_r)(to_r.start)
        mid = total(1)
        between()
        pl.when(has_l)(to_r.wait_recv)
        pl.when(has_r)(to_l.wait_recv)
        pl.when(has_l)(to_l.wait_send)
        pl.when(has_r)(to_r.wait_send)
        return mid + side_recv[0].astype(F32) + side_recv[1].astype(F32)

    spread_msg_in.start()
    spread_msg_out.start()
    load_nodes.wait()

    @pl.loop(0, RB // 16)
    def _(i):
        A.win1[rows_at(RB + 16 * i, 16)] = A.nodes_v[rows_at(16 * i, 16)].astype(BF16)

    halo = Halo(A.win1)
    halo.start()
    for win in (A.win1, A.win2, A.win3):
        clear_sides(win)
    for ref in (A.back_side_a, A.back_side_b):
        ref[...] = jnp.zeros_like(ref)

    load_nbr.wait()
    load_mask.wait()
    load_edges.wait()
    stack = jnp.concatenate(
        [A.nbr_v[...].astype(F32), A.mask_v[...].astype(F32), jnp.zeros((128 - 2 * K, RB), F32)],
        axis=0,
    )
    stack = jnp.concatenate([stack, jnp.zeros((128, 256 - RB), F32)], axis=1)
    A.columns[...] = jnp.transpose(stack)[0:RB]
    columns = A.columns[rows_at(RQ * mp, RQ)]
    local = columns[:, 0:K].astype(jnp.int32) - (res - 1) * RB + DE
    live = columns[:, K : 2 * K]
    mean_weight = live / jnp.maximum(jnp.sum(live, axis=1, keepdims=True), 1.0)
    lane256 = lax.broadcasted_iota(jnp.int32, (RQ, 256), 1)
    lane512 = lax.broadcasted_iota(jnp.int32, (RQ, 512), 1) + 256
    is_edge = lane256 < DE

    def pair_load(buf, base):
        even = buf[:, pl.ds(base, 256)]
        odd = pltpu.roll(buf[:, pl.ds(base + 128, 256)], 192, 1)
        return jnp.where(is_edge, even, 0.0), jnp.where(is_edge, odd, 0.0)

    def pair_store(buf, base, even, odd, sub=slice(None)):
        back = pltpu.roll(odd, 64, 1)
        buf[sub, pl.ds(base, 128)] = even[:, :128].astype(buf.dtype)
        buf[sub, pl.ds(base + 128, 128)] = (even[:, 128:] + back[:, :128]).astype(buf.dtype)
        buf[sub, pl.ds(base + 256, 128)] = back[:, 128:].astype(buf.dtype)

    for j in range(K // 2):
        both = pair_load(A.e_v, 384 * j)
        for p in range(2):
            k = 2 * j + p
            column = local[:, k : k + 1]
            hot = jnp.where(column == lane256, 1.0, 0.0)
            A.XE[RQ * k : RQ * k + RQ] = jnp.where(is_edge, both[p], hot).astype(BF16)
            A.XO[RQ * k : RQ * k + RQ] = jnp.where(column == lane512, 1.0, 0.0).astype(BF16)
            A.WB[RQ * k : RQ * k + RQ] = jnp.broadcast_to(mean_weight[:, k : k + 1], (RQ, 128))

    halo.forward()

    full = E // 128

    @pl.loop(0, full)
    def _(c):
        at = pl.ds(pl.multiple_of(128 * c, 128), 128)
        A.XT[0:256, at] = A.XE[at].T
        A.XT[256:768, at] = A.XO[at].T

    if E % 128:
        at = slice(full * 128, E)
        A.XT[0:256, at] = A.XE[at].T
        A.XT[256:768, at] = A.XO[at].T

    spread_msg_in.forward()
    halo.wait()

    gain_a = A.gain_a[...]
    gain_b = A.gain_b[...]
    load_msg_in.wait()
    load_msg_out.wait()

    def node_table(win):
        for blk in (1, 0, 2):
            part = dot(win[RB * blk : RB * blk + RB], A.Wm[D : 2 * D])
            A.T[DE + RB * blk : DE + RB * blk + RB] = part.astype(BF16)

    def message_mean(win, keep):
        A.selfs[...] = dot(win[quarter(mp, RB)], A.Wm[0:D])
        A.total[...] = jnp.zeros((RQ, HM), F32)

        @pl.loop(0, E // EC)
        def _(c):
            rows = rows_at(EC * c, EC)
            left = jnp.concatenate([A.XE[rows], A.XO[rows]], axis=1)
            A.base[:, 0:HM] = dot(left, A.T[...])

            @pl.loop(0, RQ // 16)
            def _(sub):
                own = rows_at(16 * sub, 16)
                mine = A.selfs[own]
                total = A.total[own]
                for k in range(6):
                    v = A.base[rows_at(RQ * k + 16 * sub, 16), 0:HM] + mine
                    at = rows_at(EC * c + RQ * k + 16 * sub, 16)
                    w = jnp.concatenate([A.WB[at]] * (HM // 128), axis=1)
                    phi = bell(v)
                    if keep:
                        A.slope[at] = (w * bell_slope(phi, v)).astype(BF16)
                    total = total + w * (v * phi)
                A.total[own] = total

        A.avg[...] = A.total[...].astype(BF16)

    def node_tail(states, ug, part_b, part_r, keep):
        normed_a, inverse_a = norm_parts(states + dot(A.avg[...], A.Wo[...]), D)
        middle = normed_a * gain_a
        ug[quarter(mp)] = middle.astype(BF16)
        moved = gather_rows(ug)
        landed(moved)
        late.extend(moved)
        A.hid[...] = dot(ug[...], A.fi_v[...])

        @pl.loop(0, RB // 16)
        def _(i):
            rows = rows_at(16 * i, 16)
            v = A.hid[rows]
            phi = bell(v)
            A.smooth[rows] = (v * phi).astype(BF16)
            if keep:
                A.hslope[rows] = bell_slope(phi, v)

        A.part[...] = dot(A.smooth[...], A.fo_v[...])
        part_b[...] = A.part[...].astype(BF16)
        moved = scatter_sum_start(part_b, part_r)
        total = middle + A.part[quarter(mp)]
        landed(moved)
        late.extend(moved)
        for d in range(3):
            total = total + part_r[d].astype(F32)
        normed_b, inverse_b = norm_parts(total, D)
        if keep:
            A.normed_a[...] = normed_a
            A.inverse_a[...] = jnp.broadcast_to(inverse_a, (RQ, 128))
            A.normed_b[...] = normed_b
            A.inverse_b[...] = jnp.broadcast_to(inverse_b, (RQ, 128))
        return normed_b * gain_b

    spread_msg_in.wait()
    spread_edge[0].start()
    spread_edge[1].start()
    A.T[0:DE] = A.Wm[2 * D : 2 * D + DE]
    node_table(A.win1)
    message_mean(A.win1, False)
    spread_msg_out.forward()
    spread_msg_out.wait()
    load_ffn_in.wait()
    load_ffn_out.wait()
    own_nodes = A.nodes_v[quarter(mp)]
    predicted = node_tail(own_nodes, A.ug1, A.pb1, A.pr1, False)
    A.mixed[...] = 0.5 * (own_nodes + predicted)
    A.win2[quarter(mp, RB)] = A.mixed[...].astype(BF16)
    window2 = Window(A.win2)
    window2.start()
    window2.forward()
    window2.wait_own()
    window2.wait()
    spread_edge[2].start()
    spread_edge[3].start()
    spread_edge[0].forward()
    spread_edge[1].forward()
    node_table(A.win2)
    message_mean(A.win2, True)
    move_avg = spread_columns(A.avg, A.avg_all)
    spread_edge[2].forward()
    spread_edge[3].forward()
    settled = node_tail(A.mixed[...], A.ug2, A.pb2, A.pr2, True)
    A.win3[quarter(mp, RB)] = settled.astype(BF16)
    window3 = Window(A.win3)
    window3.start()
    window3.forward()

    for c in (*spread_edge, *load_edge_weights):
        c.wait()
    A.Eop[...] = jnp.concatenate([A.Eo[...], jnp.zeros((HE, 64), BF16)], axis=1)
    A.Te[0:DE] = A.We[:, 2 * D : 2 * D + DE].T
    window3.wait_own()
    window3.wait()
    store = [net.copy(A.win3.at[RB : 2 * RB], A.out_nodes)]

    for blk in (1, 0, 2):
        part = dot_bt(A.win3[RB * blk : RB * blk + RB], A.We[:, D : 2 * D])
        A.Te[DE + RB * blk : DE + RB * blk + RB] = part.astype(BF16)
    A.selfe[...] = dot_bt(A.win3[quarter(mp, RB)], A.We[:, 0:D])
    A.dself[...] = jnp.zeros((RQ, HE), F32)
    load_edge_cot.wait()
    gain_c = jnp.concatenate([A.gain_c[...], jnp.zeros((1, 256 - DE), F32)], axis=1)

    def norm_parts_e(values):
        scale = 1.0 / DE
        mean = jnp.sum(values, axis=-1, keepdims=True) * scale
        centred = jnp.where(is_edge, values - mean, 0.0)
        inverse = lax.rsqrt(jnp.sum(centred * centred, axis=-1, keepdims=True) * scale + EPSILON)
        return centred * inverse, inverse

    chunks = E // EC
    stream = net.reserve(3 * chunks)

    def new_part(q, c):
        return A.new_edges.at[quarter(q), pl.ds(pl.multiple_of(6 * DE * c, 128), 6 * DE)]

    def stream_copies(make, c):
        return (
            make(stream + c, new_part(mp, c), new_part(mp, c), mp=pair),
            make(stream + chunks + c, new_part(mp, c), new_part(mp, c), mp=cross),
            make(stream + 2 * chunks + c, new_part(cross, c), new_part(cross, c), mp=pair),
        )

    def edge_chunk(c, gain_total):
        rows = rows_at(EC * c, EC)
        A.base[...] = dot(A.XO[rows], A.Te[256:768])
        A.pre2[...] = dot(A.XE[rows], A.Te[0:256])

        @pl.loop(0, EC // 16)
        def _(b):
            at = rows_at(16 * b, 16)
            base = A.base[at] + A.selfe[rows_at(16 * (b % (RQ // 16)), 16)]
            A.base[at] = base
            v = base + A.pre2[at]
            phi = bell(v)
            A.G[at] = (v * phi).astype(BF16)

        A.upd[...] = dot(A.G[...], A.Eop[...])
        for j in range(3):
            both = pair_load(A.e_v, pl.multiple_of(1152 * c + 384 * j, 128))
            for p in range(2):
                k = 2 * j + p
                mine = slice(RQ * k, RQ * k + RQ)
                at = rows_at(EC * c + RQ * k, RQ)
                normed, _ = norm_parts_e(both[p] + A.upd[mine])
                mixed = 0.5 * (both[p] + normed * gain_c)
                A.emix[mine] = mixed
                A.XM[at] = jnp.where(is_edge, mixed, A.XE[at].astype(F32)).astype(BF16)

        A.pre2[...] = dot(A.XM[rows], A.Te[0:256])

        @pl.loop(0, EC // 16)
        def _(b):
            at = rows_at(16 * b, 16)
            v = A.base[at] + A.pre2[at]
            phi = bell(v)
            A.G2[rows_at(EC * c + 16 * b, 16)] = (v * phi).astype(BF16)
            A.base[at] = bell_slope(phi, v)

        A.upd[...] = dot(A.G2[rows], A.Eop[...])
        for j in range(3):
            lanes = pl.multiple_of(1152 * c + 384 * j, 128)
            cots = pair_load(A.ec_v, lanes)
            news = []
            for p in range(2):
                k = 2 * j + p
                mine = slice(RQ * k, RQ * k + RQ)
                normed, inverse = norm_parts_e(A.emix[mine] + A.upd[mine])
                news.append(normed * gain_c)
                gain_total = gain_total + jnp.sum(
                    (cots[p] * normed).reshape(RQ // 8, 8, 256), axis=0
                )
                d_sum = jnp.where(is_edge, norm_back(cots[p], normed, inverse, gain_c, DE), 0.0)
                A.emix[mine] = d_sum
                A.DO[rows_at(EC * c + RQ * k, RQ)] = d_sum.astype(BF16)
            pair_store(A.new_edges, lanes, news[0], news[1], quarter(mp))

        to_pair, to_cross, _ = stream_copies(net.at, c)
        to_cross.start()
        to_pair.start()

        @pl.when(c > 0)
        def _():
            _, arrived, on = stream_copies(net.at, c - 1)
            arrived.wait_recv()
            on.start()


        A.pre2[...] = dot_bt(A.DO[rows], A.Eop[...])

        @pl.loop(0, EC // 16)
        def _(b):
            at = rows_at(16 * b, 16)
            own = rows_at(16 * (b % (RQ // 16)), 16)
            d = (A.pre2[at] * A.base[at]).astype(BF16)
            A.DP2[rows_at(EC * c + 16 * b, 16)] = d
            A.dself[own] = A.dself[own] + d.astype(F32)

        A.EG[rows] = 0.5 * (A.emix[...] + dot_bt(A.DP2[rows], A.Te[0:256]))
        return gain_total

    gain_total = lax.fori_loop(0, E // EC, edge_chunk, jnp.zeros((8, 256), F32))
    A.gains[...] = jnp.zeros_like(A.gains)
    A.gains[2:3, 0:256] = jnp.sum(gain_total, axis=0, keepdims=True)

    streams = [stream_copies(net.opened, c) for c in range(chunks - 1)]
    last_pair, last_cross, _ = stream_copies(net.opened, chunks - 1)
    on_last = net.remote(new_part(cross, chunks - 1), new_part(cross, chunks - 1), mp=pair)

    A.dself_low[...] = A.dself[...].astype(BF16)
    for q in range(4):
        more = A.dself[:, 4 * big + 128 * (q // 2) : 4 * big + 128 * (q // 2) + 128]
        if q % 2:
            more = pltpu.roll(more, 64, 1)
        A.ds_send[q, :, 0:128] = A.dself_low[:, 128 * q : 128 * q + 128]
        A.ds_send[q, :, 128:256] = more.astype(BF16)
    move_ds = [
        net.remote(A.ds_send.at[peer(d)], A.ds_all.at[quarter(mp)], mp=peer(d)) for d in (1, 2, 3)
    ]
    for c in move_ds:
        c.start()
    late.extend(move_ds)
    A.ds_all[quarter(mp)] = A.ds_send[mp]
    for blk in range(3):
        at = slice(RB * blk, RB * blk + RB)
        A.dq[at] = dot(A.XT[DE + RB * blk : DE + RB * blk + RB], A.DP2[...]).astype(BF16)

    load_node_cot.wait()

    def emit_edge(tile, value):
        for q in range(4):
            at = DE * tile
            A.ge[q, at : at + big] = value[big * q : big * q + big].astype(BF16)
            more = 4 * big + small * q
            A.ge[q, at + big : at + DE] = value[more : more + small].astype(BF16)

    def emit_msg(row, value):
        n = value.shape[0]
        for q in range(4):
            A.gm[q, row : row + n] = value[:, 128 * q : 128 * q + 128].astype(BF16)

    def edge_weight_gradients():
        by_in = dot_at(A.XM[...], A.DP2[...])
        by_out = dot_at(A.DO[...], A.G2[...])
        emit_edge(4, jnp.transpose(by_in[0:128]))
        emit_edge(6, jnp.transpose(by_out[0:128]))
        emit_edge(
            5, jnp.transpose(jnp.concatenate([by_in[128:DE], by_out[128:DE]], axis=0))
        )
        for t in range(4):
            at = slice(128 * t, 128 * t + 128)
            emit_edge(t, jnp.transpose(dot_at(A.win3[:, at], A.dq[...])))
        pump(sum_edge)
        landed(move_ds)
        value = dot_at(A.ds_all[...], A.win3[RB : 2 * RB])
        for t in range(4):
            A.work_e[DE * t : DE * t + DE] = value[0:DE, 128 * t : 128 * t + 128].astype(BF16)

    def message_weight_gradients():
        for t in range(4):
            at = slice(128 * t, 128 * t + 128)
            emit_msg(128 * t, dot_at(A.win2[:, at], A.dq1[...]))
        emit_msg(D, dot(A.XT[0:DE], A.DP[...]))

    def own_message_gradients():
        landed(move_avg)
        landed(move_dg1)
        landed(move_dmsg)
        A.work_m[0:D] = dot_at(A.win2[RB : 2 * RB], A.dmsg_all[...]).astype(BF16)
        value = dot_at(A.avg_all[...], A.dg1_all[...])
        for u in range(4):
            row = 2 * D + DE + 128 * u
            A.work_m[row : row + 128] = value[:, 128 * u : 128 * u + 128].astype(BF16)

    for ref, used in ((A.work_e, 11 * DE), (A.work_m, 3 * D + DE)):
        if ref.shape[0] > used:
            ref[used:] = jnp.zeros((ref.shape[0] - used, 128), BF16)

    def reduce_mp(g, got, cuts, work, base):
        rows = g.shape[1]
        a1 = net.remote(g.at[pair], got.at[0], mp=pair)
        a2 = net.remote(g.at[third], got.at[1], mp=pair)
        a2.start()
        a1.start()
        yield
        a2.wait_recv()

        @pl.loop(0, rows // 32)
        def _(i):
            at = rows_at(32 * i, 32)
            got[1, at] = (g[cross, at].astype(F32) + got[1, at].astype(F32)).astype(BF16)

        step = rows // cuts
        pieces = []
        for i in range(cuts):
            at = pl.ds(step * i, step)
            b = net.remote(got.at[1, at], got.at[2, at], mp=cross)
            b.start()
            pieces.append(b)
            yield
        for c in (a1, *pieces):
            c.wait_recv()

        @pl.loop(0, rows // 32)
        def _(i):
            at = rows_at(32 * i, 32)
            total = g[mp, at].astype(F32) + got[0, at].astype(F32) + got[2, at].astype(F32)
            work[rows_at(base + 32 * i, 32)] = total.astype(BF16)

        for c in (a1, a2, *pieces):
            c.wait_send()

    def reduce_res(work, got, out, result):
        size = work.shape[0]
        low = 0
        used = 0
        halvings = range(S.bits - 2)
        for s in halvings:
            bit = (res // (1 << s)) % 2
            size = size // 2
            keep = low + bit * size
            give = low + (1 - bit) * size
            c = net.remote(
                work.at[rows_at(give, size, S.grain)], got.at[pl.ds(used, size)], res=across(s)
            )
            c.start()
            yield
            c.wait()

            @pl.loop(0, size // S.grain)
            def _(i, keep=keep, used=used):
                at = rows_at(keep + S.grain * i, S.grain, S.grain)
                there = rows_at(used + S.grain * i, S.grain, S.grain)
                work[at] = (work[at].astype(F32) + got[there].astype(F32)).astype(BF16)

            used += size
            low = keep
        me = res // stride
        size = size // 4
        copies = []
        for d in (2, 1, 3):
            there = (me + d) % 4
            c = net.remote(
                work.at[rows_at(low + there * size, size, S.grain)],
                got.at[pl.ds(used + (d - 1) * size, size)],
                res=res + (there - me) * stride,
            )
            c.start()
            copies.append(c)
        yield
        for c in copies:
            c.wait()
        own = low + me * size

        @pl.loop(0, size // S.grain)
        def _(i):
            at = rows_at(own + S.grain * i, S.grain, S.grain)
            total = work[at].astype(F32)
            for d in range(3):
                total = total + got[rows_at(used + d * size + S.grain * i, S.grain, S.grain)].astype(F32)
            out[at] = total.astype(BF16)

        here = out.at[rows_at(own, size, S.grain)]
        copies = []
        for d in (2, 1, 3):
            c = net.remote(here, here, res=res + ((me + d) % 4 - me) * stride)
            c.start()
            copies.append(c)
        yield
        for c in copies:
            c.wait()
        size = 4 * size
        for s in reversed(halvings):
            bit = (res // (1 << s)) % 2
            here = out.at[rows_at(low, size, S.grain)]
            c = net.remote(here, here, res=across(s))
            c.start()
            yield
            c.wait()
            low = low - bit * size
            size = 2 * size
        store.append(net.copy(out, result))

    def reduce_gains():
        copies = [net.remote(A.gains, A.gains_r.at[d - 1], mp=peer(d)) for d in (1, 2, 3)]
        for c in copies:
            c.start()
        yield
        for c in copies:
            c.wait()
        A.gains_t[0] = A.gains[...] + A.gains_r[0] + A.gains_r[1] + A.gains_r[2]
        for s in range(S.bits):
            c = net.remote(A.gains_t.at[s], A.gains_r.at[3 + s], res=across(s))
            c.start()
            yield
            c.wait()
            A.gains_t[s + 1] = A.gains_t[s] + A.gains_r[3 + s]
        store.append(net.copy(A.gains_t.at[S.bits], A.out_gains))

    def chain(*parts):
        for part in parts:
            yield from part

    def pump(*sums):
        for g in sums:
            next(g, None)

    sum_edge = chain(
        reduce_mp(A.ge, A.ge_r, 2, A.work_e, 4 * DE),
        reduce_res(A.work_e, A.sum_er, A.sum_e, A.pack_e),
    )
    sum_in = reduce_res(A.grad_i, A.sum_ir, A.sum_i, A.pack_i)
    sum_out = reduce_res(A.grad_o, A.sum_or, A.sum_o, A.pack_o)
    sum_msg = chain(
        reduce_mp(A.gm, A.gm_r, 1, A.work_m, D),
        reduce_res(A.work_m, A.sum_mr, A.sum_m, A.pack_m),
    )
    sum_gains = reduce_gains()

    def between_a():
        last_cross.wait_recv()
        on_last.start()
        pump(sum_edge)

    d_settled = A.nc_v[...] + dot(A.dself_low[...], A.We[:, 0:D])
    d_settled = d_settled + return_rows(
        lambda blk: dot(A.dq[RB * blk : RB * blk + RB], A.We[:, D : 2 * D]),
        A.back_send_a,
        A.back_recv_a,
        A.back_side_send_a,
        A.back_side_a,
        edge_weight_gradients,
        between_a,
    )

    normed_b = A.normed_b[...]
    d_sum_b = norm_back(d_settled, normed_b, A.inverse_b[:, 0:1], gain_b, D)
    A.gains[1:2] = jnp.sum(d_settled * normed_b, axis=0, keepdims=True)
    A.dF[quarter(mp)] = d_sum_b.astype(BF16)
    moved = gather_rows(A.dF)
    landed(moved)
    late.extend(moved)
    A.hid[...] = dot_bt(A.dF[...], A.fo_v[...])

    @pl.loop(0, RB // 16)
    def _(i):
        rows = rows_at(16 * i, 16)
        A.dT[rows] = (A.hid[rows] * A.hslope[rows]).astype(BF16)

    A.part[...] = dot_bt(A.dT[...], A.fi_v[...])
    A.pb3[...] = A.part[...].astype(BF16)
    moved = scatter_sum_start(A.pb3, A.pr3)
    pump(sum_edge)
    A.grad_i[...] = dot_at(A.ug2[...], A.dT[...]).astype(BF16)
    pump(sum_in)
    A.grad_o[...] = dot_at(A.smooth[...], A.dF[...]).astype(BF16)
    pump(sum_out)
    d_middle = d_sum_b + A.part[quarter(mp)]
    landed(moved)
    late.extend(moved)
    for d in range(3):
        d_middle = d_middle + A.pr3[d].astype(F32)
    normed_a = A.normed_a[...]
    d_sum_a = norm_back(d_middle, normed_a, A.inverse_a[:, 0:1], gain_a, D)
    A.gains[0:1] = jnp.sum(d_middle * normed_a, axis=0, keepdims=True)
    pump(sum_gains)
    A.dsa[...] = d_sum_a
    A.dg1[...] = d_sum_a.astype(BF16)
    A.dg1_all[quarter(mp)] = A.dg1[...]
    move_dg1 = gather_rows(A.dg1_all)
    late.extend(move_dg1)
    A.davg[...] = dot_bt(A.dg1[...], A.Wo[...])

    for sub in range(RQ // 16):
        mine = A.davg[16 * sub : 16 * sub + 16]

        def back_step(k, total, sub=sub, mine=mine):
            rows = rows_at(RQ * k + 16 * sub, 16)
            d = (mine * A.slope[rows].astype(F32)).astype(BF16)
            A.DP[rows] = d
            return total + d.astype(F32)

        total = lax.fori_loop(0, K, back_step, jnp.zeros((16, HM), F32))
        A.dmsg_low[16 * sub : 16 * sub + 16] = total.astype(BF16)

    move_dmsg = spread_columns(A.dmsg_low, A.dmsg_all)
    pump(sum_edge)
    for blk in range(3):
        at = slice(RB * blk, RB * blk + RB)
        A.dq1[at] = dot(A.XT[DE + RB * blk : DE + RB * blk + RB], A.DP[...]).astype(BF16)

    message_weight_gradients()
    pump(sum_msg, sum_in, sum_gains)
    own_message_gradients()
    pump(sum_msg)

    def edge_gradient(start, stop):
        @pl.loop(start, stop)
        def _(c):
            rows = rows_at(EC * c, EC)
            A.EG[rows] = A.EG[rows] + dot_bt(A.DP[rows], A.T[0:256])
            for j in range(3):
                lanes = pl.multiple_of(1152 * c + 384 * j, 128)
                ends = [
                    jnp.where(is_edge, A.EG[rows_at(EC * c + RQ * (2 * j + p), RQ)], 0.0)
                    for p in range(2)
                ]
                pair_store(A.ec_v, lanes, ends[0], ends[1])

    def close_edges():
        store.append(net.copy(A.ec_v, A.out_edge_grad))
        for a, b, c in streams:
            a.wait()
            b.wait_send()
            c.wait()
        last_pair.wait()
        last_cross.wait_send()
        on_last.wait()
        store.append(net.copy(A.new_edges, A.out_edges))

    def fill_b():
        edge_gradient(0, 3)
        pump(sum_out, sum_gains)
        edge_gradient(3, chunks)
        close_edges()
        pump(sum_msg, sum_edge, sum_in)

    back = return_rows(
        lambda blk: dot_bt(A.dq1[RB * blk : RB * blk + RB], A.Wm[D : 2 * D]),
        A.back_send_b,
        A.back_recv_b,
        A.back_side_send_b,
        A.back_side_b,
        fill_b,
        lambda: pump(sum_out, sum_gains),
    )
    A.node_grad_v[...] = 0.5 * (A.dsa[...] + dot_bt(A.dmsg_low[...], A.Wm[0:D]) + back)
    store.append(net.copy(A.node_grad_v, A.out_node_grad))

    work = [sum_in, sum_out, sum_edge, sum_msg, sum_gains]
    while work:
        for g in list(work):
            try:
                next(g)
            except StopIteration:
                work.remove(g)
    for c in store:
        c.wait()
    for s in (spread_msg_in, spread_msg_out, *spread_edge, halo, window2, window3):
        s.sent()
    for c in late:
        c.wait_send()
    assert net.remote_count <= S.remote and net.local_count <= S.local


def build(S):
    E = S.RQ * S.K
    W = 3 * S.RB
    EC = 6 * S.RQ
    grain = S.grain * S.n_res
    rows_e = up(11 * S.DE, grain)
    rows_m = up(3 * S.D + S.DE, grain)
    in_names = ["nodes", "edges", "neighbours", "edge_mask", "msg_in", "msg_out", "gain_a"]
    in_names += ["ffn_in", "ffn_out", "gain_b", "edge_in", "edge_out", "gain_c"]
    in_names += ["node_cot", "edge_cot"]
    outs = dict(
        out_nodes=((S.RB, S.D), BF16),
        out_edges=((S.RB, S.K * S.DE), BF16),
        out_node_grad=((S.RQ, S.D), F32),
        out_edge_grad=((S.RQ, S.K * S.DE), F32),
        pack_e=((rows_e, 128), BF16),
        pack_i=((S.D, S.FL), BF16),
        pack_o=((S.FL, S.D), BF16),
        pack_m=((rows_m, 128), BF16),
        out_gains=((8, S.D), F32),
    )
    scratch = dict(
        nodes_v=((S.RB, S.D), F32),
        nbr_v=((S.K, S.RB), jnp.int32),
        mask_v=((S.K, S.RB), jnp.int32),
        columns=((S.RB, 128), F32),
        new_edges=((S.RB, S.K * S.DE), BF16),
        node_grad_v=((S.RQ, S.D), F32),
        e_v=((S.RQ, S.K * S.DE), F32),
        ec_v=((S.RQ, S.K * S.DE), F32),
        nc_v=((S.RQ, S.D), F32),
        Wm=((2 * S.D + S.DE, S.HM), BF16),
        Wo=((S.HM, S.D), BF16),
        fi_v=((S.D, S.FL), BF16),
        fo_v=((S.FL, S.D), BF16),
        We=((S.HE, 2 * S.D + S.DE), BF16),
        Eo=((S.HE, S.DE), BF16),
        Eop=((S.HE, 256), BF16),
        win1=((W, S.D), BF16),
        win2=((W, S.D), BF16),
        win3=((W, S.D), BF16),
        XE=((E, 256), BF16),
        XM=((E, 256), BF16),
        XO=((E, 512), BF16),
        XT=((768, E), BF16),
        WB=((E, 128), F32),
        T=((768, S.HM), BF16),
        Te=((768, S.HE), BF16),
        selfs=((S.RQ, S.HM), F32),
        selfe=((S.RQ, S.HE), F32),
        total=((S.RQ, S.HM), F32),
        slope=((E, S.HM), BF16),
        avg=((S.RQ, S.HM), BF16),
        ug1=((S.RB, S.D), BF16),
        ug2=((S.RB, S.D), BF16),
        hid=((S.RB, S.FL), F32),
        smooth=((S.RB, S.FL), BF16),
        hslope=((S.RB, S.FL), F32),
        part=((S.RB, S.D), F32),
        pb1=((S.RB, S.D), BF16),
        pb2=((S.RB, S.D), BF16),
        pb3=((S.RB, S.D), BF16),
        pr1=((3, S.RQ, S.D), BF16),
        pr2=((3, S.RQ, S.D), BF16),
        pr3=((3, S.RQ, S.D), BF16),
        normed_a=((S.RQ, S.D), F32),
        normed_b=((S.RQ, S.D), F32),
        inverse_a=((S.RQ, 128), F32),
        inverse_b=((S.RQ, 128), F32),
        mixed=((S.RQ, S.D), F32),
        base=((EC, S.HE), F32),
        pre2=((EC, S.HE), F32),
        G=((EC, S.HE), BF16),
        upd=((EC, 256), F32),
        emix=((EC, 256), F32),
        G2=((E, S.HE), BF16),
        DO=((E, 256), BF16),
        DP2=((E, S.HE), BF16),
        EG=((E, 256), F32),
        dself=((S.RQ, S.HE), F32),
        dself_low=((S.RQ, S.HE), BF16),
        dq=((W, S.HE), BF16),
        gains=((8, S.D), F32),
        gains_r=((3 + S.bits, 8, S.D), F32),
        gains_t=((1 + S.bits, 8, S.D), F32),
        back_send_a=((4, 3, S.RQ, S.D), BF16),
        back_recv_a=((3, 3, S.RQ, S.D), BF16),
        back_side_send_a=((2, S.RQ, S.D), BF16),
        back_side_a=((2, S.RQ, S.D), BF16),
        back_send_b=((4, 3, S.RQ, S.D), BF16),
        back_recv_b=((3, 3, S.RQ, S.D), BF16),
        back_side_send_b=((2, S.RQ, S.D), BF16),
        back_side_b=((2, S.RQ, S.D), BF16),
        dF=((S.RB, S.D), BF16),
        dT=((S.RB, S.FL), BF16),
        dsa=((S.RQ, S.D), F32),
        dg1=((S.RQ, S.D), BF16),
        davg=((S.RQ, S.HM), F32),
        DP=((E, S.HM), BF16),
        dmsg_low=((S.RQ, S.HM), BF16),
        dq1=((W, S.HM), BF16),
        ge=((4, 7 * S.DE, 128), BF16),
        ge_r=((3, 7 * S.DE, 128), BF16),
        work_e=((rows_e, 128), BF16),
        ds_send=((4, S.RQ, 256), BF16),
        ds_all=((S.RB, 256), BF16),
        avg_all=((S.RB, 128), BF16),
        dg1_all=((S.RB, S.D), BF16),
        dmsg_all=((S.RB, 128), BF16),
        sum_er=((rows_e, 128), BF16),
        sum_e=((rows_e, 128), BF16),
        grad_i=((S.D, S.FL), BF16),
        sum_ir=((S.D, S.FL), BF16),
        sum_i=((S.D, S.FL), BF16),
        grad_o=((S.FL, S.D), BF16),
        sum_or=((S.FL, S.D), BF16),
        sum_o=((S.FL, S.D), BF16),
        gm=((4, S.D + S.DE, 128), BF16),
        gm_r=((3, S.D + S.DE, 128), BF16),
        work_m=((rows_m, 128), BF16),
        sum_mr=((rows_m, 128), BF16),
        sum_m=((rows_m, 128), BF16),
    )
    names = list(scratch) + ["send", "recv", "local"]
    shapes = [pltpu.VMEM(*v) for v in scratch.values()] + [
        pltpu.SemaphoreType.DMA((S.remote,)),
        pltpu.SemaphoreType.DMA((S.remote,)),
        pltpu.SemaphoreType.DMA((S.local,)),
    ]
    body = functools.partial(kernel_body, S, in_names, list(outs), names)
    body.__name__ = "layer"
    gains = ("gain_a", "gain_b", "gain_c")
    return pl.pallas_call(
        body,
        name="layer",
        out_shape=[jax.ShapeDtypeStruct(*v) for v in outs.values()],
        in_specs=[VMEM if n in gains else ANY for n in in_names],
        out_specs=[ANY] * len(outs),
        scratch_shapes=shapes,
        compiler_params=pltpu.CompilerParams(
            collective_id=0, has_side_effects=True, vmem_limit_bytes=62 * 1024 * 1024
        ),
    )


def unpack_body(S, names, *refs):
    A = SimpleNamespace(**dict(zip(names, refs, strict=True)))
    D, DE, RB = S.D, S.DE, S.RB
    count = [0]

    def copy(src, dst):
        c = pltpu.make_async_copy(src, dst, A.sems.at[count[0]])
        count[0] += 1
        c.start()
        return c

    part = RB // 4
    edge_loads = [
        copy(A.in_edges.at[pl.ds(part * i, part)], A.edges_l.at[pl.ds(part * i, part)])
        for i in range(4)
    ]
    pairs = (
        (A.in_e, A.e_l),
        (A.in_i, A.i_l),
        (A.in_o, A.o_l),
        (A.in_m, A.m_l),
        (A.in_nodes, A.nodes_l),
        (A.in_gains, A.gains_l),
    )
    loads = [copy(*p) for p in pairs]
    grads = [copy(A.in_edge_grad, A.eg_l), copy(A.in_node_grad, A.ng_l)]
    stores = []
    for i in range(4):
        edge_loads[i].wait()

        @pl.loop(0, part // 16)
        def _(k, i=i):
            at = pl.ds(pl.multiple_of(part * i + 16 * k, 16), 16)
            A.edges_f[at] = A.edges_l[at].astype(F32)

        at = pl.ds(part * i, part)
        stores.append(copy(A.edges_f.at[at], A.o1.at[at]))
    for c in (*grads, *loads):
        c.wait()
    stores += [copy(A.eg_l, A.o3), copy(A.ng_l, A.o2)]

    def widen(src, dst, out, rows):
        @pl.loop(0, rows // 16)
        def _(k):
            at = pl.ds(pl.multiple_of(16 * k, 16), 16)
            dst[at] = src[at].astype(F32)

        stores.append(copy(dst, out))

    widen(A.i_l, A.i_f, A.o7, D)
    widen(A.o_l, A.o_f, A.o8, S.FL)
    widen(A.nodes_l, A.nodes_f, A.o0, RB)
    widen(A.m_l, A.m_f, A.o4, 2 * D + DE)
    for u in range(4):
        row = 2 * D + DE + 128 * u
        A.mo_f[:, 128 * u : 128 * u + 128] = A.m_l[row : row + 128].astype(F32)
    stores.append(copy(A.mo_f, A.o5))
    mixed = A.e_l[9 * DE : 10 * DE].astype(F32)
    for t in range(9):
        A.ei_f[:, 128 * t : 128 * t + 128] = A.e_l[DE * t : DE * t + DE].astype(F32)
    A.ei_f[:, 1152 : 1152 + 64] = mixed[:, 0:64]
    stores.append(copy(A.ei_f, A.o10))
    A.eo_f[:, 0:128] = A.e_l[10 * DE : 11 * DE].astype(F32)
    A.eo_f[:, 128:DE] = pltpu.roll(mixed, 64, 1)[:, 0:64]
    stores.append(copy(A.eo_f, A.o11))
    A.ga_f[...] = A.gains_l[0:1]
    A.gb_f[...] = A.gains_l[1:2]
    A.gc_f[...] = A.gains_l[2:3, 0:DE]
    for src, out in ((A.ga_f, A.o6), (A.gb_f, A.o9), (A.gc_f, A.o12)):
        stores.append(copy(src, out))
    for c in stores:
        c.wait()


def unpack(S, values):
    D, DE, RB, RQ, K, FL = S.D, S.DE, S.RB, S.RQ, S.K, S.FL
    ins = ["in_nodes", "in_edges", "in_node_grad", "in_edge_grad"]
    ins += ["in_e", "in_i", "in_o", "in_m", "in_gains"]
    shapes = [
        (RB, D),
        (RB, K * DE),
        (RQ, D),
        (RQ, K * DE),
        (2 * D + DE, S.HM // 4),
        (S.HM // 4, D),
        (1, D),
        (D, FL),
        (FL, D),
        (1, D),
        (S.HE // 4, 2 * D + DE),
        (S.HE // 4, DE),
        (1, DE),
    ]
    outs = ["o%d" % i for i in range(13)]
    scratch = dict(
        edges_l=((RB, K * DE), BF16),
        edges_f=((RB, K * DE), F32),
        e_l=(values[4].shape, BF16),
        i_l=((D, FL), BF16),
        o_l=((FL, D), BF16),
        m_l=(values[7].shape, BF16),
        nodes_l=((RB, D), BF16),
        gains_l=((8, D), F32),
        eg_l=((RQ, K * DE), F32),
        ng_l=((RQ, D), F32),
        i_f=((D, FL), F32),
        o_f=((FL, D), F32),
        nodes_f=((RB, D), F32),
        m_f=(shapes[4], F32),
        mo_f=(shapes[5], F32),
        ei_f=(shapes[10], F32),
        eo_f=(shapes[11], F32),
        ga_f=(shapes[6], F32),
        gb_f=(shapes[9], F32),
        gc_f=(shapes[12], F32),
    )
    names = ins + outs + list(scratch) + ["sems"]
    body = functools.partial(unpack_body, S, names)
    return list(
        pl.pallas_call(
            body,
            name="unpack",
            out_shape=[jax.ShapeDtypeStruct(x, F32) for x in shapes],
            in_specs=[ANY] * len(ins),
            out_specs=[ANY] * len(outs),
            scratch_shapes=[pltpu.VMEM(*v) for v in scratch.values()]
            + [pltpu.SemaphoreType.DMA((32,))],
            compiler_params=pltpu.CompilerParams(vmem_limit_bytes=62 * 1024 * 1024),
        )(*values)
    )


STOP = 0


def on_device(n_res, *args):
    nodes, edges, neighbours, _, _, _, _, ffn_in = args[:8]
    height = nodes.shape[0]
    degree = neighbours.shape[1]
    S = SimpleNamespace(
        n_res=n_res,
        bits=int(math.log2(n_res)),
        RB=height,
        RQ=height // 4,
        K=degree,
        D=nodes.shape[1],
        DE=edges.shape[1] // degree,
        HM=args[4].shape[1] * 4,
        HE=args[10].shape[1] * 4,
        FL=ffn_in.shape[1],
        grain=16 if n_res <= 16 else 8,
        remote=200,
        local=32,
        stop=STOP,
    )
    fixed = [a.reshape(1, -1) if a.ndim == 1 else a for a in args]
    for i in (2, 3, 10):
        fixed[i] = fixed[i].T
    out = unpack(S, build(S)(*fixed))
    for i in (6, 9, 12):
        out[i] = out[i].reshape(-1)
    out[10] = out[10].T
    return tuple(out)


def solution(mesh):
    in_specs = (
        P("res", None),
        P("res", None),
        P("res", None),
        P("res", None),
        P(None, "mp"),
        P("mp", None),
        P(),
        P(None, "mp"),
        P("mp", None),
        P(),
        P(None, "mp"),
        P("mp", None),
        P(),
        P("res", None),
        P("res", None),
    )
    out_specs = (
        P("res", None),
        P("res", None),
        P(("res", "mp"), None),
        P(("res", "mp"), None),
        P(None, "mp"),
        P("mp", None),
        P(),
        P(None, "mp"),
        P("mp", None),
        P(),
        P(None, "mp"),
        P("mp", None),
        P(),
    )
    return jax.shard_map(
        functools.partial(on_device, mesh.shape["res"]),
        mesh=mesh,
        in_specs=in_specs,
        out_specs=out_specs,
        check_vma=False,
    )
```

```python
import functools
import math
from types import SimpleNamespace

import jax
import jax.numpy as jnp
from jax import lax
from jax.experimental import pallas as pl
from jax.experimental.pallas import tpu as pltpu
from jax.sharding import PartitionSpec as P

EPSILON = 1e-05
F32 = jnp.float32
BF16 = jnp.bfloat16
MESH = pl.DeviceIdType.MESH
ROOT_TWO_PI = 0.3989422804014327
ROOT_HALF = 0.7071067811865476
ANY = pl.BlockSpec(memory_space=pl.ANY)
VMEM = pl.BlockSpec(memory_space=pltpu.VMEM)


def dot(left, right):
    return jnp.dot(left, right, preferred_element_type=F32)


def dot_bt(left, right):
    return lax.dot_general(left, right, (((1,), (1,)), ((), ())), preferred_element_type=F32)


def dot_at(left, right):
    return lax.dot_general(left, right, (((0,), (0,)), ((), ())), preferred_element_type=F32)


def bell(v):
    return 0.5 + 0.5 * lax.erf(v * ROOT_HALF)


def bell_slope(phi, v):
    return phi + v * (jnp.exp(-0.5 * (v * v)) * ROOT_TWO_PI)


def norm_parts(values, width):
    scale = 1.0 / width
    centred = values - jnp.sum(values, axis=-1, keepdims=True) * scale
    inverse = lax.rsqrt(jnp.sum(centred * centred, axis=-1, keepdims=True) * scale + EPSILON)
    return centred * inverse, inverse


def norm_back(upstream, normed, inverse, gain, width):
    scale = 1.0 / width
    scaled = upstream * gain
    mean = jnp.sum(scaled, axis=-1, keepdims=True) * scale
    along = jnp.sum(scaled * normed, axis=-1, keepdims=True) * scale
    return inverse * (scaled - mean - normed * along)


def up(rows, step):
    return -(-rows // step) * step


def unrolled(count):
    def run(step):
        for i in range(count):
            step(i)

    return run


class Net:
    def __init__(self, send, recv, local):
        self.send, self.recv, self.local = send, recv, local
        self.remote_count = 0
        self.local_count = 0

    def remote(self, src, dst, side="", **where):
        i = self.remote_count
        self.remote_count += 1
        return pltpu.make_async_remote_copy(
            src_ref=src,
            dst_ref=dst,
            send_sem=self.send.at[i],
            recv_sem=self.recv.at[i],
            device_id=where,
            device_id_type=MESH,
        )

    def reserve(self, count):
        i = self.remote_count
        self.remote_count += count
        return i

    def at(self, i, src, dst, **where):
        return pltpu.make_async_remote_copy(
            src_ref=src,
            dst_ref=dst,
            send_sem=self.send.at[i],
            recv_sem=self.recv.at[i],
            device_id=where,
            device_id_type=MESH,
        )

    def opened(self, i, src, dst, **where):
        return self.at(i, src, dst, **where)

    def copy(self, src, dst):
        i = self.local_count
        self.local_count += 1
        c = pltpu.make_async_copy(src, dst, self.local.at[i])
        c.start()
        return c


def kernel_body(S, in_names, out_names, scratch_names, *refs):
    names = in_names + out_names + scratch_names
    A = SimpleNamespace(**dict(zip(names, refs, strict=True)))
    net = Net(A.send, A.recv, A.local)
    RB, RQ, K, D, DE, HM, HE, FL = S.RB, S.RQ, S.K, S.D, S.DE, S.HM, S.HE, S.FL
    E = RQ * K
    W = 3 * RB
    EC = 6 * RQ
    res = lax.axis_index("res")
    mp = lax.axis_index("mp")
    has_l = res > 0
    has_r = res < S.n_res - 1
    pair = mp + 1 - 2 * (mp % 2)
    cross = (mp + 2) % 4
    third = (pair + 2) % 4

    def peer(d):
        return (mp + d) % 4

    def rows_at(start, size, step=16):
        return pl.ds(pl.multiple_of(start, step), size)

    def quarter(q, base=0):
        return rows_at(base + RQ * q, RQ)

    load_nodes = net.copy(A.nodes, A.nodes_v)
    load_nbr = net.copy(A.neighbours, A.nbr_v)
    load_mask = net.copy(A.edge_mask, A.mask_v)
    load_edges = net.copy(A.edges.at[quarter(mp)], A.e_v)
    own_msg_in = A.Wm.at[:, pl.ds(pl.multiple_of(mp * 128, 128), 128)]
    load_msg_in = net.copy(A.msg_in, own_msg_in)
    own_msg_out = A.Wo.at[rows_at(mp * 128, 128)]
    load_msg_out = net.copy(A.msg_out, own_msg_out)
    load_ffn_in = net.copy(A.ffn_in, A.fi_v)
    load_ffn_out = net.copy(A.ffn_out, A.fo_v)
    big, small = HE // 4 // 3 * 2, HE // 4 // 3

    def main_rows(ref):
        return lambda q: ref.at[rows_at(big * q, big)]

    def rest_rows(ref):
        return lambda q: ref.at[rows_at(4 * big + small * q, small)]

    first, rest = pl.ds(0, big), pl.ds(big, small)
    edge_parts = (
        (A.edge_in.at[first], main_rows(A.We)),
        (A.edge_out.at[first], main_rows(A.Eo)),
        (A.edge_in.at[rest], rest_rows(A.We)),
        (A.edge_out.at[rest], rest_rows(A.Eo)),
    )
    load_edge_weights = [net.copy(src, place(mp)) for src, place in edge_parts]
    load_node_cot = net.copy(A.node_cot.at[quarter(mp)], A.nc_v)
    load_edge_cot = net.copy(A.edge_cot.at[quarter(mp)], A.ec_v)

    barrier = pltpu.get_barrier_semaphore()

    def greet(**where):
        pl.semaphore_signal(barrier, inc=1, device_id=where, device_id_type=MESH)

    def across(s):
        return res + (1 << s) * (1 - 2 * ((res // (1 << s)) % 2))

    for d in (1, 2, 3):
        greet(mp=peer(d))
    for s in range(S.bits - 2):
        greet(res=across(s))
    stride = S.n_res // 4
    for d in (1, 2, 3):
        greet(res=res + ((res // stride + d) % 4 - res // stride) * stride)

    @pl.when(has_l)
    def _():
        greet(res=res - 1)

    @pl.when(has_r)
    def _():
        greet(res=res + 1)

    sides = (res + S.n_res - 1) // S.n_res + 1 - (res + 1) // S.n_res
    pl.semaphore_wait(barrier, 6 + S.bits - 2 + sides)

    class Spread:
        def __init__(self, src, place):
            own = place(mp)
            self.first = [net.remote(src, own, mp=pair), net.remote(src, own, mp=cross)]
            self.then = net.remote(place(cross), place(cross), mp=pair)

        def start(self):
            for c in self.first:
                c.start()

        def forward(self):
            self.first[1].wait_recv()
            self.then.start()

        def wait(self):
            self.first[0].wait_recv()
            self.then.wait_recv()

        def sent(self):
            for c in self.first:
                c.wait_send()
            self.then.wait_send()

    spread_msg_in = Spread(
        A.msg_in, lambda q: A.Wm.at[:, pl.ds(pl.multiple_of(q * 128, 128), 128)]
    )
    spread_msg_out = Spread(A.msg_out, lambda q: A.Wo.at[rows_at(q * 128, 128)])
    spread_edge = [Spread(src, place) for src, place in edge_parts]

    def clear_sides(win):
        @pl.when(jnp.logical_not(has_l))
        def _():
            win[0:RB] = jnp.zeros((RB, D), BF16)

        @pl.when(jnp.logical_not(has_r))
        def _():
            win[2 * RB : 3 * RB] = jnp.zeros((RB, D), BF16)

    half = RB // 2

    class Halo:
        def __init__(self, win):
            h = mp % 2
            own = win.at[rows_at(RB + half * h, half)]
            left = win.at[rows_at(half * h, half)]
            right = win.at[rows_at(2 * RB + half * h, half)]
            self.to_l = net.remote(own, right, side="l", res=res - 1)
            self.to_r = net.remote(own, left, side="r", res=res + 1)
            self.on_l = net.remote(left, left, mp=pair)
            self.on_r = net.remote(right, right, mp=pair)

        def start(self):
            pl.when(has_l)(self.to_l.start)
            pl.when(has_r)(self.to_r.start)

        def forward(self):
            @pl.when(has_l)
            def _():
                self.to_r.wait_recv()
                self.on_l.start()

            @pl.when(has_r)
            def _():
                self.to_l.wait_recv()
                self.on_r.start()

        def wait(self):
            pl.when(has_l)(self.on_l.wait_recv)
            pl.when(has_r)(self.on_r.wait_recv)

        def sent(self):
            @pl.when(has_l)
            def _():
                self.to_l.wait_send()
                self.on_l.wait_send()

            @pl.when(has_r)
            def _():
                self.to_r.wait_send()
                self.on_r.wait_send()

    class Window:
        def __init__(self, win):
            own = win.at[quarter(mp, RB)]
            left = win.at[quarter(mp)]
            right = win.at[quarter(mp, 2 * RB)]
            self.to_l = net.remote(own, right, side="l", res=res - 1)
            self.to_r = net.remote(own, left, side="r", res=res + 1)
            self.mine = [net.remote(own, own, mp=peer(d)) for d in (1, 2, 3)]
            self.on_l = [net.remote(left, left, mp=peer(d)) for d in (1, 2, 3)]
            self.on_r = [net.remote(right, right, mp=peer(d)) for d in (1, 2, 3)]

        def start(self):
            pl.when(has_l)(self.to_l.start)
            pl.when(has_r)(self.to_r.start)
            for c in self.mine:
                c.start()

        def forward(self):
            @pl.when(has_l)
            def _():
                self.to_r.wait_recv()
                for c in self.on_l:
                    c.start()

            @pl.when(has_r)
            def _():
                self.to_l.wait_recv()
                for c in self.on_r:
                    c.start()

        def wait_own(self):
            for c in self.mine:
                c.wait_recv()

        def wait(self):
            @pl.when(has_l)
            def _():
                for c in self.on_l:
                    c.wait_recv()

            @pl.when(has_r)
            def _():
                for c in self.on_r:
                    c.wait_recv()

        def sent(self):
            for c in self.mine:
                c.wait_send()

            @pl.when(has_l)
            def _():
                self.to_l.wait_send()
                for c in self.on_l:
                    c.wait_send()

            @pl.when(has_r)
            def _():
                self.to_r.wait_send()
                for c in self.on_r:
                    c.wait_send()

    def gather_rows(buf):
        own = buf.at[quarter(mp)]
        copies = [net.remote(own, own, mp=peer(d)) for d in (1, 2, 3)]
        for c in copies:
            c.start()
        return copies

    def scatter_sum_start(buf, into):
        copies = [
            net.remote(buf.at[quarter(peer(d))], into.at[d - 1], mp=peer(d)) for d in (1, 2, 3)
        ]
        for c in copies:
            c.start()
        return copies

    def landed(copies):
        for c in copies:
            c.wait_recv()

    late = []

    def lanes_at(q):
        return pl.ds(pl.multiple_of(128 * q, 128), 128)

    def spread_columns(src, dst):
        copies = [
            net.remote(src.at[:, lanes_at(peer(d))], dst.at[quarter(mp)], mp=peer(d))
            for d in (1, 2, 3)
        ]
        for c in copies:
            c.start()
        late.extend(copies)
        dst[quarter(mp)] = src[:, lanes_at(mp)]
        return copies

    def return_rows(product, send, recv, side_send, side_recv, fill, between):
        for blk in range(3):
            part = product(blk)
            for q in range(4):
                send[q, blk] = part[RQ * q : RQ * q + RQ].astype(BF16)
        copies = [net.remote(send.at[peer(d)], recv.at[d - 1], mp=peer(d)) for d in (1, 2, 3)]
        for c in copies:
            c.start()
        fill()
        landed(copies)
        late.extend(copies)

        def total(blk):
            out = send[mp, blk].astype(F32)
            for d in range(3):
                out = out + recv[d, blk].astype(F32)
            return out

        side_send[0] = total(0).astype(BF16)
        side_send[1] = total(2).astype(BF16)
        to_l = net.remote(side_send.at[0], side_recv.at[1], side="l", res=res - 1)
        to_r = net.remote(side_send.at[1], side_recv.at[0], side="r", res=res + 1)
        pl.when(has_l)(to_l.start)
        pl.when(has_r)(to_r.start)
        mid = total(1)
        between()
        pl.when(has_l)(to_r.wait_recv)
        pl.when(has_r)(to_l.wait_recv)
        pl.when(has_l)(to_l.wait_send)
        pl.when(has_r)(to_r.wait_send)
        return mid + side_recv[0].astype(F32) + side_recv[1].astype(F32)

    spread_msg_in.start()
    spread_msg_out.start()
    load_nodes.wait()

    @unrolled(RB // 16)
    def _(i):
        A.win1[rows_at(RB + 16 * i, 16)] = A.nodes_v[rows_at(16 * i, 16)].astype(BF16)

    halo = Halo(A.win1)
    halo.start()
    for win in (A.win1, A.win2, A.win3):
        clear_sides(win)
    for ref in (A.back_side_a, A.back_side_b):
        ref[...] = jnp.zeros_like(ref)

    load_nbr.wait()
    load_mask.wait()
    load_edges.wait()
    stack = jnp.concatenate(
        [A.nbr_v[...].astype(F32), A.mask_v[...].astype(F32), jnp.zeros((128 - 2 * K, RB), F32)],
        axis=0,
    )
    stack = jnp.concatenate([stack, jnp.zeros((128, 256 - RB), F32)], axis=1)
    A.columns[...] = jnp.transpose(stack)[0:RB]
    columns = A.columns[rows_at(RQ * mp, RQ)]
    local = columns[:, 0:K].astype(jnp.int32) - (res - 1) * RB + DE
    live = columns[:, K : 2 * K]
    mean_weight = live / jnp.maximum(jnp.sum(live, axis=1, keepdims=True), 1.0)
    lane256 = lax.broadcasted_iota(jnp.int32, (RQ, 256), 1)
    lane512 = lax.broadcasted_iota(jnp.int32, (RQ, 512), 1) + 256
    is_edge = lane256 < DE

    def pair_load(buf, base):
        even = buf[:, pl.ds(base, 256)]
        odd = pltpu.roll(buf[:, pl.ds(base + 128, 256)], 192, 1)
        return jnp.where(is_edge, even, 0.0), jnp.where(is_edge, odd, 0.0)

    def pair_store(buf, base, even, odd, sub=slice(None)):
        back = pltpu.roll(odd, 64, 1)
        buf[sub, pl.ds(base, 128)] = even[:, :128].astype(buf.dtype)
        buf[sub, pl.ds(base + 128, 128)] = (even[:, 128:] + back[:, :128]).astype(buf.dtype)
        buf[sub, pl.ds(base + 256, 128)] = back[:, 128:].astype(buf.dtype)

    for j in range(K // 2):
        both = pair_load(A.e_v, 384 * j)
        for p in range(2):
            k = 2 * j + p
            column = local[:, k : k + 1]
            hot = jnp.where(column == lane256, 1.0, 0.0)
            A.XE[RQ * k : RQ * k + RQ] = jnp.where(is_edge, both[p], hot).astype(BF16)
            A.XO[RQ * k : RQ * k + RQ] = jnp.where(column == lane512, 1.0, 0.0).astype(BF16)
            A.WB[RQ * k : RQ * k + RQ] = jnp.broadcast_to(mean_weight[:, k : k + 1], (RQ, 128))

    halo.forward()

    full = E // 128

    @pl.loop(0, full)
    def _(c):
        at = pl.ds(pl.multiple_of(128 * c, 128), 128)
        A.XT[0:256, at] = A.XE[at].T
        A.XT[256:768, at] = A.XO[at].T

    if E % 128:
        at = slice(full * 128, E)
        A.XT[0:256, at] = A.XE[at].T
        A.XT[256:768, at] = A.XO[at].T

    spread_msg_in.forward()
    halo.wait()

    gain_a = A.gain_a[...]
    gain_b = A.gain_b[...]
    load_msg_in.wait()
    load_msg_out.wait()

    def node_table(win):
        for blk in (1, 0, 2):
            part = dot(win[RB * blk : RB * blk + RB], A.Wm[D : 2 * D])
            A.T[DE + RB * blk : DE + RB * blk + RB] = part.astype(BF16)

    def message_mean(win, keep):
        A.selfs[...] = dot(win[quarter(mp, RB)], A.Wm[0:D])
        A.total[...] = jnp.zeros((RQ, HM), F32)

        @pl.loop(0, E // EC)
        def _(c):
            rows = rows_at(EC * c, EC)
            left = jnp.concatenate([A.XE[rows], A.XO[rows]], axis=1)
            A.pre[...] = dot(left, A.T[...])

            @unrolled(RQ // 16)
            def _(sub):
                own = slice(16 * sub, 16 * sub + 16)
                mine = A.selfs[own]
                total = A.total[own]
                for k in range(6):
                    at = RQ * k + 16 * sub
                    v = A.pre[at : at + 16] + mine
                    there = rows_at(EC * c + at, 16)
                    w = jnp.concatenate([A.WB[there]] * (HM // 128), axis=1)
                    phi = bell(v)
                    if keep:
                        A.slope[there] = (w * bell_slope(phi, v)).astype(BF16)
                    total = total + w * (v * phi)
                A.total[own] = total

        A.avg[...] = A.total[...].astype(BF16)

    def node_tail(states, ug, part_b, part_r, keep):
        normed_a, inverse_a = norm_parts(states + dot(A.avg[...], A.Wo[...]), D)
        middle = normed_a * gain_a
        ug[quarter(mp)] = middle.astype(BF16)
        moved = gather_rows(ug)
        landed(moved)
        late.extend(moved)
        A.hid[...] = dot(ug[...], A.fi_v[...])

        @unrolled(RB // 16)
        def _(i):
            rows = rows_at(16 * i, 16)
            v = A.hid[rows]
            phi = bell(v)
            A.smooth[rows] = (v * phi).astype(BF16)
            if keep:
                A.hslope[rows] = bell_slope(phi, v)

        A.part[...] = dot(A.smooth[...], A.fo_v[...])
        part_b[...] = A.part[...].astype(BF16)
        moved = scatter_sum_start(part_b, part_r)
        total = middle + A.part[quarter(mp)]
        landed(moved)
        late.extend(moved)
        for d in range(3):
            total = total + part_r[d].astype(F32)
        normed_b, inverse_b = norm_parts(total, D)
        if keep:
            A.normed_a[...] = normed_a
            A.inverse_a[...] = jnp.broadcast_to(inverse_a, (RQ, 128))
            A.normed_b[...] = normed_b
            A.inverse_b[...] = jnp.broadcast_to(inverse_b, (RQ, 128))
        return normed_b * gain_b

    spread_msg_in.wait()
    spread_edge[0].start()
    spread_edge[1].start()
    A.T[0:DE] = A.Wm[2 * D : 2 * D + DE]
    node_table(A.win1)
    message_mean(A.win1, False)
    spread_msg_out.forward()
    spread_msg_out.wait()
    load_ffn_in.wait()
    load_ffn_out.wait()
    own_nodes = A.nodes_v[quarter(mp)]
    predicted = node_tail(own_nodes, A.ug1, A.pb1, A.pr1, False)
    A.mixed[...] = 0.5 * (own_nodes + predicted)
    A.win2[quarter(mp, RB)] = A.mixed[...].astype(BF16)
    window2 = Window(A.win2)
    window2.start()
    window2.forward()
    window2.wait_own()
    window2.wait()
    spread_edge[2].start()
    spread_edge[3].start()
    spread_edge[0].forward()
    spread_edge[1].forward()
    node_table(A.win2)
    message_mean(A.win2, True)
    move_avg = spread_columns(A.avg, A.avg_all)
    spread_edge[2].forward()
    spread_edge[3].forward()
    settled = node_tail(A.mixed[...], A.ug2, A.pb2, A.pr2, True)
    A.win3[quarter(mp, RB)] = settled.astype(BF16)
    window3 = Window(A.win3)
    window3.start()
    window3.forward()

    for c in (*spread_edge, *load_edge_weights):
        c.wait()
    A.Eop[...] = jnp.concatenate([A.Eo[...], jnp.zeros((HE, 64), BF16)], axis=1)
    A.Te[0:DE] = A.We[:, 2 * D : 2 * D + DE].T
    window3.wait_own()
    window3.wait()
    store = [net.copy(A.win3.at[RB : 2 * RB], A.out_nodes)]

    for blk in (1, 0, 2):
        part = dot_bt(A.win3[RB * blk : RB * blk + RB], A.We[:, D : 2 * D])
        A.Te[DE + RB * blk : DE + RB * blk + RB] = part.astype(BF16)
    A.selfe[...] = dot_bt(A.win3[quarter(mp, RB)], A.We[:, 0:D])
    A.dself[...] = jnp.zeros((RQ, HE), F32)
    load_edge_cot.wait()
    gain_c = jnp.concatenate([A.gain_c[...], jnp.zeros((1, 256 - DE), F32)], axis=1)

    def norm_parts_e(values):
        scale = 1.0 / DE
        mean = jnp.sum(values, axis=-1, keepdims=True) * scale
        centred = jnp.where(is_edge, values - mean, 0.0)
        inverse = lax.rsqrt(jnp.sum(centred * centred, axis=-1, keepdims=True) * scale + EPSILON)
        return centred * inverse, inverse

    chunks = E // EC
    stream = net.reserve(3 * chunks)

    def new_part(q, c):
        return A.new_edges.at[quarter(q), pl.ds(pl.multiple_of(6 * DE * c, 128), 6 * DE)]

    def stream_copies(make, c):
        return (
            make(stream + c, new_part(mp, c), new_part(mp, c), mp=pair),
            make(stream + chunks + c, new_part(mp, c), new_part(mp, c), mp=cross),
            make(stream + 2 * chunks + c, new_part(cross, c), new_part(cross, c), mp=pair),
        )

    def edge_chunk(c, part, gain_out):
        rows = rows_at(EC * c, EC)
        base, pre2, upd, emix, G = (x.at[part] for x in (A.base, A.pre2, A.upd, A.emix, A.G))
        base[...] = dot(A.XO[rows], A.Te[256:768])
        pre2[...] = dot(A.XE[rows], A.Te[0:256])
        yield

        @unrolled(EC // 16)
        def _(b):
            at = slice(16 * b, 16 * b + 16)
            own = 16 * (b % (RQ // 16))
            total = base[at] + A.selfe[own : own + 16]
            base[at] = total
            v = total + pre2[at]
            G[at] = (v * bell(v)).astype(BF16)

        yield
        upd[...] = dot(G[...], A.Eop[...])
        yield
        for j in range(3):
            both = pair_load(A.e_v, pl.multiple_of(1152 * c + 384 * j, 128))
            for p in range(2):
                k = 2 * j + p
                mine = slice(RQ * k, RQ * k + RQ)
                at = rows_at(EC * c + RQ * k, RQ)
                normed, _ = norm_parts_e(both[p] + upd[mine])
                mixed = 0.5 * (both[p] + normed * gain_c)
                emix[mine] = mixed
                A.XM[at] = jnp.where(is_edge, mixed, A.XE[at].astype(F32)).astype(BF16)

        yield
        pre2[...] = dot(A.XM[rows], A.Te[0:256])
        yield

        @unrolled(EC // 16)
        def _(b):
            at = slice(16 * b, 16 * b + 16)
            v = base[at] + pre2[at]
            phi = bell(v)
            A.G2[rows_at(EC * c + 16 * b, 16)] = (v * phi).astype(BF16)
            base[at] = bell_slope(phi, v)

        yield
        upd[...] = dot(A.G2[rows], A.Eop[...])
        yield
        gain_total = jnp.zeros((8, 256), F32)
        for j in range(3):
            lanes = pl.multiple_of(1152 * c + 384 * j, 128)
            cots = pair_load(A.ec_v, lanes)
            news = []
            for p in range(2):
                k = 2 * j + p
                mine = slice(RQ * k, RQ * k + RQ)
                normed, inverse = norm_parts_e(emix[mine] + upd[mine])
                news.append(normed * gain_c)
                gain_total = gain_total + jnp.sum(
                    (cots[p] * normed).reshape(RQ // 8, 8, 256), axis=0
                )
                d_sum = jnp.where(is_edge, norm_back(cots[p], normed, inverse, gain_c, DE), 0.0)
                emix[mine] = d_sum
                A.DO[rows_at(EC * c + RQ * k, RQ)] = d_sum.astype(BF16)
            pair_store(A.new_edges, lanes, news[0], news[1], quarter(mp))
        gain_out.append(gain_total)
        yield
        pre2[...] = dot_bt(A.DO[rows], A.Eop[...])
        yield

        @unrolled(RQ // 16)
        def _(sub):
            own = slice(16 * sub, 16 * sub + 16)
            total = A.dself[own]
            for k in range(6):
                at = slice(RQ * k + 16 * sub, RQ * k + 16 * sub + 16)
                d = (pre2[at] * base[at]).astype(BF16)
                A.DP2[rows_at(EC * c + RQ * k + 16 * sub, 16)] = d
                total = total + d.astype(F32)
            A.dself[own] = total

        yield
        A.EG[rows] = 0.5 * (emix[...] + dot_bt(A.DP2[rows], A.Te[0:256]))

    def send_chunk(c):
        to_pair, to_cross, _ = stream_copies(net.at, c)
        to_cross.start()
        to_pair.start()

        @pl.when(c > 0)
        def _():
            _, arrived, on = stream_copies(net.at, c - 1)
            arrived.wait_recv()
            on.start()

    def edge_chunks(i, gain_total):
        gains = []
        parts = [edge_chunk(2 * i + h, h, gains) for h in range(2)]
        next(parts[0])
        running = list(parts)
        while running:
            for g in list(running):
                try:
                    next(g)
                except StopIteration:
                    running.remove(g)
        for h in range(2):
            send_chunk(2 * i + h)
        return gain_total + gains[0] + gains[1]

    gain_total = lax.fori_loop(0, chunks // 2, edge_chunks, jnp.zeros((8, 256), F32))
    A.gains[...] = jnp.zeros_like(A.gains)
    A.gains[2:3, 0:256] = jnp.sum(gain_total, axis=0, keepdims=True)

    streams = [stream_copies(net.opened, c) for c in range(chunks - 1)]
    last_pair, last_cross, _ = stream_copies(net.opened, chunks - 1)
    on_last = net.remote(new_part(cross, chunks - 1), new_part(cross, chunks - 1), mp=pair)

    A.dself_low[...] = A.dself[...].astype(BF16)
    for q in range(4):
        more = A.dself[:, 4 * big + 128 * (q // 2) : 4 * big + 128 * (q // 2) + 128]
        if q % 2:
            more = pltpu.roll(more, 64, 1)
        A.ds_send[q, :, 0:128] = A.dself_low[:, 128 * q : 128 * q + 128]
        A.ds_send[q, :, 128:256] = more.astype(BF16)
    move_ds = [
        net.remote(A.ds_send.at[peer(d)], A.ds_all.at[quarter(mp)], mp=peer(d)) for d in (1, 2, 3)
    ]
    for c in move_ds:
        c.start()
    late.extend(move_ds)
    A.ds_all[quarter(mp)] = A.ds_send[mp]
    for blk in range(3):
        at = slice(RB * blk, RB * blk + RB)
        A.dq[at] = dot(A.XT[DE + RB * blk : DE + RB * blk + RB], A.DP2[...]).astype(BF16)

    load_node_cot.wait()

    def emit_edge(tile, value):
        for q in range(4):
            at = DE * tile
            A.ge[q, at : at + big] = value[big * q : big * q + big].astype(BF16)
            more = 4 * big + small * q
            A.ge[q, at + big : at + DE] = value[more : more + small].astype(BF16)

    def emit_msg(row, value):
        n = value.shape[0]
        for q in range(4):
            A.gm[q, row : row + n] = value[:, 128 * q : 128 * q + 128].astype(BF16)

    def edge_weight_gradients():
        by_in = dot_at(A.XM[...], A.DP2[...])
        by_out = dot_at(A.DO[...], A.G2[...])
        emit_edge(4, jnp.transpose(by_in[0:128]))
        emit_edge(6, jnp.transpose(by_out[0:128]))
        emit_edge(
            5, jnp.transpose(jnp.concatenate([by_in[128:DE], by_out[128:DE]], axis=0))
        )
        for t in range(4):
            at = slice(128 * t, 128 * t + 128)
            emit_edge(t, jnp.transpose(dot_at(A.win3[:, at], A.dq[...])))
        pump(sum_edge)
        landed(move_ds)
        value = dot_at(A.ds_all[...], A.win3[RB : 2 * RB])
        for t in range(4):
            A.work_e[DE * t : DE * t + DE] = value[0:DE, 128 * t : 128 * t + 128].astype(BF16)

    def message_weight_gradients():
        for t in range(4):
            at = slice(128 * t, 128 * t + 128)
            emit_msg(128 * t, dot_at(A.win2[:, at], A.dq1[...]))
        emit_msg(D, dot(A.XT[0:DE], A.DP[...]))

    def own_message_gradients():
        landed(move_avg)
        landed(move_dg1)
        landed(move_dmsg)
        A.work_m[0:D] = dot_at(A.win2[RB : 2 * RB], A.dmsg_all[...]).astype(BF16)
        value = dot_at(A.avg_all[...], A.dg1_all[...])
        for u in range(4):
            row = 2 * D + DE + 128 * u
            A.work_m[row : row + 128] = value[:, 128 * u : 128 * u + 128].astype(BF16)

    for ref, used in ((A.work_e, 11 * DE), (A.work_m, 3 * D + DE)):
        if ref.shape[0] > used:
            ref[used:] = jnp.zeros((ref.shape[0] - used, 128), BF16)

    def reduce_mp(g, got, cuts, work, base):
        rows = g.shape[1]
        a1 = net.remote(g.at[pair], got.at[0], mp=pair)
        a2 = net.remote(g.at[third], got.at[1], mp=pair)
        a2.start()
        a1.start()
        yield
        a2.wait_recv()

        @pl.loop(0, rows // 32)
        def _(i):
            at = rows_at(32 * i, 32)
            got[1, at] = (g[cross, at].astype(F32) + got[1, at].astype(F32)).astype(BF16)

        step = rows // cuts
        pieces = []
        for i in range(cuts):
            at = pl.ds(step * i, step)
            b = net.remote(got.at[1, at], got.at[2, at], mp=cross)
            b.start()
            pieces.append(b)
            yield
        for c in (a1, *pieces):
            c.wait_recv()

        @pl.loop(0, rows // 32)
        def _(i):
            at = rows_at(32 * i, 32)
            total = g[mp, at].astype(F32) + got[0, at].astype(F32) + got[2, at].astype(F32)
            work[rows_at(base + 32 * i, 32)] = total.astype(BF16)

        for c in (a1, a2, *pieces):
            c.wait_send()

    def reduce_res(work, got, out, result, plan):
        size = work.shape[0]
        low = 0
        used = 0
        me = res // stride
        grain = S.grain
        for n, s in enumerate(plan):
            into = out if n == len(plan) - 1 else work
            if s >= 0:
                bit = (res // (1 << s)) % 2
                size = size // 2
                keep = low + bit * size
                give = low + (1 - bit) * size
                copies = [
                    net.remote(
                        work.at[rows_at(give, size, grain)],
                        got.at[pl.ds(used, size)],
                        res=across(s),
                    )
                ]
            else:
                size = size // 4
                keep = low + me * size
                copies = []
                for d in (2, 1, 3):
                    there = (me + d) % 4
                    copies.append(
                        net.remote(
                            work.at[rows_at(low + there * size, size, grain)],
                            got.at[pl.ds(used + (d - 1) * size, size)],
                            res=res + (there - me) * stride,
                        )
                    )
            for c in copies:
                c.start()
            yield
            for c in copies:
                c.wait()

            @pl.loop(0, size // grain)
            def _(i, keep=keep, used=used, into=into, terms=len(copies), size=size):
                at = rows_at(keep + grain * i, grain, grain)
                total = work[at].astype(F32)
                for d in range(terms):
                    total = total + got[rows_at(used + d * size + grain * i, grain, grain)].astype(F32)
                into[at] = total.astype(BF16)

            used += size * len(copies)
            low = keep
        for s in reversed(plan):
            here = out.at[rows_at(low, size, grain)]
            if s >= 0:
                copies = [net.remote(here, here, res=across(s))]
                low = low - (res // (1 << s)) % 2 * size
                grow = 2
            else:
                copies = [
                    net.remote(here, here, res=res + ((me + d) % 4 - me) * stride)
                    for d in (2, 1, 3)
                ]
                low = low - me * size
                grow = 4
            for c in copies:
                c.start()
            yield
            for c in copies:
                c.wait()
            size = grow * size
        store.append(net.copy(out, result))

    def reduce_gains():
        copies = [net.remote(A.gains, A.gains_r.at[d - 1], mp=peer(d)) for d in (1, 2, 3)]
        for c in copies:
            c.start()
        yield
        for c in copies:
            c.wait()
        A.gains_t[0] = A.gains[...] + A.gains_r[0] + A.gains_r[1] + A.gains_r[2]
        for s in range(S.bits):
            c = net.remote(A.gains_t.at[s], A.gains_r.at[3 + s], res=across(s))
            c.start()
            yield
            c.wait()
            A.gains_t[s + 1] = A.gains_t[s] + A.gains_r[3 + s]
        store.append(net.copy(A.gains_t.at[S.bits], A.out_gains))

    def chain(*parts):
        for part in parts:
            yield from part

    def pump(*sums):
        for g in sums:
            next(g, None)

    sum_edge = chain(
        reduce_mp(A.ge, A.ge_r, 2, A.work_e, 4 * DE),
        reduce_res(A.work_e, A.sum_er, A.sum_e, A.pack_e, plans(S.bits)[0]),
    )
    sum_in = reduce_res(A.grad_i, A.sum_ir, A.sum_i, A.pack_i, plans(S.bits)[1])
    sum_out = reduce_res(A.grad_o, A.sum_or, A.sum_o, A.pack_o, plans(S.bits)[2])
    sum_msg = chain(
        reduce_mp(A.gm, A.gm_r, 1, A.work_m, D),
        reduce_res(A.work_m, A.sum_mr, A.sum_m, A.pack_m, plans(S.bits)[3]),
    )
    sum_gains = reduce_gains()

    def between_a():
        last_cross.wait_recv()
        on_last.start()
        pump(sum_edge)

    d_settled = A.nc_v[...] + dot(A.dself_low[...], A.We[:, 0:D])
    d_settled = d_settled + return_rows(
        lambda blk: dot(A.dq[RB * blk : RB * blk + RB], A.We[:, D : 2 * D]),
        A.back_send_a,
        A.back_recv_a,
        A.back_side_send_a,
        A.back_side_a,
        edge_weight_gradients,
        between_a,
    )

    normed_b = A.normed_b[...]
    d_sum_b = norm_back(d_settled, normed_b, A.inverse_b[:, 0:1], gain_b, D)
    A.gains[1:2] = jnp.sum(d_settled * normed_b, axis=0, keepdims=True)
    A.dF[quarter(mp)] = d_sum_b.astype(BF16)
    moved = gather_rows(A.dF)
    landed(moved)
    late.extend(moved)
    A.hid[...] = dot_bt(A.dF[...], A.fo_v[...])

    @unrolled(RB // 16)
    def _(i):
        rows = rows_at(16 * i, 16)
        A.dT[rows] = (A.hid[rows] * A.hslope[rows]).astype(BF16)

    A.part[...] = dot_bt(A.dT[...], A.fi_v[...])
    A.pb3[...] = A.part[...].astype(BF16)
    moved = scatter_sum_start(A.pb3, A.pr3)
    pump(sum_edge)
    A.grad_i[...] = dot_at(A.ug2[...], A.dT[...]).astype(BF16)
    pump(sum_in)
    A.grad_o[...] = dot_at(A.smooth[...], A.dF[...]).astype(BF16)
    pump(sum_out)
    d_middle = d_sum_b + A.part[quarter(mp)]
    landed(moved)
    late.extend(moved)
    for d in range(3):
        d_middle = d_middle + A.pr3[d].astype(F32)
    normed_a = A.normed_a[...]
    d_sum_a = norm_back(d_middle, normed_a, A.inverse_a[:, 0:1], gain_a, D)
    A.gains[0:1] = jnp.sum(d_middle * normed_a, axis=0, keepdims=True)
    pump(sum_gains)
    A.dsa[...] = d_sum_a
    A.dg1[...] = d_sum_a.astype(BF16)
    A.dg1_all[quarter(mp)] = A.dg1[...]
    move_dg1 = gather_rows(A.dg1_all)
    late.extend(move_dg1)
    A.davg[...] = dot_bt(A.dg1[...], A.Wo[...])

    for sub in range(RQ // 16):
        mine = A.davg[16 * sub : 16 * sub + 16]

        def back_step(k, total, sub=sub, mine=mine):
            rows = rows_at(RQ * k + 16 * sub, 16)
            d = (mine * A.slope[rows].astype(F32)).astype(BF16)
            A.DP[rows] = d
            return total + d.astype(F32)

        total = lax.fori_loop(0, K, back_step, jnp.zeros((16, HM), F32))
        A.dmsg_low[16 * sub : 16 * sub + 16] = total.astype(BF16)

    move_dmsg = spread_columns(A.dmsg_low, A.dmsg_all)
    pump(sum_edge)
    for blk in range(3):
        at = slice(RB * blk, RB * blk + RB)
        A.dq1[at] = dot(A.XT[DE + RB * blk : DE + RB * blk + RB], A.DP[...]).astype(BF16)

    pump(sum_in, sum_out)
    message_weight_gradients()
    pump(sum_msg, sum_gains)
    own_message_gradients()
    pump(sum_msg)

    def edge_gradient(start, stop):
        @pl.loop(start, stop)
        def _(c):
            rows = rows_at(EC * c, EC)
            A.EG[rows] = A.EG[rows] + dot_bt(A.DP[rows], A.T[0:256])
            for j in range(3):
                lanes = pl.multiple_of(1152 * c + 384 * j, 128)
                ends = [
                    jnp.where(is_edge, A.EG[rows_at(EC * c + RQ * (2 * j + p), RQ)], 0.0)
                    for p in range(2)
                ]
                pair_store(A.ec_v, lanes, ends[0], ends[1])

    def close_edges():
        store.append(net.copy(A.ec_v, A.out_edge_grad))
        for a, b, c in streams:
            a.wait()
            b.wait_send()
            c.wait()
        last_pair.wait()
        last_cross.wait_send()
        on_last.wait()
        store.append(net.copy(A.new_edges, A.out_edges))

    def fill_b():
        edge_gradient(0, 3)
        pump(sum_in, sum_out, sum_gains)
        edge_gradient(3, chunks)
        pump(sum_msg, sum_edge)

    back = return_rows(
        lambda blk: dot_bt(A.dq1[RB * blk : RB * blk + RB], A.Wm[D : 2 * D]),
        A.back_send_b,
        A.back_recv_b,
        A.back_side_send_b,
        A.back_side_b,
        fill_b,
        lambda: pump(sum_in, sum_out, sum_gains),
    )
    A.node_grad_v[...] = 0.5 * (A.dsa[...] + dot_bt(A.dmsg_low[...], A.Wm[0:D]) + back)
    store.append(net.copy(A.node_grad_v, A.out_node_grad))

    pump(sum_edge, sum_msg)
    close_edges()
    work = [sum_msg, sum_edge, sum_in, sum_out, sum_gains]
    while work:
        for g in list(work):
            try:
                next(g)
            except StopIteration:
                work.remove(g)
    for c in store:
        c.wait()
    for s in (spread_msg_in, spread_msg_out, *spread_edge, halo, window2, window3):
        s.sent()
    for c in late:
        c.wait_send()
    assert net.remote_count <= S.remote and net.local_count <= S.local


def build(S):
    E = S.RQ * S.K
    W = 3 * S.RB
    EC = 6 * S.RQ
    grain = S.grain * S.n_res
    rows_e = up(11 * S.DE, grain)
    rows_m = up(3 * S.D + S.DE, grain)
    in_names = ["nodes", "edges", "neighbours", "edge_mask", "msg_in", "msg_out", "gain_a"]
    in_names += ["ffn_in", "ffn_out", "gain_b", "edge_in", "edge_out", "gain_c"]
    in_names += ["node_cot", "edge_cot"]
    outs = dict(
        out_nodes=((S.RB, S.D), BF16),
        out_edges=((S.RB, S.K * S.DE), BF16),
        out_node_grad=((S.RQ, S.D), F32),
        out_edge_grad=((S.RQ, S.K * S.DE), F32),
        pack_e=((rows_e, 128), BF16),
        pack_i=((S.D, S.FL), BF16),
        pack_o=((S.FL, S.D), BF16),
        pack_m=((rows_m, 128), BF16),
        out_gains=((8, S.D), F32),
    )
    scratch = dict(
        nodes_v=((S.RB, S.D), F32),
        nbr_v=((S.K, S.RB), jnp.int32),
        mask_v=((S.K, S.RB), jnp.int32),
        columns=((S.RB, 128), F32),
        new_edges=((S.RB, S.K * S.DE), BF16),
        node_grad_v=((S.RQ, S.D), F32),
        e_v=((S.RQ, S.K * S.DE), F32),
        ec_v=((S.RQ, S.K * S.DE), F32),
        nc_v=((S.RQ, S.D), F32),
        Wm=((2 * S.D + S.DE, S.HM), BF16),
        Wo=((S.HM, S.D), BF16),
        fi_v=((S.D, S.FL), BF16),
        fo_v=((S.FL, S.D), BF16),
        We=((S.HE, 2 * S.D + S.DE), BF16),
        Eo=((S.HE, S.DE), BF16),
        Eop=((S.HE, 256), BF16),
        win1=((W, S.D), BF16),
        win2=((W, S.D), BF16),
        win3=((W, S.D), BF16),
        XE=((E, 256), BF16),
        XM=((E, 256), BF16),
        XO=((E, 512), BF16),
        XT=((768, E), BF16),
        WB=((E, 128), F32),
        T=((768, S.HM), BF16),
        Te=((768, S.HE), BF16),
        selfs=((S.RQ, S.HM), F32),
        selfe=((S.RQ, S.HE), F32),
        total=((S.RQ, S.HM), F32),
        slope=((E, S.HM), BF16),
        avg=((S.RQ, S.HM), BF16),
        ug1=((S.RB, S.D), BF16),
        ug2=((S.RB, S.D), BF16),
        hid=((S.RB, S.FL), F32),
        smooth=((S.RB, S.FL), BF16),
        hslope=((S.RB, S.FL), F32),
        part=((S.RB, S.D), F32),
        pb1=((S.RB, S.D), BF16),
        pb2=((S.RB, S.D), BF16),
        pb3=((S.RB, S.D), BF16),
        pr1=((3, S.RQ, S.D), BF16),
        pr2=((3, S.RQ, S.D), BF16),
        pr3=((3, S.RQ, S.D), BF16),
        normed_a=((S.RQ, S.D), F32),
        normed_b=((S.RQ, S.D), F32),
        inverse_a=((S.RQ, 128), F32),
        inverse_b=((S.RQ, 128), F32),
        mixed=((S.RQ, S.D), F32),
        pre=((EC, S.HM), F32),
        base=((2, EC, S.HE), F32),
        pre2=((2, EC, S.HE), F32),
        G=((2, EC, S.HE), BF16),
        upd=((2, EC, 256), F32),
        emix=((2, EC, 256), F32),
        G2=((E, S.HE), BF16),
        DO=((E, 256), BF16),
        DP2=((E, S.HE), BF16),
        EG=((E, 256), F32),
        dself=((S.RQ, S.HE), F32),
        dself_low=((S.RQ, S.HE), BF16),
        dq=((W, S.HE), BF16),
        gains=((8, S.D), F32),
        gains_r=((3 + S.bits, 8, S.D), F32),
        gains_t=((1 + S.bits, 8, S.D), F32),
        back_send_a=((4, 3, S.RQ, S.D), BF16),
        back_recv_a=((3, 3, S.RQ, S.D), BF16),
        back_side_send_a=((2, S.RQ, S.D), BF16),
        back_side_a=((2, S.RQ, S.D), BF16),
        back_send_b=((4, 3, S.RQ, S.D), BF16),
        back_recv_b=((3, 3, S.RQ, S.D), BF16),
        back_side_send_b=((2, S.RQ, S.D), BF16),
        back_side_b=((2, S.RQ, S.D), BF16),
        dF=((S.RB, S.D), BF16),
        dT=((S.RB, S.FL), BF16),
        dsa=((S.RQ, S.D), F32),
        dg1=((S.RQ, S.D), BF16),
        davg=((S.RQ, S.HM), F32),
        DP=((E, S.HM), BF16),
        dmsg_low=((S.RQ, S.HM), BF16),
        dq1=((W, S.HM), BF16),
        ge=((4, 7 * S.DE, 128), BF16),
        ge_r=((3, 7 * S.DE, 128), BF16),
        work_e=((rows_e, 128), BF16),
        ds_send=((4, S.RQ, 256), BF16),
        ds_all=((S.RB, 256), BF16),
        avg_all=((S.RB, 128), BF16),
        dg1_all=((S.RB, S.D), BF16),
        dmsg_all=((S.RB, 128), BF16),
        sum_er=((rows_e, 128), BF16),
        sum_e=((rows_e, 128), BF16),
        grad_i=((S.D, S.FL), BF16),
        sum_ir=((S.D, S.FL), BF16),
        sum_i=((S.D, S.FL), BF16),
        grad_o=((S.FL, S.D), BF16),
        sum_or=((S.FL, S.D), BF16),
        sum_o=((S.FL, S.D), BF16),
        gm=((4, S.D + S.DE, 128), BF16),
        gm_r=((3, S.D + S.DE, 128), BF16),
        work_m=((rows_m, 128), BF16),
        sum_mr=((rows_m, 128), BF16),
        sum_m=((rows_m, 128), BF16),
    )
    names = list(scratch) + ["send", "recv", "local"]
    shapes = [pltpu.VMEM(*v) for v in scratch.values()] + [
        pltpu.SemaphoreType.DMA((S.remote,)),
        pltpu.SemaphoreType.DMA((S.remote,)),
        pltpu.SemaphoreType.DMA((S.local,)),
    ]
    body = functools.partial(kernel_body, S, in_names, list(outs), names)
    body.__name__ = "layer"
    gains = ("gain_a", "gain_b", "gain_c")
    return pl.pallas_call(
        body,
        name="layer",
        out_shape=[jax.ShapeDtypeStruct(*v) for v in outs.values()],
        in_specs=[VMEM if n in gains else ANY for n in in_names],
        out_specs=[ANY] * len(outs),
        scratch_shapes=shapes,
        compiler_params=pltpu.CompilerParams(
            collective_id=0, has_side_effects=True, vmem_limit_bytes=62 * 1024 * 1024
        ),
    )


def unpack_body(S, names, *refs):
    A = SimpleNamespace(**dict(zip(names, refs, strict=True)))
    D, DE, RB = S.D, S.DE, S.RB
    count = [0]

    def copy(src, dst):
        c = pltpu.make_async_copy(src, dst, A.sems.at[count[0]])
        count[0] += 1
        c.start()
        return c

    part = RB // 4
    edge_loads = [
        copy(A.in_edges.at[pl.ds(part * i, part)], A.edges_l.at[pl.ds(part * i, part)])
        for i in range(4)
    ]
    pairs = (
        (A.in_e, A.e_l),
        (A.in_i, A.i_l),
        (A.in_o, A.o_l),
        (A.in_m, A.m_l),
        (A.in_nodes, A.nodes_l),
        (A.in_gains, A.gains_l),
    )
    loads = [copy(*p) for p in pairs]
    grads = [copy(A.in_edge_grad, A.eg_l), copy(A.in_node_grad, A.ng_l)]
    stores = []
    for i in range(4):
        edge_loads[i].wait()

        @pl.loop(0, part // 16)
        def _(k, i=i):
            at = pl.ds(pl.multiple_of(part * i + 16 * k, 16), 16)
            A.edges_f[at] = A.edges_l[at].astype(F32)

        at = pl.ds(part * i, part)
        stores.append(copy(A.edges_f.at[at], A.o1.at[at]))
    for c in (*grads, *loads):
        c.wait()
    stores += [copy(A.eg_l, A.o3), copy(A.ng_l, A.o2)]

    def widen(src, dst, out, rows):
        @pl.loop(0, rows // 16)
        def _(k):
            at = pl.ds(pl.multiple_of(16 * k, 16), 16)
            dst[at] = src[at].astype(F32)

        stores.append(copy(dst, out))

    widen(A.i_l, A.i_f, A.o7, D)
    widen(A.o_l, A.o_f, A.o8, S.FL)
    widen(A.nodes_l, A.nodes_f, A.o0, RB)
    widen(A.m_l, A.m_f, A.o4, 2 * D + DE)
    for u in range(4):
        row = 2 * D + DE + 128 * u
        A.mo_f[:, 128 * u : 128 * u + 128] = A.m_l[row : row + 128].astype(F32)
    stores.append(copy(A.mo_f, A.o5))
    mixed = A.e_l[9 * DE : 10 * DE].astype(F32)
    for t in range(9):
        A.ei_f[:, 128 * t : 128 * t + 128] = A.e_l[DE * t : DE * t + DE].astype(F32)
    A.ei_f[:, 1152 : 1152 + 64] = mixed[:, 0:64]
    stores.append(copy(A.ei_f, A.o10))
    A.eo_f[:, 0:128] = A.e_l[10 * DE : 11 * DE].astype(F32)
    A.eo_f[:, 128:DE] = pltpu.roll(mixed, 64, 1)[:, 0:64]
    stores.append(copy(A.eo_f, A.o11))
    A.ga_f[...] = A.gains_l[0:1]
    A.gb_f[...] = A.gains_l[1:2]
    A.gc_f[...] = A.gains_l[2:3, 0:DE]
    for src, out in ((A.ga_f, A.o6), (A.gb_f, A.o9), (A.gc_f, A.o12)):
        stores.append(copy(src, out))
    for c in stores:
        c.wait()


def unpack(S, values):
    D, DE, RB, RQ, K, FL = S.D, S.DE, S.RB, S.RQ, S.K, S.FL
    ins = ["in_nodes", "in_edges", "in_node_grad", "in_edge_grad"]
    ins += ["in_e", "in_i", "in_o", "in_m", "in_gains"]
    shapes = [
        (RB, D),
        (RB, K * DE),
        (RQ, D),
        (RQ, K * DE),
        (2 * D + DE, S.HM // 4),
        (S.HM // 4, D),
        (1, D),
        (D, FL),
        (FL, D),
        (1, D),
        (S.HE // 4, 2 * D + DE),
        (S.HE // 4, DE),
        (1, DE),
    ]
    outs = ["o%d" % i for i in range(13)]
    scratch = dict(
        edges_l=((RB, K * DE), BF16),
        edges_f=((RB, K * DE), F32),
        e_l=(values[4].shape, BF16),
        i_l=((D, FL), BF16),
        o_l=((FL, D), BF16),
        m_l=(values[7].shape, BF16),
        nodes_l=((RB, D), BF16),
        gains_l=((8, D), F32),
        eg_l=((RQ, K * DE), F32),
        ng_l=((RQ, D), F32),
        i_f=((D, FL), F32),
        o_f=((FL, D), F32),
        nodes_f=((RB, D), F32),
        m_f=(shapes[4], F32),
        mo_f=(shapes[5], F32),
        ei_f=(shapes[10], F32),
        eo_f=(shapes[11], F32),
        ga_f=(shapes[6], F32),
        gb_f=(shapes[9], F32),
        gc_f=(shapes[12], F32),
    )
    names = ins + outs + list(scratch) + ["sems"]
    body = functools.partial(unpack_body, S, names)
    return list(
        pl.pallas_call(
            body,
            name="unpack",
            out_shape=[jax.ShapeDtypeStruct(x, F32) for x in shapes],
            in_specs=[ANY] * len(ins),
            out_specs=[ANY] * len(outs),
            scratch_shapes=[pltpu.VMEM(*v) for v in scratch.values()]
            + [pltpu.SemaphoreType.DMA((32,))],
            compiler_params=pltpu.CompilerParams(vmem_limit_bytes=62 * 1024 * 1024),
        )(*values)
    )


STOP = 0


def plans(bits):
    low = list(range(bits - 2))
    high = [bits - 2, bits - 1]
    return [low + [-1], low + high, high + low, low + [-1]]


def on_device(n_res, *args):
    nodes, edges, neighbours, _, _, _, _, ffn_in = args[:8]
    height = nodes.shape[0]
    degree = neighbours.shape[1]
    S = SimpleNamespace(
        n_res=n_res,
        bits=int(math.log2(n_res)),
        RB=height,
        RQ=height // 4,
        K=degree,
        D=nodes.shape[1],
        DE=edges.shape[1] // degree,
        HM=args[4].shape[1] * 4,
        HE=args[10].shape[1] * 4,
        FL=ffn_in.shape[1],
        grain=16 if n_res <= 16 else 8,
        remote=200,
        local=32,
        stop=STOP,
    )
    fixed = [a.reshape(1, -1) if a.ndim == 1 else a for a in args]
    for i in (2, 3, 10):
        fixed[i] = fixed[i].T
    out = unpack(S, build(S)(*fixed))
    for i in (6, 9, 12):
        out[i] = out[i].reshape(-1)
    out[10] = out[10].T
    return tuple(out)


def solution(mesh):
    in_specs = (
        P("res", None),
        P("res", None),
        P("res", None),
        P("res", None),
        P(None, "mp"),
        P("mp", None),
        P(),
        P(None, "mp"),
        P("mp", None),
        P(),
        P(None, "mp"),
        P("mp", None),
        P(),
        P("res", None),
        P("res", None),
    )
    out_specs = (
        P("res", None),
        P("res", None),
        P(("res", "mp"), None),
        P(("res", "mp"), None),
        P(None, "mp"),
        P("mp", None),
        P(),
        P(None, "mp"),
        P("mp", None),
        P(),
        P(None, "mp"),
        P("mp", None),
        P(),
    )
    return jax.shard_map(
        functools.partial(on_device, mesh.shape["res"]),
        mesh=mesh,
        in_specs=in_specs,
        out_specs=out_specs,
        check_vma=False,
    )
```

```python
import functools
import math
from types import SimpleNamespace

import jax
import jax.numpy as jnp
from jax import lax
from jax.experimental import pallas as pl
from jax.experimental.pallas import tpu as pltpu
from jax.sharding import PartitionSpec as P

EPSILON = 1e-05
F32 = jnp.float32
BF16 = jnp.bfloat16
MESH = pl.DeviceIdType.MESH
ROOT_TWO_PI = 0.3989422804014327
ROOT_HALF = 0.7071067811865476
ANY = pl.BlockSpec(memory_space=pl.ANY)
VMEM = pl.BlockSpec(memory_space=pltpu.VMEM)


def dot(left, right):
    return jnp.dot(left, right, preferred_element_type=F32)


def dot_bt(left, right):
    return lax.dot_general(left, right, (((1,), (1,)), ((), ())), preferred_element_type=F32)


def dot_at(left, right):
    return lax.dot_general(left, right, (((0,), (0,)), ((), ())), preferred_element_type=F32)


def bell(v):
    return 0.5 + 0.5 * lax.erf(v * ROOT_HALF)


def bell_slope(phi, v):
    return phi + v * (jnp.exp(-0.5 * (v * v)) * ROOT_TWO_PI)


def norm_parts(values, width):
    scale = 1.0 / width
    centred = values - jnp.sum(values, axis=-1, keepdims=True) * scale
    inverse = lax.rsqrt(jnp.sum(centred * centred, axis=-1, keepdims=True) * scale + EPSILON)
    return centred * inverse, inverse


def norm_back(upstream, normed, inverse, gain, width):
    scale = 1.0 / width
    scaled = upstream * gain
    mean = jnp.sum(scaled, axis=-1, keepdims=True) * scale
    along = jnp.sum(scaled * normed, axis=-1, keepdims=True) * scale
    return inverse * (scaled - mean - normed * along)


def up(rows, step):
    return -(-rows // step) * step


def add_step(rows, grain, lanes):
    parts = rows // grain
    return grain * max(
        n for n in range(1, parts + 1) if parts % n == 0 and (n == 1 or n * grain * lanes <= 32768)
    )


def unrolled(count):
    def run(step):
        for i in range(count):
            step(i)

    return run


class Net:
    def __init__(self, send, recv, local):
        self.send, self.recv, self.local = send, recv, local
        self.remote_count = 0
        self.local_count = 0

    def remote(self, src, dst, side="", **where):
        i = self.remote_count
        self.remote_count += 1
        return pltpu.make_async_remote_copy(
            src_ref=src,
            dst_ref=dst,
            send_sem=self.send.at[i],
            recv_sem=self.recv.at[i],
            device_id=where,
            device_id_type=MESH,
        )

    def reserve(self, count):
        i = self.remote_count
        self.remote_count += count
        return i

    def at(self, i, src, dst, **where):
        return pltpu.make_async_remote_copy(
            src_ref=src,
            dst_ref=dst,
            send_sem=self.send.at[i],
            recv_sem=self.recv.at[i],
            device_id=where,
            device_id_type=MESH,
        )

    def opened(self, i, src, dst, **where):
        return self.at(i, src, dst, **where)

    def copy(self, src, dst):
        i = self.local_count
        self.local_count += 1
        c = pltpu.make_async_copy(src, dst, self.local.at[i])
        c.start()
        return c


def kernel_body(S, in_names, out_names, scratch_names, *refs):
    names = in_names + out_names + scratch_names
    A = SimpleNamespace(**dict(zip(names, refs, strict=True)))
    net = Net(A.send, A.recv, A.local)
    RB, RQ, K, D, DE, HM, HE, FL = S.RB, S.RQ, S.K, S.D, S.DE, S.HM, S.HE, S.FL
    E = RQ * K
    W = 3 * RB
    EC = 6 * RQ
    res = lax.axis_index("res")
    mp = lax.axis_index("mp")
    has_l = res > 0
    has_r = res < S.n_res - 1
    pair = mp + 1 - 2 * (mp % 2)
    cross = (mp + 2) % 4
    third = (pair + 2) % 4

    def peer(d):
        return (mp + d) % 4

    def rows_at(start, size, step=16):
        return pl.ds(pl.multiple_of(start, step), size)

    def quarter(q, base=0):
        return rows_at(base + RQ * q, RQ)

    load_nodes = net.copy(A.nodes, A.nodes_v)
    load_nbr = net.copy(A.neighbours, A.nbr_v)
    load_mask = net.copy(A.edge_mask, A.mask_v)
    load_edges = net.copy(A.edges.at[quarter(mp)], A.e_v)
    own_msg_in = A.Wm.at[:, pl.ds(pl.multiple_of(mp * 128, 128), 128)]
    load_msg_in = net.copy(A.msg_in, own_msg_in)
    own_msg_out = A.Wo.at[rows_at(mp * 128, 128)]
    load_msg_out = net.copy(A.msg_out, own_msg_out)
    load_ffn_in = net.copy(A.ffn_in, A.fi_v)
    load_ffn_out = net.copy(A.ffn_out, A.fo_v)
    big, small = HE // 4 // 3 * 2, HE // 4 // 3

    def main_rows(ref):
        return lambda q: ref.at[rows_at(big * q, big)]

    def rest_rows(ref):
        return lambda q: ref.at[rows_at(4 * big + small * q, small)]

    first, rest = pl.ds(0, big), pl.ds(big, small)
    edge_parts = (
        (A.edge_in.at[first], main_rows(A.We)),
        (A.edge_out.at[first], main_rows(A.Eo)),
        (A.edge_in.at[rest], rest_rows(A.We)),
        (A.edge_out.at[rest], rest_rows(A.Eo)),
    )
    load_edge_weights = [net.copy(src, place(mp)) for src, place in edge_parts]
    load_node_cot = net.copy(A.node_cot.at[quarter(mp)], A.nc_v)
    load_edge_cot = net.copy(A.edge_cot.at[quarter(mp)], A.ec_v)

    barrier = pltpu.get_barrier_semaphore()

    def greet(**where):
        pl.semaphore_signal(barrier, inc=1, device_id=where, device_id_type=MESH)

    def across(s):
        return res + (1 << s) * (1 - 2 * ((res // (1 << s)) % 2))

    for d in (1, 2, 3):
        greet(mp=peer(d))
    for s in range(S.bits - 2):
        greet(res=across(s))
    stride = S.n_res // 4
    for d in (1, 2, 3):
        greet(res=res + ((res // stride + d) % 4 - res // stride) * stride)

    @pl.when(has_l)
    def _():
        greet(res=res - 1)

    @pl.when(has_r)
    def _():
        greet(res=res + 1)

    sides = (res + S.n_res - 1) // S.n_res + 1 - (res + 1) // S.n_res
    pl.semaphore_wait(barrier, 6 + S.bits - 2 + sides)

    class Spread:
        def __init__(self, src, place):
            own = place(mp)
            self.first = [net.remote(src, own, mp=pair), net.remote(src, own, mp=cross)]
            self.then = net.remote(place(cross), place(cross), mp=pair)

        def start(self):
            for c in self.first:
                c.start()

        def forward(self):
            self.first[1].wait_recv()
            self.then.start()

        def wait(self):
            self.first[0].wait_recv()
            self.then.wait_recv()

        def sent(self):
            for c in self.first:
                c.wait_send()
            self.then.wait_send()

    spread_msg_in = Spread(
        A.msg_in, lambda q: A.Wm.at[:, pl.ds(pl.multiple_of(q * 128, 128), 128)]
    )
    spread_msg_out = Spread(A.msg_out, lambda q: A.Wo.at[rows_at(q * 128, 128)])
    spread_edge = [Spread(src, place) for src, place in edge_parts]

    def clear_sides(win):
        @pl.when(jnp.logical_not(has_l))
        def _():
            win[0:RB] = jnp.zeros((RB, D), BF16)

        @pl.when(jnp.logical_not(has_r))
        def _():
            win[2 * RB : 3 * RB] = jnp.zeros((RB, D), BF16)

    half = RB // 2

    class Halo:
        def __init__(self, win):
            h = mp % 2
            own = win.at[rows_at(RB + half * h, half)]
            left = win.at[rows_at(half * h, half)]
            right = win.at[rows_at(2 * RB + half * h, half)]
            self.to_l = net.remote(own, right, side="l", res=res - 1)
            self.to_r = net.remote(own, left, side="r", res=res + 1)
            self.on_l = net.remote(left, left, mp=pair)
            self.on_r = net.remote(right, right, mp=pair)

        def start(self):
            pl.when(has_l)(self.to_l.start)
            pl.when(has_r)(self.to_r.start)

        def forward(self):
            @pl.when(has_l)
            def _():
                self.to_r.wait_recv()
                self.on_l.start()

            @pl.when(has_r)
            def _():
                self.to_l.wait_recv()
                self.on_r.start()

        def wait(self):
            pl.when(has_l)(self.on_l.wait_recv)
            pl.when(has_r)(self.on_r.wait_recv)

        def sent(self):
            @pl.when(has_l)
            def _():
                self.to_l.wait_send()
                self.on_l.wait_send()

            @pl.when(has_r)
            def _():
                self.to_r.wait_send()
                self.on_r.wait_send()

    class Window:
        def __init__(self, win):
            own = win.at[quarter(mp, RB)]
            left = win.at[quarter(mp)]
            right = win.at[quarter(mp, 2 * RB)]
            self.to_l = net.remote(own, right, side="l", res=res - 1)
            self.to_r = net.remote(own, left, side="r", res=res + 1)
            self.mine = [net.remote(own, own, mp=peer(d)) for d in (1, 2, 3)]
            self.on_l = [net.remote(left, left, mp=peer(d)) for d in (1, 2, 3)]
            self.on_r = [net.remote(right, right, mp=peer(d)) for d in (1, 2, 3)]

        def start(self):
            pl.when(has_l)(self.to_l.start)
            pl.when(has_r)(self.to_r.start)
            for c in self.mine:
                c.start()

        def forward(self):
            @pl.when(has_l)
            def _():
                self.to_r.wait_recv()
                for c in self.on_l:
                    c.start()

            @pl.when(has_r)
            def _():
                self.to_l.wait_recv()
                for c in self.on_r:
                    c.start()

        def wait_own(self):
            for c in self.mine:
                c.wait_recv()

        def wait(self):
            @pl.when(has_l)
            def _():
                for c in self.on_l:
                    c.wait_recv()

            @pl.when(has_r)
            def _():
                for c in self.on_r:
                    c.wait_recv()

        def sent(self):
            for c in self.mine:
                c.wait_send()

            @pl.when(has_l)
            def _():
                self.to_l.wait_send()
                for c in self.on_l:
                    c.wait_send()

            @pl.when(has_r)
            def _():
                self.to_r.wait_send()
                for c in self.on_r:
                    c.wait_send()

    def gather_rows(buf):
        own = buf.at[quarter(mp)]
        copies = [net.remote(own, own, mp=peer(d)) for d in (1, 2, 3)]
        for c in copies:
            c.start()
        return copies

    def scatter_sum_start(buf, into):
        copies = [
            net.remote(buf.at[quarter(peer(d))], into.at[d - 1], mp=peer(d)) for d in (1, 2, 3)
        ]
        for c in copies:
            c.start()
        return copies

    def landed(copies):
        for c in copies:
            c.wait_recv()

    late = []

    def lanes_at(q):
        return pl.ds(pl.multiple_of(128 * q, 128), 128)

    def spread_columns(src, dst):
        copies = [
            net.remote(src.at[:, lanes_at(peer(d))], dst.at[quarter(mp)], mp=peer(d))
            for d in (1, 2, 3)
        ]
        for c in copies:
            c.start()
        late.extend(copies)
        dst[quarter(mp)] = src[:, lanes_at(mp)]
        return copies

    def return_rows(product, send, recv, side_send, side_recv, fill, between):
        for blk in range(3):
            part = product(blk)
            for q in range(4):
                send[q, blk] = part[RQ * q : RQ * q + RQ].astype(BF16)
        copies = [net.remote(send.at[peer(d)], recv.at[d - 1], mp=peer(d)) for d in (1, 2, 3)]
        for c in copies:
            c.start()
        fill()
        landed(copies)
        late.extend(copies)

        def total(blk):
            out = send[mp, blk].astype(F32)
            for d in range(3):
                out = out + recv[d, blk].astype(F32)
            return out

        side_send[0] = total(0).astype(BF16)
        side_send[1] = total(2).astype(BF16)
        to_l = net.remote(side_send.at[0], side_recv.at[1], side="l", res=res - 1)
        to_r = net.remote(side_send.at[1], side_recv.at[0], side="r", res=res + 1)
        pl.when(has_l)(to_l.start)
        pl.when(has_r)(to_r.start)
        mid = total(1)
        between()
        pl.when(has_l)(to_r.wait_recv)
        pl.when(has_r)(to_l.wait_recv)
        pl.when(has_l)(to_l.wait_send)
        pl.when(has_r)(to_r.wait_send)
        return mid + side_recv[0].astype(F32) + side_recv[1].astype(F32)

    spread_msg_in.start()
    spread_msg_out.start()
    load_nodes.wait()

    @unrolled(RB // 16)
    def _(i):
        A.win1[rows_at(RB + 16 * i, 16)] = A.nodes_v[rows_at(16 * i, 16)].astype(BF16)

    halo = Halo(A.win1)
    halo.start()
    for win in (A.win1, A.win2, A.win3):
        clear_sides(win)
    for ref in (A.back_side_a, A.back_side_b):
        ref[...] = jnp.zeros_like(ref)

    load_nbr.wait()
    load_mask.wait()
    load_edges.wait()
    stack = jnp.concatenate(
        [A.nbr_v[...].astype(F32), A.mask_v[...].astype(F32), jnp.zeros((128 - 2 * K, RB), F32)],
        axis=0,
    )
    stack = jnp.concatenate([stack, jnp.zeros((128, 256 - RB), F32)], axis=1)
    A.columns[...] = jnp.transpose(stack)[0:RB]
    columns = A.columns[rows_at(RQ * mp, RQ)]
    local = columns[:, 0:K].astype(jnp.int32) - (res - 1) * RB + DE
    live = columns[:, K : 2 * K]
    mean_weight = live / jnp.maximum(jnp.sum(live, axis=1, keepdims=True), 1.0)
    lane256 = lax.broadcasted_iota(jnp.int32, (RQ, 256), 1)
    lane512 = lax.broadcasted_iota(jnp.int32, (RQ, 512), 1) + 256
    is_edge = lane256 < DE

    def pair_load(buf, base):
        even = buf[:, pl.ds(base, 256)]
        odd = pltpu.roll(buf[:, pl.ds(base + 128, 256)], 192, 1)
        return jnp.where(is_edge, even, 0.0), jnp.where(is_edge, odd, 0.0)

    def pair_store(buf, base, even, odd, sub=slice(None)):
        back = pltpu.roll(odd, 64, 1)
        buf[sub, pl.ds(base, 128)] = even[:, :128].astype(buf.dtype)
        buf[sub, pl.ds(base + 128, 128)] = (even[:, 128:] + back[:, :128]).astype(buf.dtype)
        buf[sub, pl.ds(base + 256, 128)] = back[:, 128:].astype(buf.dtype)

    for j in range(K // 2):
        both = pair_load(A.e_v, 384 * j)
        for p in range(2):
            k = 2 * j + p
            column = local[:, k : k + 1]
            hot = jnp.where(column == lane256, 1.0, 0.0)
            A.XE[RQ * k : RQ * k + RQ] = jnp.where(is_edge, both[p], hot).astype(BF16)
            A.XO[RQ * k : RQ * k + RQ] = jnp.where(column == lane512, 1.0, 0.0).astype(BF16)
            A.WB[RQ * k : RQ * k + RQ] = jnp.broadcast_to(mean_weight[:, k : k + 1], (RQ, 128))

    halo.forward()

    full = E // 128

    @pl.loop(0, full)
    def _(c):
        at = pl.ds(pl.multiple_of(128 * c, 128), 128)
        A.XT[0:256, at] = A.XE[at].T
        A.XT[256:768, at] = A.XO[at].T

    if E % 128:
        at = slice(full * 128, E)
        A.XT[0:256, at] = A.XE[at].T
        A.XT[256:768, at] = A.XO[at].T

    spread_msg_in.forward()
    halo.wait()

    gain_a = A.gain_a[...]
    gain_b = A.gain_b[...]
    load_msg_in.wait()
    load_msg_out.wait()

    def node_table(win):
        for blk in (1, 0, 2):
            part = dot(win[RB * blk : RB * blk + RB], A.Wm[D : 2 * D])
            A.T[DE + RB * blk : DE + RB * blk + RB] = part.astype(BF16)

    def message_mean(win, keep):
        A.selfs[...] = dot(win[quarter(mp, RB)], A.Wm[0:D])
        A.total[...] = jnp.zeros((RQ, HM), F32)

        @pl.loop(0, E // EC)
        def _(c):
            rows = rows_at(EC * c, EC)
            left = jnp.concatenate([A.XE[rows], A.XO[rows]], axis=1)
            A.pre[...] = dot(left, A.T[...])

            @unrolled(RQ // 16)
            def _(sub):
                own = slice(16 * sub, 16 * sub + 16)
                mine = A.selfs[own]
                total = A.total[own]
                for k in range(6):
                    at = RQ * k + 16 * sub
                    v = A.pre[at : at + 16] + mine
                    there = rows_at(EC * c + at, 16)
                    w = jnp.concatenate([A.WB[there]] * (HM // 128), axis=1)
                    phi = bell(v)
                    if keep:
                        A.slope[there] = (w * bell_slope(phi, v)).astype(BF16)
                    total = total + w * (v * phi)
                A.total[own] = total

        A.avg[...] = A.total[...].astype(BF16)

    def node_tail(states, ug, part_b, part_r, keep):
        normed_a, inverse_a = norm_parts(states + dot(A.avg[...], A.Wo[...]), D)
        middle = normed_a * gain_a
        ug[quarter(mp)] = middle.astype(BF16)
        moved = gather_rows(ug)
        landed(moved)
        late.extend(moved)
        A.hid[...] = dot(ug[...], A.fi_v[...])

        @unrolled(RB // 16)
        def _(i):
            rows = rows_at(16 * i, 16)
            v = A.hid[rows]
            phi = bell(v)
            A.smooth[rows] = (v * phi).astype(BF16)
            if keep:
                A.hslope[rows] = bell_slope(phi, v)

        A.part[...] = dot(A.smooth[...], A.fo_v[...])
        part_b[...] = A.part[...].astype(BF16)
        moved = scatter_sum_start(part_b, part_r)
        total = middle + A.part[quarter(mp)]
        landed(moved)
        late.extend(moved)
        for d in range(3):
            total = total + part_r[d].astype(F32)
        normed_b, inverse_b = norm_parts(total, D)
        if keep:
            A.normed_a[...] = normed_a
            A.inverse_a[...] = jnp.broadcast_to(inverse_a, (RQ, 128))
            A.normed_b[...] = normed_b
            A.inverse_b[...] = jnp.broadcast_to(inverse_b, (RQ, 128))
        return normed_b * gain_b

    spread_msg_in.wait()
    spread_edge[0].start()
    spread_edge[1].start()
    A.T[0:DE] = A.Wm[2 * D : 2 * D + DE]
    node_table(A.win1)
    message_mean(A.win1, False)
    spread_msg_out.forward()
    spread_msg_out.wait()
    load_ffn_in.wait()
    load_ffn_out.wait()
    own_nodes = A.nodes_v[quarter(mp)]
    predicted = node_tail(own_nodes, A.ug1, A.pb1, A.pr1, False)
    A.mixed[...] = 0.5 * (own_nodes + predicted)
    A.win2[quarter(mp, RB)] = A.mixed[...].astype(BF16)
    window2 = Window(A.win2)
    window2.start()
    window2.forward()
    window2.wait_own()
    window2.wait()
    spread_edge[2].start()
    spread_edge[3].start()
    spread_edge[0].forward()
    spread_edge[1].forward()
    node_table(A.win2)
    message_mean(A.win2, True)
    move_avg = spread_columns(A.avg, A.avg_all)
    spread_edge[2].forward()
    spread_edge[3].forward()
    settled = node_tail(A.mixed[...], A.ug2, A.pb2, A.pr2, True)
    A.win3[quarter(mp, RB)] = settled.astype(BF16)
    window3 = Window(A.win3)
    window3.start()
    window3.forward()

    for c in (*spread_edge, *load_edge_weights):
        c.wait()
    A.Eop[...] = jnp.concatenate([A.Eo[...], jnp.zeros((HE, 64), BF16)], axis=1)
    A.Te[0:DE] = A.We[:, 2 * D : 2 * D + DE].T
    window3.wait_own()
    window3.wait()
    store = [net.copy(A.win3.at[RB : 2 * RB], A.out_nodes)]

    for blk in (1, 0, 2):
        part = dot_bt(A.win3[RB * blk : RB * blk + RB], A.We[:, D : 2 * D])
        A.Te[DE + RB * blk : DE + RB * blk + RB] = part.astype(BF16)
    A.selfe[...] = dot_bt(A.win3[quarter(mp, RB)], A.We[:, 0:D])
    A.dself[...] = jnp.zeros((RQ, HE), F32)
    load_edge_cot.wait()
    gain_c = jnp.concatenate([A.gain_c[...], jnp.zeros((1, 256 - DE), F32)], axis=1)

    def norm_parts_e(values):
        scale = 1.0 / DE
        mean = jnp.sum(values, axis=-1, keepdims=True) * scale
        centred = jnp.where(is_edge, values - mean, 0.0)
        inverse = lax.rsqrt(jnp.sum(centred * centred, axis=-1, keepdims=True) * scale + EPSILON)
        return centred * inverse, inverse

    chunks = E // EC
    stream = net.reserve(3 * chunks)

    def new_part(q, c):
        return A.new_edges.at[quarter(q), pl.ds(pl.multiple_of(6 * DE * c, 128), 6 * DE)]

    def stream_copies(make, c):
        return (
            make(stream + c, new_part(mp, c), new_part(mp, c), mp=pair),
            make(stream + chunks + c, new_part(mp, c), new_part(mp, c), mp=cross),
            make(stream + 2 * chunks + c, new_part(cross, c), new_part(cross, c), mp=pair),
        )

    def edge_chunk(c, part, gain_out):
        rows = rows_at(EC * c, EC)
        base, pre2, upd, emix, G = (x.at[part] for x in (A.base, A.pre2, A.upd, A.emix, A.G))
        base[...] = dot(A.XO[rows], A.Te[256:768])
        pre2[...] = dot(A.XE[rows], A.Te[0:256])
        yield

        @unrolled(EC // 16)
        def _(b):
            at = slice(16 * b, 16 * b + 16)
            own = 16 * (b % (RQ // 16))
            total = base[at] + A.selfe[own : own + 16]
            base[at] = total
            v = total + pre2[at]
            G[at] = (v * bell(v)).astype(BF16)

        yield
        upd[...] = dot(G[...], A.Eop[...])
        yield
        for j in range(3):
            both = pair_load(A.e_v, pl.multiple_of(1152 * c + 384 * j, 128))
            for p in range(2):
                k = 2 * j + p
                mine = slice(RQ * k, RQ * k + RQ)
                at = rows_at(EC * c + RQ * k, RQ)
                normed, _ = norm_parts_e(both[p] + upd[mine])
                mixed = 0.5 * (both[p] + normed * gain_c)
                emix[mine] = mixed
                A.XM[at] = jnp.where(is_edge, mixed, A.XE[at].astype(F32)).astype(BF16)

        yield
        pre2[...] = dot(A.XM[rows], A.Te[0:256])
        yield

        @unrolled(EC // 16)
        def _(b):
            at = slice(16 * b, 16 * b + 16)
            v = base[at] + pre2[at]
            phi = bell(v)
            A.G2[rows_at(EC * c + 16 * b, 16)] = (v * phi).astype(BF16)
            base[at] = bell_slope(phi, v)

        yield
        upd[...] = dot(A.G2[rows], A.Eop[...])
        yield
        gain_total = jnp.zeros((8, 256), F32)
        for j in range(3):
            lanes = pl.multiple_of(1152 * c + 384 * j, 128)
            cots = pair_load(A.ec_v, lanes)
            news = []
            for p in range(2):
                k = 2 * j + p
                mine = slice(RQ * k, RQ * k + RQ)
                normed, inverse = norm_parts_e(emix[mine] + upd[mine])
                news.append(normed * gain_c)
                gain_total = gain_total + jnp.sum(
                    (cots[p] * normed).reshape(RQ // 8, 8, 256), axis=0
                )
                d_sum = jnp.where(is_edge, norm_back(cots[p], normed, inverse, gain_c, DE), 0.0)
                emix[mine] = d_sum
                A.DO[rows_at(EC * c + RQ * k, RQ)] = d_sum.astype(BF16)
            pair_store(A.new_edges, lanes, news[0], news[1], quarter(mp))
        gain_out.append(gain_total)
        yield
        pre2[...] = dot_bt(A.DO[rows], A.Eop[...])
        yield

        @unrolled(RQ // 16)
        def _(sub):
            own = slice(16 * sub, 16 * sub + 16)
            total = A.dself[own]
            for k in range(6):
                at = slice(RQ * k + 16 * sub, RQ * k + 16 * sub + 16)
                d = (pre2[at] * base[at]).astype(BF16)
                A.DP2[rows_at(EC * c + RQ * k + 16 * sub, 16)] = d
                total = total + d.astype(F32)
            A.dself[own] = total

        yield
        A.EG[rows] = 0.5 * (emix[...] + dot_bt(A.DP2[rows], A.Te[0:256]))

    def send_chunk(c):
        to_pair, to_cross, _ = stream_copies(net.at, c)
        to_cross.start()
        to_pair.start()

        @pl.when(c > 0)
        def _():
            _, arrived, on = stream_copies(net.at, c - 1)
            arrived.wait_recv()
            on.start()

    def edge_chunks(i, gain_total):
        gains = []
        parts = [edge_chunk(2 * i + h, h, gains) for h in range(2)]
        next(parts[0])
        running = list(parts)
        while running:
            for g in list(running):
                try:
                    next(g)
                except StopIteration:
                    running.remove(g)
        for h in range(2):
            send_chunk(2 * i + h)
        return gain_total + gains[0] + gains[1]

    gain_total = lax.fori_loop(0, chunks // 2, edge_chunks, jnp.zeros((8, 256), F32))
    A.gains[...] = jnp.zeros_like(A.gains)
    A.gains[2:3, 0:256] = jnp.sum(gain_total, axis=0, keepdims=True)

    streams = [stream_copies(net.opened, c) for c in range(chunks - 1)]
    last_pair, last_cross, _ = stream_copies(net.opened, chunks - 1)
    on_last = net.remote(new_part(cross, chunks - 1), new_part(cross, chunks - 1), mp=pair)

    A.dself_low[...] = A.dself[...].astype(BF16)
    for q in range(4):
        more = A.dself[:, 4 * big + 128 * (q // 2) : 4 * big + 128 * (q // 2) + 128]
        if q % 2:
            more = pltpu.roll(more, 64, 1)
        A.ds_send[q, :, 0:128] = A.dself_low[:, 128 * q : 128 * q + 128]
        A.ds_send[q, :, 128:256] = more.astype(BF16)
    move_ds = [
        net.remote(A.ds_send.at[peer(d)], A.ds_all.at[quarter(mp)], mp=peer(d)) for d in (1, 2, 3)
    ]
    for c in move_ds:
        c.start()
    late.extend(move_ds)
    A.ds_all[quarter(mp)] = A.ds_send[mp]
    for blk in range(3):
        at = slice(RB * blk, RB * blk + RB)
        A.dq[at] = dot(A.XT[DE + RB * blk : DE + RB * blk + RB], A.DP2[...]).astype(BF16)

    load_node_cot.wait()

    def emit_edge(tile, value):
        for q in range(4):
            at = DE * tile
            A.ge[q, at : at + big] = value[big * q : big * q + big].astype(BF16)
            more = 4 * big + small * q
            A.ge[q, at + big : at + DE] = value[more : more + small].astype(BF16)

    def emit_msg(row, value):
        n = value.shape[0]
        for q in range(4):
            A.gm[q, row : row + n] = value[:, 128 * q : 128 * q + 128].astype(BF16)

    def edge_weight_gradients():
        by_in = dot_at(A.XM[...], A.DP2[...])
        by_out = dot_at(A.DO[...], A.G2[...])
        emit_edge(4, jnp.transpose(by_in[0:128]))
        emit_edge(6, jnp.transpose(by_out[0:128]))
        emit_edge(
            5, jnp.transpose(jnp.concatenate([by_in[128:DE], by_out[128:DE]], axis=0))
        )
        for t in range(4):
            at = slice(128 * t, 128 * t + 128)
            emit_edge(t, jnp.transpose(dot_at(A.win3[:, at], A.dq[...])))
        pump(sum_edge)
        landed(move_ds)
        value = dot_at(A.ds_all[...], A.win3[RB : 2 * RB])
        for t in range(4):
            A.work_e[DE * t : DE * t + DE] = value[0:DE, 128 * t : 128 * t + 128].astype(BF16)

    def message_weight_gradients():
        for t in range(4):
            at = slice(128 * t, 128 * t + 128)
            emit_msg(128 * t, dot_at(A.win2[:, at], A.dq1[...]))
        emit_msg(D, dot(A.XT[0:DE], A.DP[...]))

    def own_message_gradients():
        landed(move_avg)
        landed(move_dg1)
        landed(move_dmsg)
        A.work_m[0:D] = dot_at(A.win2[RB : 2 * RB], A.dmsg_all[...]).astype(BF16)
        value = dot_at(A.avg_all[...], A.dg1_all[...])
        for u in range(4):
            row = 2 * D + DE + 128 * u
            A.work_m[row : row + 128] = value[:, 128 * u : 128 * u + 128].astype(BF16)

    for ref, used in ((A.work_e, 11 * DE), (A.work_m, 3 * D + DE)):
        if ref.shape[0] > used:
            ref[used:] = jnp.zeros((ref.shape[0] - used, 128), BF16)

    def reduce_mp(g, got, cuts, work, base):
        rows = g.shape[1]
        a1 = net.remote(g.at[pair], got.at[0], mp=pair)
        a2 = net.remote(g.at[third], got.at[1], mp=pair)
        a2.start()
        a1.start()
        yield
        a2.wait_recv()

        part = add_step(rows, 16, 128)

        @pl.loop(0, rows // part)
        def _(i):
            at = rows_at(part * i, part)
            got[1, at] = (g[cross, at].astype(F32) + got[1, at].astype(F32)).astype(BF16)

        step = rows // cuts
        pieces = []
        for i in range(cuts):
            at = pl.ds(step * i, step)
            b = net.remote(got.at[1, at], got.at[2, at], mp=cross)
            b.start()
            pieces.append(b)
            yield
        for c in (a1, *pieces):
            c.wait_recv()

        @pl.loop(0, rows // part)
        def _(i):
            at = rows_at(part * i, part)
            total = g[mp, at].astype(F32) + got[0, at].astype(F32) + got[2, at].astype(F32)
            work[rows_at(base + part * i, part)] = total.astype(BF16)

        for c in (a1, a2, *pieces):
            c.wait_send()

    def reduce_res(work, got, out, result, plan):
        size = work.shape[0]
        low = 0
        used = 0
        me = res // stride
        grain = S.grain
        for n, s in enumerate(plan):
            into = out if n == len(plan) - 1 else work
            if s >= 0:
                bit = (res // (1 << s)) % 2
                size = size // 2
                keep = low + bit * size
                give = low + (1 - bit) * size
                copies = [
                    net.remote(
                        work.at[rows_at(give, size, grain)],
                        got.at[pl.ds(used, size)],
                        res=across(s),
                    )
                ]
            else:
                size = size // 4
                keep = low + me * size
                copies = []
                for d in (2, 1, 3):
                    there = (me + d) % 4
                    copies.append(
                        net.remote(
                            work.at[rows_at(low + there * size, size, grain)],
                            got.at[pl.ds(used + (d - 1) * size, size)],
                            res=res + (there - me) * stride,
                        )
                    )
            for c in copies:
                c.start()
            yield
            for c in copies:
                c.wait()

            step = add_step(size, grain, work.shape[1])

            @pl.loop(0, size // step)
            def _(i, keep=keep, used=used, into=into, terms=len(copies), size=size, step=step):
                at = rows_at(keep + step * i, step, grain)
                total = work[at].astype(F32)
                for d in range(terms):
                    total = total + got[rows_at(used + d * size + step * i, step, grain)].astype(F32)
                into[at] = total.astype(BF16)

            used += size * len(copies)
            low = keep
        for s in reversed(plan):
            here = out.at[rows_at(low, size, grain)]
            if s >= 0:
                copies = [net.remote(here, here, res=across(s))]
                low = low - (res // (1 << s)) % 2 * size
                grow = 2
            else:
                copies = [
                    net.remote(here, here, res=res + ((me + d) % 4 - me) * stride)
                    for d in (2, 1, 3)
                ]
                low = low - me * size
                grow = 4
            for c in copies:
                c.start()
            yield
            for c in copies:
                c.wait()
            size = grow * size
        store.append(net.copy(out, result))

    def reduce_gains():
        copies = [net.remote(A.gains, A.gains_r.at[d - 1], mp=peer(d)) for d in (1, 2, 3)]
        for c in copies:
            c.start()
        yield
        for c in copies:
            c.wait()
        A.gains_t[0] = A.gains[...] + A.gains_r[0] + A.gains_r[1] + A.gains_r[2]
        for s in range(S.bits):
            c = net.remote(A.gains_t.at[s], A.gains_r.at[3 + s], res=across(s))
            c.start()
            yield
            c.wait()
            A.gains_t[s + 1] = A.gains_t[s] + A.gains_r[3 + s]
        store.append(net.copy(A.gains_t.at[S.bits], A.out_gains))

    def chain(*parts):
        for part in parts:
            yield from part

    def pump(*sums):
        for g in sums:
            next(g, None)

    sum_edge = chain(
        reduce_mp(A.ge, A.ge_r, 2, A.work_e, 4 * DE),
        reduce_res(A.work_e, A.sum_er, A.sum_e, A.pack_e, plans(S.bits)[0]),
    )
    sum_in = reduce_res(A.grad_i, A.sum_ir, A.sum_i, A.pack_i, plans(S.bits)[1])
    sum_out = reduce_res(A.grad_o, A.sum_or, A.sum_o, A.pack_o, plans(S.bits)[2])
    sum_msg = chain(
        reduce_mp(A.gm, A.gm_r, 1, A.work_m, D),
        reduce_res(A.work_m, A.sum_mr, A.sum_m, A.pack_m, plans(S.bits)[3]),
    )
    sum_gains = reduce_gains()

    def between_a():
        last_cross.wait_recv()
        on_last.start()
        pump(sum_edge)

    d_settled = A.nc_v[...] + dot(A.dself_low[...], A.We[:, 0:D])
    d_settled = d_settled + return_rows(
        lambda blk: dot(A.dq[RB * blk : RB * blk + RB], A.We[:, D : 2 * D]),
        A.back_send_a,
        A.back_recv_a,
        A.back_side_send_a,
        A.back_side_a,
        edge_weight_gradients,
        between_a,
    )

    normed_b = A.normed_b[...]
    d_sum_b = norm_back(d_settled, normed_b, A.inverse_b[:, 0:1], gain_b, D)
    A.gains[1:2] = jnp.sum(d_settled * normed_b, axis=0, keepdims=True)
    A.dF[quarter(mp)] = d_sum_b.astype(BF16)
    moved = gather_rows(A.dF)
    landed(moved)
    late.extend(moved)
    A.hid[...] = dot_bt(A.dF[...], A.fo_v[...])

    @unrolled(RB // 16)
    def _(i):
        rows = rows_at(16 * i, 16)
        A.dT[rows] = (A.hid[rows] * A.hslope[rows]).astype(BF16)

    A.part[...] = dot_bt(A.dT[...], A.fi_v[...])
    A.pb3[...] = A.part[...].astype(BF16)
    moved = scatter_sum_start(A.pb3, A.pr3)
    pump(sum_edge)
    A.grad_i[...] = dot_at(A.ug2[...], A.dT[...]).astype(BF16)
    pump(sum_in)
    A.grad_o[...] = dot_at(A.smooth[...], A.dF[...]).astype(BF16)
    pump(sum_out)
    d_middle = d_sum_b + A.part[quarter(mp)]
    landed(moved)
    late.extend(moved)
    for d in range(3):
        d_middle = d_middle + A.pr3[d].astype(F32)
    normed_a = A.normed_a[...]
    d_sum_a = norm_back(d_middle, normed_a, A.inverse_a[:, 0:1], gain_a, D)
    A.gains[0:1] = jnp.sum(d_middle * normed_a, axis=0, keepdims=True)
    pump(sum_gains)
    A.dsa[...] = d_sum_a
    A.dg1[...] = d_sum_a.astype(BF16)
    A.dg1_all[quarter(mp)] = A.dg1[...]
    move_dg1 = gather_rows(A.dg1_all)
    late.extend(move_dg1)
    A.davg[...] = dot_bt(A.dg1[...], A.Wo[...])

    for sub in range(RQ // 16):
        mine = A.davg[16 * sub : 16 * sub + 16]

        def back_step(k, total, sub=sub, mine=mine):
            rows = rows_at(RQ * k + 16 * sub, 16)
            d = (mine * A.slope[rows].astype(F32)).astype(BF16)
            A.DP[rows] = d
            return total + d.astype(F32)

        total = lax.fori_loop(0, K, back_step, jnp.zeros((16, HM), F32), unroll=4)
        A.dmsg_low[16 * sub : 16 * sub + 16] = total.astype(BF16)

    move_dmsg = spread_columns(A.dmsg_low, A.dmsg_all)
    pump(sum_edge)
    for blk in range(3):
        at = slice(RB * blk, RB * blk + RB)
        A.dq1[at] = dot(A.XT[DE + RB * blk : DE + RB * blk + RB], A.DP[...]).astype(BF16)

    pump(sum_in, sum_out)
    message_weight_gradients()
    pump(sum_msg, sum_gains)
    own_message_gradients()
    pump(sum_msg)

    def edge_gradient(start, stop):
        @pl.loop(start, stop)
        def _(c):
            rows = rows_at(EC * c, EC)
            A.EG[rows] = A.EG[rows] + dot_bt(A.DP[rows], A.T[0:256])
            for j in range(3):
                lanes = pl.multiple_of(1152 * c + 384 * j, 128)
                ends = [
                    jnp.where(is_edge, A.EG[rows_at(EC * c + RQ * (2 * j + p), RQ)], 0.0)
                    for p in range(2)
                ]
                pair_store(A.ec_v, lanes, ends[0], ends[1])

    def close_edges():
        store.append(net.copy(A.ec_v, A.out_edge_grad))
        for a, b, c in streams:
            a.wait()
            b.wait_send()
            c.wait()
        last_pair.wait()
        last_cross.wait_send()
        on_last.wait()
        store.append(net.copy(A.new_edges, A.out_edges))

    def fill_b():
        edge_gradient(0, 3)
        pump(sum_in, sum_out, sum_gains)
        edge_gradient(3, chunks)
        pump(sum_msg, sum_edge)

    back = return_rows(
        lambda blk: dot_bt(A.dq1[RB * blk : RB * blk + RB], A.Wm[D : 2 * D]),
        A.back_send_b,
        A.back_recv_b,
        A.back_side_send_b,
        A.back_side_b,
        fill_b,
        lambda: pump(sum_in, sum_out, sum_gains),
    )
    A.node_grad_v[...] = 0.5 * (A.dsa[...] + dot_bt(A.dmsg_low[...], A.Wm[0:D]) + back)
    store.append(net.copy(A.node_grad_v, A.out_node_grad))

    pump(sum_edge, sum_msg)
    close_edges()
    work = [sum_msg, sum_edge, sum_in, sum_out, sum_gains]
    while work:
        for g in list(work):
            try:
                next(g)
            except StopIteration:
                work.remove(g)
    for c in store:
        c.wait()
    for s in (spread_msg_in, spread_msg_out, *spread_edge, halo, window2, window3):
        s.sent()
    for c in late:
        c.wait_send()
    assert net.remote_count <= S.remote and net.local_count <= S.local


def build(S):
    E = S.RQ * S.K
    W = 3 * S.RB
    EC = 6 * S.RQ
    grain = S.grain * S.n_res
    rows_e = up(11 * S.DE, grain)
    rows_m = up(3 * S.D + S.DE, grain)
    in_names = ["nodes", "edges", "neighbours", "edge_mask", "msg_in", "msg_out", "gain_a"]
    in_names += ["ffn_in", "ffn_out", "gain_b", "edge_in", "edge_out", "gain_c"]
    in_names += ["node_cot", "edge_cot"]
    outs = dict(
        out_nodes=((S.RB, S.D), BF16),
        out_edges=((S.RB, S.K * S.DE), BF16),
        out_node_grad=((S.RQ, S.D), F32),
        out_edge_grad=((S.RQ, S.K * S.DE), F32),
        pack_e=((rows_e, 128), BF16),
        pack_i=((S.D, S.FL), BF16),
        pack_o=((S.FL, S.D), BF16),
        pack_m=((rows_m, 128), BF16),
        out_gains=((8, S.D), F32),
    )
    scratch = dict(
        nodes_v=((S.RB, S.D), F32),
        nbr_v=((S.K, S.RB), jnp.int32),
        mask_v=((S.K, S.RB), jnp.int32),
        columns=((S.RB, 128), F32),
        new_edges=((S.RB, S.K * S.DE), BF16),
        node_grad_v=((S.RQ, S.D), F32),
        e_v=((S.RQ, S.K * S.DE), F32),
        ec_v=((S.RQ, S.K * S.DE), F32),
        nc_v=((S.RQ, S.D), F32),
        Wm=((2 * S.D + S.DE, S.HM), BF16),
        Wo=((S.HM, S.D), BF16),
        fi_v=((S.D, S.FL), BF16),
        fo_v=((S.FL, S.D), BF16),
        We=((S.HE, 2 * S.D + S.DE), BF16),
        Eo=((S.HE, S.DE), BF16),
        Eop=((S.HE, 256), BF16),
        win1=((W, S.D), BF16),
        win2=((W, S.D), BF16),
        win3=((W, S.D), BF16),
        XE=((E, 256), BF16),
        XM=((E, 256), BF16),
        XO=((E, 512), BF16),
        XT=((768, E), BF16),
        WB=((E, 128), F32),
        T=((768, S.HM), BF16),
        Te=((768, S.HE), BF16),
        selfs=((S.RQ, S.HM), F32),
        selfe=((S.RQ, S.HE), F32),
        total=((S.RQ, S.HM), F32),
        slope=((E, S.HM), BF16),
        avg=((S.RQ, S.HM), BF16),
        ug1=((S.RB, S.D), BF16),
        ug2=((S.RB, S.D), BF16),
        hid=((S.RB, S.FL), F32),
        smooth=((S.RB, S.FL), BF16),
        hslope=((S.RB, S.FL), F32),
        part=((S.RB, S.D), F32),
        pb1=((S.RB, S.D), BF16),
        pb2=((S.RB, S.D), BF16),
        pb3=((S.RB, S.D), BF16),
        pr1=((3, S.RQ, S.D), BF16),
        pr2=((3, S.RQ, S.D), BF16),
        pr3=((3, S.RQ, S.D), BF16),
        normed_a=((S.RQ, S.D), F32),
        normed_b=((S.RQ, S.D), F32),
        inverse_a=((S.RQ, 128), F32),
        inverse_b=((S.RQ, 128), F32),
        mixed=((S.RQ, S.D), F32),
        pre=((EC, S.HM), F32),
        base=((2, EC, S.HE), F32),
        pre2=((2, EC, S.HE), F32),
        G=((2, EC, S.HE), BF16),
        upd=((2, EC, 256), F32),
        emix=((2, EC, 256), F32),
        G2=((E, S.HE), BF16),
        DO=((E, 256), BF16),
        DP2=((E, S.HE), BF16),
        EG=((E, 256), F32),
        dself=((S.RQ, S.HE), F32),
        dself_low=((S.RQ, S.HE), BF16),
        dq=((W, S.HE), BF16),
        gains=((8, S.D), F32),
        gains_r=((3 + S.bits, 8, S.D), F32),
        gains_t=((1 + S.bits, 8, S.D), F32),
        back_send_a=((4, 3, S.RQ, S.D), BF16),
        back_recv_a=((3, 3, S.RQ, S.D), BF16),
        back_side_send_a=((2, S.RQ, S.D), BF16),
        back_side_a=((2, S.RQ, S.D), BF16),
        back_send_b=((4, 3, S.RQ, S.D), BF16),
        back_recv_b=((3, 3, S.RQ, S.D), BF16),
        back_side_send_b=((2, S.RQ, S.D), BF16),
        back_side_b=((2, S.RQ, S.D), BF16),
        dF=((S.RB, S.D), BF16),
        dT=((S.RB, S.FL), BF16),
        dsa=((S.RQ, S.D), F32),
        dg1=((S.RQ, S.D), BF16),
        davg=((S.RQ, S.HM), F32),
        DP=((E, S.HM), BF16),
        dmsg_low=((S.RQ, S.HM), BF16),
        dq1=((W, S.HM), BF16),
        ge=((4, 7 * S.DE, 128), BF16),
        ge_r=((3, 7 * S.DE, 128), BF16),
        work_e=((rows_e, 128), BF16),
        ds_send=((4, S.RQ, 256), BF16),
        ds_all=((S.RB, 256), BF16),
        avg_all=((S.RB, 128), BF16),
        dg1_all=((S.RB, S.D), BF16),
        dmsg_all=((S.RB, 128), BF16),
        sum_er=((rows_e, 128), BF16),
        sum_e=((rows_e, 128), BF16),
        grad_i=((S.D, S.FL), BF16),
        sum_ir=((S.D, S.FL), BF16),
        sum_i=((S.D, S.FL), BF16),
        grad_o=((S.FL, S.D), BF16),
        sum_or=((S.FL, S.D), BF16),
        sum_o=((S.FL, S.D), BF16),
        gm=((4, S.D + S.DE, 128), BF16),
        gm_r=((3, S.D + S.DE, 128), BF16),
        work_m=((rows_m, 128), BF16),
        sum_mr=((rows_m, 128), BF16),
        sum_m=((rows_m, 128), BF16),
    )
    names = list(scratch) + ["send", "recv", "local"]
    shapes = [pltpu.VMEM(*v) for v in scratch.values()] + [
        pltpu.SemaphoreType.DMA((S.remote,)),
        pltpu.SemaphoreType.DMA((S.remote,)),
        pltpu.SemaphoreType.DMA((S.local,)),
    ]
    body = functools.partial(kernel_body, S, in_names, list(outs), names)
    body.__name__ = "layer"
    gains = ("gain_a", "gain_b", "gain_c")
    return pl.pallas_call(
        body,
        name="layer",
        out_shape=[jax.ShapeDtypeStruct(*v) for v in outs.values()],
        in_specs=[VMEM if n in gains else ANY for n in in_names],
        out_specs=[ANY] * len(outs),
        scratch_shapes=shapes,
        compiler_params=pltpu.CompilerParams(
            collective_id=0, has_side_effects=True, vmem_limit_bytes=62 * 1024 * 1024
        ),
    )


def unpack_body(S, names, *refs):
    A = SimpleNamespace(**dict(zip(names, refs, strict=True)))
    D, DE, RB = S.D, S.DE, S.RB
    count = [0]

    def copy(src, dst):
        c = pltpu.make_async_copy(src, dst, A.sems.at[count[0]])
        count[0] += 1
        c.start()
        return c

    part = RB // 4
    edge_loads = [
        copy(A.in_edges.at[pl.ds(part * i, part)], A.edges_l.at[pl.ds(part * i, part)])
        for i in range(4)
    ]
    pairs = (
        (A.in_e, A.e_l),
        (A.in_i, A.i_l),
        (A.in_o, A.o_l),
        (A.in_m, A.m_l),
        (A.in_nodes, A.nodes_l),
        (A.in_gains, A.gains_l),
    )
    loads = [copy(*p) for p in pairs]
    grads = [copy(A.in_edge_grad, A.eg_l), copy(A.in_node_grad, A.ng_l)]
    stores = []
    for i in range(4):
        edge_loads[i].wait()

        @pl.loop(0, part // 16)
        def _(k, i=i):
            at = pl.ds(pl.multiple_of(part * i + 16 * k, 16), 16)
            A.edges_f[at] = A.edges_l[at].astype(F32)

        at = pl.ds(part * i, part)
        stores.append(copy(A.edges_f.at[at], A.o1.at[at]))
    for c in (*grads, *loads):
        c.wait()
    stores += [copy(A.eg_l, A.o3), copy(A.ng_l, A.o2)]

    def widen(src, dst, out, rows):
        dst[...] = src[0:rows].astype(F32)
        stores.append(copy(dst, out))

    widen(A.i_l, A.i_f, A.o7, D)
    widen(A.o_l, A.o_f, A.o8, S.FL)
    widen(A.nodes_l, A.nodes_f, A.o0, RB)
    widen(A.m_l, A.m_f, A.o4, 2 * D + DE)
    for u in range(4):
        row = 2 * D + DE + 128 * u
        A.mo_f[:, 128 * u : 128 * u + 128] = A.m_l[row : row + 128].astype(F32)
    stores.append(copy(A.mo_f, A.o5))
    mixed = A.e_l[9 * DE : 10 * DE].astype(F32)
    for t in range(9):
        A.ei_f[:, 128 * t : 128 * t + 128] = A.e_l[DE * t : DE * t + DE].astype(F32)
    A.ei_f[:, 1152 : 1152 + 64] = mixed[:, 0:64]
    stores.append(copy(A.ei_f, A.o10))
    A.eo_f[:, 0:128] = A.e_l[10 * DE : 11 * DE].astype(F32)
    A.eo_f[:, 128:DE] = pltpu.roll(mixed, 64, 1)[:, 0:64]
    stores.append(copy(A.eo_f, A.o11))
    A.ga_f[...] = A.gains_l[0:1]
    A.gb_f[...] = A.gains_l[1:2]
    A.gc_f[...] = A.gains_l[2:3, 0:DE]
    for src, out in ((A.ga_f, A.o6), (A.gb_f, A.o9), (A.gc_f, A.o12)):
        stores.append(copy(src, out))
    for c in stores:
        c.wait()


def unpack(S, values):
    D, DE, RB, RQ, K, FL = S.D, S.DE, S.RB, S.RQ, S.K, S.FL
    ins = ["in_nodes", "in_edges", "in_node_grad", "in_edge_grad"]
    ins += ["in_e", "in_i", "in_o", "in_m", "in_gains"]
    shapes = [
        (RB, D),
        (RB, K * DE),
        (RQ, D),
        (RQ, K * DE),
        (2 * D + DE, S.HM // 4),
        (S.HM // 4, D),
        (1, D),
        (D, FL),
        (FL, D),
        (1, D),
        (S.HE // 4, 2 * D + DE),
        (S.HE // 4, DE),
        (1, DE),
    ]
    outs = ["o%d" % i for i in range(13)]
    scratch = dict(
        edges_l=((RB, K * DE), BF16),
        edges_f=((RB, K * DE), F32),
        e_l=(values[4].shape, BF16),
        i_l=((D, FL), BF16),
        o_l=((FL, D), BF16),
        m_l=(values[7].shape, BF16),
        nodes_l=((RB, D), BF16),
        gains_l=((8, D), F32),
        eg_l=((RQ, K * DE), F32),
        ng_l=((RQ, D), F32),
        i_f=((D, FL), F32),
        o_f=((FL, D), F32),
        nodes_f=((RB, D), F32),
        m_f=(shapes[4], F32),
        mo_f=(shapes[5], F32),
        ei_f=(shapes[10], F32),
        eo_f=(shapes[11], F32),
        ga_f=(shapes[6], F32),
        gb_f=(shapes[9], F32),
        gc_f=(shapes[12], F32),
    )
    names = ins + outs + list(scratch) + ["sems"]
    body = functools.partial(unpack_body, S, names)
    return list(
        pl.pallas_call(
            body,
            name="unpack",
            out_shape=[jax.ShapeDtypeStruct(x, F32) for x in shapes],
            in_specs=[ANY] * len(ins),
            out_specs=[ANY] * len(outs),
            scratch_shapes=[pltpu.VMEM(*v) for v in scratch.values()]
            + [pltpu.SemaphoreType.DMA((32,))],
            compiler_params=pltpu.CompilerParams(vmem_limit_bytes=62 * 1024 * 1024),
        )(*values)
    )


STOP = 0


def plans(bits):
    low = list(range(bits - 2))
    high = [bits - 2, bits - 1]
    return [low + [-1], low + high, high + low, low + [-1]]


def on_device(n_res, *args):
    nodes, edges, neighbours, _, _, _, _, ffn_in = args[:8]
    height = nodes.shape[0]
    degree = neighbours.shape[1]
    S = SimpleNamespace(
        n_res=n_res,
        bits=int(math.log2(n_res)),
        RB=height,
        RQ=height // 4,
        K=degree,
        D=nodes.shape[1],
        DE=edges.shape[1] // degree,
        HM=args[4].shape[1] * 4,
        HE=args[10].shape[1] * 4,
        FL=ffn_in.shape[1],
        grain=16 if n_res <= 16 else 8,
        remote=200,
        local=32,
        stop=STOP,
    )
    fixed = [a.reshape(1, -1) if a.ndim == 1 else a for a in args]
    for i in (2, 3, 10):
        fixed[i] = fixed[i].T
    out = unpack(S, build(S)(*fixed))
    for i in (6, 9, 12):
        out[i] = out[i].reshape(-1)
    out[10] = out[10].T
    return tuple(out)


def solution(mesh):
    in_specs = (
        P("res", None),
        P("res", None),
        P("res", None),
        P("res", None),
        P(None, "mp"),
        P("mp", None),
        P(),
        P(None, "mp"),
        P("mp", None),
        P(),
        P(None, "mp"),
        P("mp", None),
        P(),
        P("res", None),
        P("res", None),
    )
    out_specs = (
        P("res", None),
        P("res", None),
        P(("res", "mp"), None),
        P(("res", "mp"), None),
        P(None, "mp"),
        P("mp", None),
        P(),
        P(None, "mp"),
        P("mp", None),
        P(),
        P(None, "mp"),
        P("mp", None),
        P(),
    )
    return jax.shard_map(
        functools.partial(on_device, mesh.shape["res"]),
        mesh=mesh,
        in_specs=in_specs,
        out_specs=out_specs,
        check_vma=False,
    )
```

```python
import functools
import math
from types import SimpleNamespace

import jax
import jax.numpy as jnp
from jax import lax
from jax.experimental import pallas as pl
from jax.experimental.pallas import tpu as pltpu
from jax.sharding import PartitionSpec as P

EPSILON = 1e-05
F32 = jnp.float32
BF16 = jnp.bfloat16
MESH = pl.DeviceIdType.MESH
ROOT_TWO_PI = 0.3989422804014327
ROOT_HALF = 0.7071067811865476
ANY = pl.BlockSpec(memory_space=pl.ANY)
VMEM = pl.BlockSpec(memory_space=pltpu.VMEM)


def dot(left, right):
    return jnp.dot(left, right, preferred_element_type=F32)


def dot_bt(left, right):
    return lax.dot_general(left, right, (((1,), (1,)), ((), ())), preferred_element_type=F32)


def dot_at(left, right):
    return lax.dot_general(left, right, (((0,), (0,)), ((), ())), preferred_element_type=F32)


def bell(v):
    return 0.5 + 0.5 * lax.erf(v * ROOT_HALF)


def bell_slope(phi, v):
    return phi + v * (jnp.exp(-0.5 * (v * v)) * ROOT_TWO_PI)


def norm_parts(values, width):
    scale = 1.0 / width
    centred = values - jnp.sum(values, axis=-1, keepdims=True) * scale
    inverse = lax.rsqrt(jnp.sum(centred * centred, axis=-1, keepdims=True) * scale + EPSILON)
    return centred * inverse, inverse


def norm_back(upstream, normed, inverse, gain, width):
    scale = 1.0 / width
    scaled = upstream * gain
    mean = jnp.sum(scaled, axis=-1, keepdims=True) * scale
    along = jnp.sum(scaled * normed, axis=-1, keepdims=True) * scale
    return inverse * (scaled - mean - normed * along)


def up(rows, step):
    return -(-rows // step) * step


def add_step(rows, grain, lanes):
    parts = rows // grain
    return grain * max(
        n for n in range(1, parts + 1) if parts % n == 0 and (n == 1 or n * grain * lanes <= 32768)
    )


def unrolled(count):
    def run(step):
        for i in range(count):
            step(i)

    return run


class Net:
    def __init__(self, send, recv, local):
        self.send, self.recv, self.local = send, recv, local
        self.remote_count = 0
        self.local_count = 0

    def remote(self, src, dst, side="", **where):
        i = self.remote_count
        self.remote_count += 1
        return pltpu.make_async_remote_copy(
            src_ref=src,
            dst_ref=dst,
            send_sem=self.send.at[i],
            recv_sem=self.recv.at[i],
            device_id=where,
            device_id_type=MESH,
        )

    def reserve(self, count):
        i = self.remote_count
        self.remote_count += count
        return i

    def at(self, i, src, dst, **where):
        return pltpu.make_async_remote_copy(
            src_ref=src,
            dst_ref=dst,
            send_sem=self.send.at[i],
            recv_sem=self.recv.at[i],
            device_id=where,
            device_id_type=MESH,
        )

    def opened(self, i, src, dst, **where):
        return self.at(i, src, dst, **where)

    def copy(self, src, dst):
        i = self.local_count
        self.local_count += 1
        c = pltpu.make_async_copy(src, dst, self.local.at[i])
        c.start()
        return c


def kernel_body(S, in_names, out_names, scratch_names, *refs):
    names = in_names + out_names + scratch_names
    A = SimpleNamespace(**dict(zip(names, refs, strict=True)))
    net = Net(A.send, A.recv, A.local)
    RB, RQ, K, D, DE, HM, HE, FL = S.RB, S.RQ, S.K, S.D, S.DE, S.HM, S.HE, S.FL
    E = RQ * K
    W = 3 * RB
    EC = 6 * RQ
    res = lax.axis_index("res")
    mp = lax.axis_index("mp")
    has_l = res > 0
    has_r = res < S.n_res - 1
    pair = mp + 1 - 2 * (mp % 2)
    cross = (mp + 2) % 4
    third = (pair + 2) % 4

    def peer(d):
        return (mp + d) % 4

    def rows_at(start, size, step=16):
        return pl.ds(pl.multiple_of(start, step), size)

    def quarter(q, base=0):
        return rows_at(base + RQ * q, RQ)

    load_nodes = net.copy(A.nodes, A.nodes_v)
    load_nbr = net.copy(A.neighbours, A.nbr_v)
    load_mask = net.copy(A.edge_mask, A.mask_v)
    load_edges = net.copy(A.edges.at[quarter(mp)], A.e_v)
    own_msg_in = A.Wm.at[:, pl.ds(pl.multiple_of(mp * 128, 128), 128)]
    load_msg_in = net.copy(A.msg_in, own_msg_in)
    own_msg_out = A.Wo.at[rows_at(mp * 128, 128)]
    load_msg_out = net.copy(A.msg_out, own_msg_out)
    load_ffn_in = net.copy(A.ffn_in, A.fi_v)
    load_ffn_out = net.copy(A.ffn_out, A.fo_v)
    big, small = HE // 4 // 3 * 2, HE // 4 // 3

    def main_rows(ref):
        return lambda q: ref.at[rows_at(big * q, big)]

    def rest_rows(ref):
        return lambda q: ref.at[rows_at(4 * big + small * q, small)]

    first, rest = pl.ds(0, big), pl.ds(big, small)
    edge_parts = (
        (A.edge_in.at[first], main_rows(A.We)),
        (A.edge_out.at[first], main_rows(A.Eo)),
        (A.edge_in.at[rest], rest_rows(A.We)),
        (A.edge_out.at[rest], rest_rows(A.Eo)),
    )
    load_edge_weights = [net.copy(src, place(mp)) for src, place in edge_parts]
    load_node_cot = net.copy(A.node_cot.at[quarter(mp)], A.nc_v)
    load_edge_cot = net.copy(A.edge_cot.at[quarter(mp)], A.ec_v)

    barrier = pltpu.get_barrier_semaphore()

    def greet(**where):
        pl.semaphore_signal(barrier, inc=1, device_id=where, device_id_type=MESH)

    def across(s):
        return res + (1 << s) * (1 - 2 * ((res // (1 << s)) % 2))

    for d in (1, 2, 3):
        greet(mp=peer(d))
    for s in range(S.bits - 2):
        greet(res=across(s))
    stride = S.n_res // 4
    for d in (1, 2, 3):
        greet(res=res + ((res // stride + d) % 4 - res // stride) * stride)

    @pl.when(has_l)
    def _():
        greet(res=res - 1)

    @pl.when(has_r)
    def _():
        greet(res=res + 1)

    sides = (res + S.n_res - 1) // S.n_res + 1 - (res + 1) // S.n_res
    pl.semaphore_wait(barrier, 6 + S.bits - 2 + sides)

    class Spread:
        def __init__(self, src, place):
            own = place(mp)
            self.first = [net.remote(src, own, mp=pair), net.remote(src, own, mp=cross)]
            self.then = net.remote(place(cross), place(cross), mp=pair)

        def start(self):
            for c in self.first:
                c.start()

        def forward(self):
            self.first[1].wait_recv()
            self.then.start()

        def wait(self):
            self.first[0].wait_recv()
            self.then.wait_recv()

        def sent(self):
            for c in self.first:
                c.wait_send()
            self.then.wait_send()

    spread_msg_in = Spread(
        A.msg_in, lambda q: A.Wm.at[:, pl.ds(pl.multiple_of(q * 128, 128), 128)]
    )
    spread_msg_out = Spread(A.msg_out, lambda q: A.Wo.at[rows_at(q * 128, 128)])
    spread_edge = [Spread(src, place) for src, place in edge_parts]

    def clear_sides(win):
        @pl.when(jnp.logical_not(has_l))
        def _():
            win[0:RB] = jnp.zeros((RB, D), BF16)

        @pl.when(jnp.logical_not(has_r))
        def _():
            win[2 * RB : 3 * RB] = jnp.zeros((RB, D), BF16)

    half = RB // 2

    class Halo:
        def __init__(self, win):
            h = mp % 2
            own = win.at[rows_at(RB + half * h, half)]
            left = win.at[rows_at(half * h, half)]
            right = win.at[rows_at(2 * RB + half * h, half)]
            self.to_l = net.remote(own, right, side="l", res=res - 1)
            self.to_r = net.remote(own, left, side="r", res=res + 1)
            self.on_l = net.remote(left, left, mp=pair)
            self.on_r = net.remote(right, right, mp=pair)

        def start(self):
            pl.when(has_l)(self.to_l.start)
            pl.when(has_r)(self.to_r.start)

        def forward(self):
            @pl.when(has_l)
            def _():
                self.to_r.wait_recv()
                self.on_l.start()

            @pl.when(has_r)
            def _():
                self.to_l.wait_recv()
                self.on_r.start()

        def wait(self):
            pl.when(has_l)(self.on_l.wait_recv)
            pl.when(has_r)(self.on_r.wait_recv)

        def sent(self):
            @pl.when(has_l)
            def _():
                self.to_l.wait_send()
                self.on_l.wait_send()

            @pl.when(has_r)
            def _():
                self.to_r.wait_send()
                self.on_r.wait_send()

    class Window:
        def __init__(self, win):
            own = win.at[quarter(mp, RB)]
            left = win.at[quarter(mp)]
            right = win.at[quarter(mp, 2 * RB)]
            self.to_l = net.remote(own, right, side="l", res=res - 1)
            self.to_r = net.remote(own, left, side="r", res=res + 1)
            self.mine = [net.remote(own, own, mp=peer(d)) for d in (1, 2, 3)]
            self.on_l = [net.remote(left, left, mp=peer(d)) for d in (1, 2, 3)]
            self.on_r = [net.remote(right, right, mp=peer(d)) for d in (1, 2, 3)]

        def start(self):
            pl.when(has_l)(self.to_l.start)
            pl.when(has_r)(self.to_r.start)
            for c in self.mine:
                c.start()

        def forward(self):
            @pl.when(has_l)
            def _():
                self.to_r.wait_recv()
                for c in self.on_l:
                    c.start()

            @pl.when(has_r)
            def _():
                self.to_l.wait_recv()
                for c in self.on_r:
                    c.start()

        def wait_own(self):
            for c in self.mine:
                c.wait_recv()

        def wait(self):
            @pl.when(has_l)
            def _():
                for c in self.on_l:
                    c.wait_recv()

            @pl.when(has_r)
            def _():
                for c in self.on_r:
                    c.wait_recv()

        def sent(self):
            for c in self.mine:
                c.wait_send()

            @pl.when(has_l)
            def _():
                self.to_l.wait_send()
                for c in self.on_l:
                    c.wait_send()

            @pl.when(has_r)
            def _():
                self.to_r.wait_send()
                for c in self.on_r:
                    c.wait_send()

    def gather_rows(buf):
        own = buf.at[quarter(mp)]
        copies = [net.remote(own, own, mp=peer(d)) for d in (1, 2, 3)]
        for c in copies:
            c.start()
        return copies

    def scatter_sum_start(buf, into):
        copies = [
            net.remote(buf.at[quarter(peer(d))], into.at[d - 1], mp=peer(d)) for d in (1, 2, 3)
        ]
        for c in copies:
            c.start()
        return copies

    def landed(copies):
        for c in copies:
            c.wait_recv()

    late = []

    def lanes_at(q):
        return pl.ds(pl.multiple_of(128 * q, 128), 128)

    def spread_columns(src, dst):
        copies = [
            net.remote(src.at[:, lanes_at(peer(d))], dst.at[quarter(mp)], mp=peer(d))
            for d in (1, 2, 3)
        ]
        for c in copies:
            c.start()
        late.extend(copies)
        dst[quarter(mp)] = src[:, lanes_at(mp)]
        return copies

    def return_rows(product, send, recv, side_send, side_recv, fill, between):
        for blk in range(3):
            part = product(blk)
            for q in range(4):
                send[q, blk] = part[RQ * q : RQ * q + RQ].astype(BF16)
        copies = [net.remote(send.at[peer(d)], recv.at[d - 1], mp=peer(d)) for d in (1, 2, 3)]
        for c in copies:
            c.start()
        fill()
        landed(copies)
        late.extend(copies)

        def total(blk):
            out = send[mp, blk].astype(F32)
            for d in range(3):
                out = out + recv[d, blk].astype(F32)
            return out

        side_send[0] = total(0).astype(BF16)
        side_send[1] = total(2).astype(BF16)
        to_l = net.remote(side_send.at[0], side_recv.at[1], side="l", res=res - 1)
        to_r = net.remote(side_send.at[1], side_recv.at[0], side="r", res=res + 1)
        pl.when(has_l)(to_l.start)
        pl.when(has_r)(to_r.start)
        mid = total(1)
        between()
        pl.when(has_l)(to_r.wait_recv)
        pl.when(has_r)(to_l.wait_recv)
        pl.when(has_l)(to_l.wait_send)
        pl.when(has_r)(to_r.wait_send)
        return mid + side_recv[0].astype(F32) + side_recv[1].astype(F32)

    spread_msg_in.start()
    spread_msg_out.start()
    load_nodes.wait()

    @unrolled(RB // 16)
    def _(i):
        A.win1[rows_at(RB + 16 * i, 16)] = A.nodes_v[rows_at(16 * i, 16)].astype(BF16)

    halo = Halo(A.win1)
    halo.start()
    for win in (A.win1, A.win2, A.win3):
        clear_sides(win)
    for ref in (A.back_side_a, A.back_side_b):
        ref[...] = jnp.zeros_like(ref)

    load_nbr.wait()
    load_mask.wait()
    load_edges.wait()
    stack = jnp.concatenate(
        [A.nbr_v[...].astype(F32), A.mask_v[...].astype(F32), jnp.zeros((128 - 2 * K, RB), F32)],
        axis=0,
    )
    stack = jnp.concatenate([stack, jnp.zeros((128, 256 - RB), F32)], axis=1)
    A.columns[...] = jnp.transpose(stack)[0:RB]
    columns = A.columns[rows_at(RQ * mp, RQ)]
    local = columns[:, 0:K].astype(jnp.int32) - (res - 1) * RB + DE
    live = columns[:, K : 2 * K]
    mean_weight = live / jnp.maximum(jnp.sum(live, axis=1, keepdims=True), 1.0)
    lane256 = lax.broadcasted_iota(jnp.int32, (RQ, 256), 1)
    lane512 = lax.broadcasted_iota(jnp.int32, (RQ, 512), 1) + 256
    is_edge = lane256 < DE

    def pair_load(buf, base):
        even = buf[:, pl.ds(base, 256)]
        odd = pltpu.roll(buf[:, pl.ds(base + 128, 256)], 192, 1)
        return jnp.where(is_edge, even, 0.0), jnp.where(is_edge, odd, 0.0)

    def pair_store(buf, base, even, odd, sub=slice(None)):
        back = pltpu.roll(odd, 64, 1)
        buf[sub, pl.ds(base, 128)] = even[:, :128].astype(buf.dtype)
        buf[sub, pl.ds(base + 128, 128)] = (even[:, 128:] + back[:, :128]).astype(buf.dtype)
        buf[sub, pl.ds(base + 256, 128)] = back[:, 128:].astype(buf.dtype)

    for j in range(K // 2):
        both = pair_load(A.e_v, 384 * j)
        for p in range(2):
            k = 2 * j + p
            column = local[:, k : k + 1]
            hot = jnp.where(column == lane256, 1.0, 0.0)
            A.XE[RQ * k : RQ * k + RQ] = jnp.where(is_edge, both[p], hot).astype(BF16)
            A.XO[RQ * k : RQ * k + RQ] = jnp.where(column == lane512, 1.0, 0.0).astype(BF16)
            A.WB[RQ * k : RQ * k + RQ] = jnp.broadcast_to(mean_weight[:, k : k + 1], (RQ, 128))

    halo.forward()

    full = E // 128

    @pl.loop(0, full)
    def _(c):
        at = pl.ds(pl.multiple_of(128 * c, 128), 128)
        A.XT[0:256, at] = A.XE[at].T
        A.XT[256:768, at] = A.XO[at].T

    if E % 128:
        at = slice(full * 128, E)
        A.XT[0:256, at] = A.XE[at].T
        A.XT[256:768, at] = A.XO[at].T

    spread_msg_in.forward()
    halo.wait()

    gain_a = A.gain_a[...]
    gain_b = A.gain_b[...]
    load_msg_in.wait()
    load_msg_out.wait()

    def node_table(win):
        for blk in (1, 0, 2):
            part = dot(win[RB * blk : RB * blk + RB], A.Wm[D : 2 * D])
            A.T[DE + RB * blk : DE + RB * blk + RB] = part.astype(BF16)

    def message_mean(win, keep):
        A.selfs[...] = dot(win[quarter(mp, RB)], A.Wm[0:D])
        A.total[...] = jnp.zeros((RQ, HM), F32)

        @pl.loop(0, E // EC)
        def _(c):
            rows = rows_at(EC * c, EC)
            left = jnp.concatenate([A.XE[rows], A.XO[rows]], axis=1)
            A.pre[...] = dot(left, A.T[...])

            @unrolled(RQ // 16)
            def _(sub):
                own = slice(16 * sub, 16 * sub + 16)
                mine = A.selfs[own]
                total = A.total[own]
                for k in range(6):
                    at = RQ * k + 16 * sub
                    v = A.pre[at : at + 16] + mine
                    there = rows_at(EC * c + at, 16)
                    w = jnp.concatenate([A.WB[there]] * (HM // 128), axis=1)
                    phi = bell(v)
                    if keep:
                        A.slope[there] = (w * bell_slope(phi, v)).astype(BF16)
                    total = total + w * (v * phi)
                A.total[own] = total

        A.avg[...] = A.total[...].astype(BF16)

    def node_tail(states, ug, part_b, part_r, keep):
        normed_a, inverse_a = norm_parts(states + dot(A.avg[...], A.Wo[...]), D)
        middle = normed_a * gain_a
        ug[quarter(mp)] = middle.astype(BF16)
        moved = gather_rows(ug)
        landed(moved)
        late.extend(moved)
        A.hid[...] = dot(ug[...], A.fi_v[...])

        @unrolled(RB // 16)
        def _(i):
            rows = rows_at(16 * i, 16)
            v = A.hid[rows]
            phi = bell(v)
            A.smooth[rows] = (v * phi).astype(BF16)
            if keep:
                A.hslope[rows] = bell_slope(phi, v)

        A.part[...] = dot(A.smooth[...], A.fo_v[...])
        part_b[...] = A.part[...].astype(BF16)
        moved = scatter_sum_start(part_b, part_r)
        total = middle + A.part[quarter(mp)]
        landed(moved)
        late.extend(moved)
        for d in range(3):
            total = total + part_r[d].astype(F32)
        normed_b, inverse_b = norm_parts(total, D)
        if keep:
            A.normed_a[...] = normed_a
            A.inverse_a[...] = jnp.broadcast_to(inverse_a, (RQ, 128))
            A.normed_b[...] = normed_b
            A.inverse_b[...] = jnp.broadcast_to(inverse_b, (RQ, 128))
        return normed_b * gain_b

    spread_msg_in.wait()
    spread_edge[0].start()
    spread_edge[1].start()
    A.T[0:DE] = A.Wm[2 * D : 2 * D + DE]
    node_table(A.win1)
    message_mean(A.win1, False)
    spread_msg_out.forward()
    spread_msg_out.wait()
    load_ffn_in.wait()
    load_ffn_out.wait()
    own_nodes = A.nodes_v[quarter(mp)]
    predicted = node_tail(own_nodes, A.ug1, A.pb1, A.pr1, False)
    A.mixed[...] = 0.5 * (own_nodes + predicted)
    A.win2[quarter(mp, RB)] = A.mixed[...].astype(BF16)
    window2 = Window(A.win2)
    window2.start()
    window2.forward()
    window2.wait_own()
    window2.wait()
    spread_edge[2].start()
    spread_edge[3].start()
    spread_edge[0].forward()
    spread_edge[1].forward()
    node_table(A.win2)
    message_mean(A.win2, True)
    move_avg = spread_columns(A.avg, A.avg_all)
    spread_edge[2].forward()
    spread_edge[3].forward()
    settled = node_tail(A.mixed[...], A.ug2, A.pb2, A.pr2, True)
    A.win3[quarter(mp, RB)] = settled.astype(BF16)
    window3 = Window(A.win3)
    window3.start()
    window3.forward()

    for c in (*spread_edge, *load_edge_weights):
        c.wait()
    A.Eop[...] = jnp.concatenate([A.Eo[...], jnp.zeros((HE, 64), BF16)], axis=1)
    A.Te[0:DE] = A.We[:, 2 * D : 2 * D + DE].T
    window3.wait_own()
    window3.wait()
    store = [net.copy(A.win3.at[RB : 2 * RB], A.out_nodes)]

    for blk in (1, 0, 2):
        part = dot_bt(A.win3[RB * blk : RB * blk + RB], A.We[:, D : 2 * D])
        A.Te[DE + RB * blk : DE + RB * blk + RB] = part.astype(BF16)
    A.selfe[...] = dot_bt(A.win3[quarter(mp, RB)], A.We[:, 0:D])
    A.dself[...] = jnp.zeros((RQ, HE), F32)
    load_edge_cot.wait()
    gain_c = jnp.concatenate([A.gain_c[...], jnp.zeros((1, 256 - DE), F32)], axis=1)

    def norm_parts_e(values):
        scale = 1.0 / DE
        mean = jnp.sum(values, axis=-1, keepdims=True) * scale
        centred = jnp.where(is_edge, values - mean, 0.0)
        inverse = lax.rsqrt(jnp.sum(centred * centred, axis=-1, keepdims=True) * scale + EPSILON)
        return centred * inverse, inverse

    chunks = E // EC
    stream = net.reserve(3 * chunks)

    def new_part(q, c):
        return A.new_edges.at[quarter(q), pl.ds(pl.multiple_of(6 * DE * c, 128), 6 * DE)]

    def stream_copies(make, c):
        return (
            make(stream + c, new_part(mp, c), new_part(mp, c), mp=pair),
            make(stream + chunks + c, new_part(mp, c), new_part(mp, c), mp=cross),
            make(stream + 2 * chunks + c, new_part(cross, c), new_part(cross, c), mp=pair),
        )

    def edge_chunk(c, part, gain_out):
        rows = rows_at(EC * c, EC)
        base, pre2, upd, emix, G = (x.at[part] for x in (A.base, A.pre2, A.upd, A.emix, A.G))
        base[...] = dot(A.XO[rows], A.Te[256:768])
        pre2[...] = dot(A.XE[rows], A.Te[0:256])
        yield

        @unrolled(EC // 16)
        def _(b):
            at = slice(16 * b, 16 * b + 16)
            own = 16 * (b % (RQ // 16))
            total = base[at] + A.selfe[own : own + 16]
            base[at] = total
            v = total + pre2[at]
            G[at] = (v * bell(v)).astype(BF16)

        yield
        upd[...] = dot(G[...], A.Eop[...])
        yield
        for j in range(3):
            both = pair_load(A.e_v, pl.multiple_of(1152 * c + 384 * j, 128))
            for p in range(2):
                k = 2 * j + p
                mine = slice(RQ * k, RQ * k + RQ)
                at = rows_at(EC * c + RQ * k, RQ)
                normed, _ = norm_parts_e(both[p] + upd[mine])
                mixed = 0.5 * (both[p] + normed * gain_c)
                emix[mine] = mixed
                A.XM[at] = jnp.where(is_edge, mixed, A.XE[at].astype(F32)).astype(BF16)

        yield
        pre2[...] = dot(A.XM[rows], A.Te[0:256])
        yield

        @unrolled(EC // 16)
        def _(b):
            at = slice(16 * b, 16 * b + 16)
            v = base[at] + pre2[at]
            phi = bell(v)
            A.G2[rows_at(EC * c + 16 * b, 16)] = (v * phi).astype(BF16)
            base[at] = bell_slope(phi, v)

        yield
        upd[...] = dot(A.G2[rows], A.Eop[...])
        yield
        gain_total = jnp.zeros((8, 256), F32)
        for j in range(3):
            lanes = pl.multiple_of(1152 * c + 384 * j, 128)
            cots = pair_load(A.ec_v, lanes)
            news = []
            for p in range(2):
                k = 2 * j + p
                mine = slice(RQ * k, RQ * k + RQ)
                normed, inverse = norm_parts_e(emix[mine] + upd[mine])
                news.append(normed * gain_c)
                gain_total = gain_total + jnp.sum(
                    (cots[p] * normed).reshape(RQ // 8, 8, 256), axis=0
                )
                d_sum = jnp.where(is_edge, norm_back(cots[p], normed, inverse, gain_c, DE), 0.0)
                emix[mine] = d_sum
                A.DO[rows_at(EC * c + RQ * k, RQ)] = d_sum.astype(BF16)
            pair_store(A.new_edges, lanes, news[0], news[1], quarter(mp))
        gain_out.append(gain_total)
        yield
        pre2[...] = dot_bt(A.DO[rows], A.Eop[...])
        yield

        @unrolled(RQ // 16)
        def _(sub):
            own = slice(16 * sub, 16 * sub + 16)
            total = A.dself[own]
            for k in range(6):
                at = slice(RQ * k + 16 * sub, RQ * k + 16 * sub + 16)
                d = (pre2[at] * base[at]).astype(BF16)
                A.DP2[rows_at(EC * c + RQ * k + 16 * sub, 16)] = d
                total = total + d.astype(F32)
            A.dself[own] = total

        yield
        A.EG[rows] = 0.5 * (emix[...] + dot_bt(A.DP2[rows], A.Te[0:256]))

    def send_chunk(c):
        to_pair, to_cross, _ = stream_copies(net.at, c)
        to_cross.start()
        to_pair.start()

        @pl.when(c > 0)
        def _():
            _, arrived, on = stream_copies(net.at, c - 1)
            arrived.wait_recv()
            on.start()

    def edge_chunks(i, gain_total):
        gains = []
        parts = [edge_chunk(2 * i + h, h, gains) for h in range(2)]
        next(parts[0])
        running = list(parts)
        while running:
            for g in list(running):
                try:
                    next(g)
                except StopIteration:
                    running.remove(g)
        for h in range(2):
            send_chunk(2 * i + h)
        return gain_total + gains[0] + gains[1]

    gain_total = lax.fori_loop(0, chunks // 2, edge_chunks, jnp.zeros((8, 256), F32))
    A.gains[...] = jnp.zeros_like(A.gains)
    A.gains[2:3, 0:256] = jnp.sum(gain_total, axis=0, keepdims=True)

    streams = [stream_copies(net.opened, c) for c in range(chunks - 1)]
    last_pair, last_cross, _ = stream_copies(net.opened, chunks - 1)
    on_last = net.remote(new_part(cross, chunks - 1), new_part(cross, chunks - 1), mp=pair)

    A.dself_low[...] = A.dself[...].astype(BF16)
    for q in range(4):
        more = A.dself[:, 4 * big + 128 * (q // 2) : 4 * big + 128 * (q // 2) + 128]
        if q % 2:
            more = pltpu.roll(more, 64, 1)
        A.ds_send[q, :, 0:128] = A.dself_low[:, 128 * q : 128 * q + 128]
        A.ds_send[q, :, 128:256] = more.astype(BF16)
    move_ds = [
        net.remote(A.ds_send.at[peer(d)], A.ds_all.at[quarter(mp)], mp=peer(d)) for d in (1, 2, 3)
    ]
    for c in move_ds:
        c.start()
    late.extend(move_ds)
    A.ds_all[quarter(mp)] = A.ds_send[mp]
    for blk in range(3):
        at = slice(RB * blk, RB * blk + RB)
        A.dq[at] = dot(A.XT[DE + RB * blk : DE + RB * blk + RB], A.DP2[...]).astype(BF16)

    load_node_cot.wait()

    def emit_edge(tile, value):
        for q in range(4):
            at = DE * tile
            A.ge[q, at : at + big] = value[big * q : big * q + big].astype(BF16)
            more = 4 * big + small * q
            A.ge[q, at + big : at + DE] = value[more : more + small].astype(BF16)

    def emit_msg(row, value):
        n = value.shape[0]
        for q in range(4):
            A.gm[q, row : row + n] = value[:, 128 * q : 128 * q + 128].astype(BF16)

    def edge_weight_gradients():
        by_in = dot_at(A.XM[...], A.DP2[...])
        by_out = dot_at(A.DO[...], A.G2[...])
        emit_edge(4, jnp.transpose(by_in[0:128]))
        emit_edge(6, jnp.transpose(by_out[0:128]))
        emit_edge(
            5, jnp.transpose(jnp.concatenate([by_in[128:DE], by_out[128:DE]], axis=0))
        )
        for t in range(4):
            at = slice(128 * t, 128 * t + 128)
            emit_edge(t, jnp.transpose(dot_at(A.win3[:, at], A.dq[...])))
        pump(sum_edge)

    def own_edge_gradients():
        landed(move_ds)
        value = dot_at(A.ds_all[...], A.win3[RB : 2 * RB])
        for t in range(4):
            A.work_e[DE * t : DE * t + DE] = value[0:DE, 128 * t : 128 * t + 128].astype(BF16)

    def message_weight_gradients():
        for t in range(4):
            at = slice(128 * t, 128 * t + 128)
            emit_msg(128 * t, dot_at(A.win2[:, at], A.dq1[...]))
        emit_msg(D, dot(A.XT[0:DE], A.DP[...]))

    def own_message_gradients():
        landed(move_avg)
        landed(move_dg1)
        landed(move_dmsg)
        A.work_m[0:D] = dot_at(A.win2[RB : 2 * RB], A.dmsg_all[...]).astype(BF16)
        value = dot_at(A.avg_all[...], A.dg1_all[...])
        for u in range(4):
            row = 2 * D + DE + 128 * u
            A.work_m[row : row + 128] = value[:, 128 * u : 128 * u + 128].astype(BF16)

    for ref, used in ((A.work_e, 11 * DE), (A.work_m, 3 * D + DE)):
        if ref.shape[0] > used:
            ref[used:] = jnp.zeros((ref.shape[0] - used, 128), BF16)

    def reduce_mp(g, got, cuts, work, base):
        rows = g.shape[1]
        a1 = net.remote(g.at[pair], got.at[0], mp=pair)
        a2 = net.remote(g.at[third], got.at[1], mp=pair)
        a2.start()
        a1.start()
        yield
        a2.wait_recv()

        part = add_step(rows, 16, 128)

        @pl.loop(0, rows // part)
        def _(i):
            at = rows_at(part * i, part)
            got[1, at] = (g[cross, at].astype(F32) + got[1, at].astype(F32)).astype(BF16)

        step = rows // cuts
        pieces = []
        for i in range(cuts):
            at = pl.ds(step * i, step)
            b = net.remote(got.at[1, at], got.at[2, at], mp=cross)
            b.start()
            pieces.append(b)
            yield
        for c in (a1, *pieces):
            c.wait_recv()

        @pl.loop(0, rows // part)
        def _(i):
            at = rows_at(part * i, part)
            total = g[mp, at].astype(F32) + got[0, at].astype(F32) + got[2, at].astype(F32)
            work[rows_at(base + part * i, part)] = total.astype(BF16)

        for c in (a1, a2, *pieces):
            c.wait_send()

    def reduce_res(work, got, out, result, plan):
        size = work.shape[0]
        low = 0
        used = 0
        me = res // stride
        grain = S.grain
        for n, s in enumerate(plan):
            into = out if n == len(plan) - 1 else work
            if s >= 0:
                bit = (res // (1 << s)) % 2
                size = size // 2
                keep = low + bit * size
                give = low + (1 - bit) * size
                copies = [
                    net.remote(
                        work.at[rows_at(give, size, grain)],
                        got.at[pl.ds(used, size)],
                        res=across(s),
                    )
                ]
            else:
                size = size // 4
                keep = low + me * size
                copies = []
                for d in (2, 1, 3):
                    there = (me + d) % 4
                    copies.append(
                        net.remote(
                            work.at[rows_at(low + there * size, size, grain)],
                            got.at[pl.ds(used + (d - 1) * size, size)],
                            res=res + (there - me) * stride,
                        )
                    )
            for c in copies:
                c.start()
            yield
            for c in copies:
                c.wait()

            step = add_step(size, grain, work.shape[1])

            @pl.loop(0, size // step)
            def _(i, keep=keep, used=used, into=into, terms=len(copies), size=size, step=step):
                at = rows_at(keep + step * i, step, grain)
                total = work[at].astype(F32)
                for d in range(terms):
                    total = total + got[rows_at(used + d * size + step * i, step, grain)].astype(F32)
                into[at] = total.astype(BF16)

            used += size * len(copies)
            low = keep
        for s in reversed(plan):
            here = out.at[rows_at(low, size, grain)]
            if s >= 0:
                copies = [net.remote(here, here, res=across(s))]
                low = low - (res // (1 << s)) % 2 * size
                grow = 2
            else:
                copies = [
                    net.remote(here, here, res=res + ((me + d) % 4 - me) * stride)
                    for d in (2, 1, 3)
                ]
                low = low - me * size
                grow = 4
            for c in copies:
                c.start()
            yield
            for c in copies:
                c.wait()
            size = grow * size
        store.append(net.copy(out, result))

    def reduce_gains():
        copies = [net.remote(A.gains, A.gains_r.at[d - 1], mp=peer(d)) for d in (1, 2, 3)]
        for c in copies:
            c.start()
        yield
        for c in copies:
            c.wait()
        A.gains_t[0] = A.gains[...] + A.gains_r[0] + A.gains_r[1] + A.gains_r[2]
        for s in range(S.bits):
            c = net.remote(A.gains_t.at[s], A.gains_r.at[3 + s], res=across(s))
            c.start()
            yield
            c.wait()
            A.gains_t[s + 1] = A.gains_t[s] + A.gains_r[3 + s]
        store.append(net.copy(A.gains_t.at[S.bits], A.out_gains))

    def chain(*parts):
        for part in parts:
            yield from part

    def pump(*sums):
        for g in sums:
            next(g, None)

    sum_edge = chain(
        reduce_mp(A.ge, A.ge_r, 2, A.work_e, 4 * DE),
        reduce_res(A.work_e, A.sum_er, A.sum_e, A.pack_e, plans(S.bits)[0]),
    )
    sum_in = reduce_res(A.grad_i, A.sum_ir, A.sum_i, A.pack_i, plans(S.bits)[1])
    sum_out = reduce_res(A.grad_o, A.sum_or, A.sum_o, A.pack_o, plans(S.bits)[2])
    sum_msg = chain(
        reduce_mp(A.gm, A.gm_r, 1, A.work_m, D),
        reduce_res(A.work_m, A.sum_mr, A.sum_m, A.pack_m, plans(S.bits)[3]),
    )
    sum_gains = reduce_gains()

    def between_a():
        last_cross.wait_recv()
        on_last.start()
        pump(sum_edge)
        own_edge_gradients()

    d_settled = A.nc_v[...] + dot(A.dself_low[...], A.We[:, 0:D])
    d_settled = d_settled + return_rows(
        lambda blk: dot(A.dq[RB * blk : RB * blk + RB], A.We[:, D : 2 * D]),
        A.back_send_a,
        A.back_recv_a,
        A.back_side_send_a,
        A.back_side_a,
        edge_weight_gradients,
        between_a,
    )

    normed_b = A.normed_b[...]
    d_sum_b = norm_back(d_settled, normed_b, A.inverse_b[:, 0:1], gain_b, D)
    A.gains[1:2] = jnp.sum(d_settled * normed_b, axis=0, keepdims=True)
    A.dF[quarter(mp)] = d_sum_b.astype(BF16)
    moved = gather_rows(A.dF)
    landed(moved)
    late.extend(moved)
    A.hid[...] = dot_bt(A.dF[...], A.fo_v[...])

    @unrolled(RB // 16)
    def _(i):
        rows = rows_at(16 * i, 16)
        A.dT[rows] = (A.hid[rows] * A.hslope[rows]).astype(BF16)

    A.part[...] = dot_bt(A.dT[...], A.fi_v[...])
    A.pb3[...] = A.part[...].astype(BF16)
    moved = scatter_sum_start(A.pb3, A.pr3)
    pump(sum_edge)
    A.grad_i[...] = dot_at(A.ug2[...], A.dT[...]).astype(BF16)
    pump(sum_in)
    A.grad_o[...] = dot_at(A.smooth[...], A.dF[...]).astype(BF16)
    pump(sum_out)
    d_middle = d_sum_b + A.part[quarter(mp)]
    landed(moved)
    late.extend(moved)
    for d in range(3):
        d_middle = d_middle + A.pr3[d].astype(F32)
    normed_a = A.normed_a[...]
    d_sum_a = norm_back(d_middle, normed_a, A.inverse_a[:, 0:1], gain_a, D)
    A.gains[0:1] = jnp.sum(d_middle * normed_a, axis=0, keepdims=True)
    pump(sum_gains)
    A.dsa[...] = d_sum_a
    A.dg1[...] = d_sum_a.astype(BF16)
    A.dg1_all[quarter(mp)] = A.dg1[...]
    move_dg1 = gather_rows(A.dg1_all)
    late.extend(move_dg1)
    A.davg[...] = dot_bt(A.dg1[...], A.Wo[...])

    for sub in range(RQ // 16):
        mine = A.davg[16 * sub : 16 * sub + 16]

        def back_step(k, total, sub=sub, mine=mine):
            rows = rows_at(RQ * k + 16 * sub, 16)
            d = (mine * A.slope[rows].astype(F32)).astype(BF16)
            A.DP[rows] = d
            return total + d.astype(F32)

        total = lax.fori_loop(0, K, back_step, jnp.zeros((16, HM), F32), unroll=4)
        A.dmsg_low[16 * sub : 16 * sub + 16] = total.astype(BF16)

    move_dmsg = spread_columns(A.dmsg_low, A.dmsg_all)
    pump(sum_edge)
    for blk in range(3):
        at = slice(RB * blk, RB * blk + RB)
        A.dq1[at] = dot(A.XT[DE + RB * blk : DE + RB * blk + RB], A.DP[...]).astype(BF16)

    pump(sum_in, sum_out)
    message_weight_gradients()
    pump(sum_msg, sum_gains)
    own_message_gradients()
    pump(sum_msg)

    def edge_gradient(start, stop):
        @pl.loop(start, stop)
        def _(c):
            rows = rows_at(EC * c, EC)
            A.EG[rows] = A.EG[rows] + dot_bt(A.DP[rows], A.T[0:256])
            for j in range(3):
                lanes = pl.multiple_of(1152 * c + 384 * j, 128)
                ends = [
                    jnp.where(is_edge, A.EG[rows_at(EC * c + RQ * (2 * j + p), RQ)], 0.0)
                    for p in range(2)
                ]
                pair_store(A.ec_v, lanes, ends[0], ends[1])

    def close_edges():
        store.append(net.copy(A.ec_v, A.out_edge_grad))
        for a, b, c in streams:
            a.wait()
            b.wait_send()
            c.wait()
        last_pair.wait()
        last_cross.wait_send()
        on_last.wait()
        store.append(net.copy(A.new_edges, A.out_edges))

    def fill_b():
        edge_gradient(0, 3)
        pump(sum_in, sum_out, sum_gains)
        edge_gradient(3, chunks)
        pump(sum_msg, sum_edge)

    back = return_rows(
        lambda blk: dot_bt(A.dq1[RB * blk : RB * blk + RB], A.Wm[D : 2 * D]),
        A.back_send_b,
        A.back_recv_b,
        A.back_side_send_b,
        A.back_side_b,
        fill_b,
        lambda: pump(sum_in, sum_out, sum_gains),
    )
    A.node_grad_v[...] = 0.5 * (A.dsa[...] + dot_bt(A.dmsg_low[...], A.Wm[0:D]) + back)
    store.append(net.copy(A.node_grad_v, A.out_node_grad))

    pump(sum_edge, sum_msg)
    close_edges()
    work = [sum_msg, sum_edge, sum_in, sum_out, sum_gains]
    while work:
        for g in list(work):
            try:
                next(g)
            except StopIteration:
                work.remove(g)
    for c in store:
        c.wait()
    for s in (spread_msg_in, spread_msg_out, *spread_edge, halo, window2, window3):
        s.sent()
    for c in late:
        c.wait_send()
    assert net.remote_count <= S.remote and net.local_count <= S.local


def build(S):
    E = S.RQ * S.K
    W = 3 * S.RB
    EC = 6 * S.RQ
    grain = S.grain * S.n_res
    rows_e = up(11 * S.DE, grain)
    rows_m = up(3 * S.D + S.DE, grain)
    in_names = ["nodes", "edges", "neighbours", "edge_mask", "msg_in", "msg_out", "gain_a"]
    in_names += ["ffn_in", "ffn_out", "gain_b", "edge_in", "edge_out", "gain_c"]
    in_names += ["node_cot", "edge_cot"]
    outs = dict(
        out_nodes=((S.RB, S.D), BF16),
        out_edges=((S.RB, S.K * S.DE), BF16),
        out_node_grad=((S.RQ, S.D), F32),
        out_edge_grad=((S.RQ, S.K * S.DE), F32),
        pack_e=((rows_e, 128), BF16),
        pack_i=((S.D, S.FL), BF16),
        pack_o=((S.FL, S.D), BF16),
        pack_m=((rows_m, 128), BF16),
        out_gains=((8, S.D), F32),
    )
    scratch = dict(
        nodes_v=((S.RB, S.D), F32),
        nbr_v=((S.K, S.RB), jnp.int32),
        mask_v=((S.K, S.RB), jnp.int32),
        columns=((S.RB, 128), F32),
        new_edges=((S.RB, S.K * S.DE), BF16),
        node_grad_v=((S.RQ, S.D), F32),
        e_v=((S.RQ, S.K * S.DE), F32),
        ec_v=((S.RQ, S.K * S.DE), F32),
        nc_v=((S.RQ, S.D), F32),
        Wm=((2 * S.D + S.DE, S.HM), BF16),
        Wo=((S.HM, S.D), BF16),
        fi_v=((S.D, S.FL), BF16),
        fo_v=((S.FL, S.D), BF16),
        We=((S.HE, 2 * S.D + S.DE), BF16),
        Eo=((S.HE, S.DE), BF16),
        Eop=((S.HE, 256), BF16),
        win1=((W, S.D), BF16),
        win2=((W, S.D), BF16),
        win3=((W, S.D), BF16),
        XE=((E, 256), BF16),
        XM=((E, 256), BF16),
        XO=((E, 512), BF16),
        XT=((768, E), BF16),
        WB=((E, 128), F32),
        T=((768, S.HM), BF16),
        Te=((768, S.HE), BF16),
        selfs=((S.RQ, S.HM), F32),
        selfe=((S.RQ, S.HE), F32),
        total=((S.RQ, S.HM), F32),
        slope=((E, S.HM), BF16),
        avg=((S.RQ, S.HM), BF16),
        ug1=((S.RB, S.D), BF16),
        ug2=((S.RB, S.D), BF16),
        hid=((S.RB, S.FL), F32),
        smooth=((S.RB, S.FL), BF16),
        hslope=((S.RB, S.FL), F32),
        part=((S.RB, S.D), F32),
        pb1=((S.RB, S.D), BF16),
        pb2=((S.RB, S.D), BF16),
        pb3=((S.RB, S.D), BF16),
        pr1=((3, S.RQ, S.D), BF16),
        pr2=((3, S.RQ, S.D), BF16),
        pr3=((3, S.RQ, S.D), BF16),
        normed_a=((S.RQ, S.D), F32),
        normed_b=((S.RQ, S.D), F32),
        inverse_a=((S.RQ, 128), F32),
        inverse_b=((S.RQ, 128), F32),
        mixed=((S.RQ, S.D), F32),
        pre=((EC, S.HM), F32),
        base=((2, EC, S.HE), F32),
        pre2=((2, EC, S.HE), F32),
        G=((2, EC, S.HE), BF16),
        upd=((2, EC, 256), F32),
        emix=((2, EC, 256), F32),
        G2=((E, S.HE), BF16),
        DO=((E, 256), BF16),
        DP2=((E, S.HE), BF16),
        EG=((E, 256), F32),
        dself=((S.RQ, S.HE), F32),
        dself_low=((S.RQ, S.HE), BF16),
        dq=((W, S.HE), BF16),
        gains=((8, S.D), F32),
        gains_r=((3 + S.bits, 8, S.D), F32),
        gains_t=((1 + S.bits, 8, S.D), F32),
        back_send_a=((4, 3, S.RQ, S.D), BF16),
        back_recv_a=((3, 3, S.RQ, S.D), BF16),
        back_side_send_a=((2, S.RQ, S.D), BF16),
        back_side_a=((2, S.RQ, S.D), BF16),
        back_send_b=((4, 3, S.RQ, S.D), BF16),
        back_recv_b=((3, 3, S.RQ, S.D), BF16),
        back_side_send_b=((2, S.RQ, S.D), BF16),
        back_side_b=((2, S.RQ, S.D), BF16),
        dF=((S.RB, S.D), BF16),
        dT=((S.RB, S.FL), BF16),
        dsa=((S.RQ, S.D), F32),
        dg1=((S.RQ, S.D), BF16),
        davg=((S.RQ, S.HM), F32),
        DP=((E, S.HM), BF16),
        dmsg_low=((S.RQ, S.HM), BF16),
        dq1=((W, S.HM), BF16),
        ge=((4, 7 * S.DE, 128), BF16),
        ge_r=((3, 7 * S.DE, 128), BF16),
        work_e=((rows_e, 128), BF16),
        ds_send=((4, S.RQ, 256), BF16),
        ds_all=((S.RB, 256), BF16),
        avg_all=((S.RB, 128), BF16),
        dg1_all=((S.RB, S.D), BF16),
        dmsg_all=((S.RB, 128), BF16),
        sum_er=((rows_e, 128), BF16),
        sum_e=((rows_e, 128), BF16),
        grad_i=((S.D, S.FL), BF16),
        sum_ir=((S.D, S.FL), BF16),
        sum_i=((S.D, S.FL), BF16),
        grad_o=((S.FL, S.D), BF16),
        sum_or=((S.FL, S.D), BF16),
        sum_o=((S.FL, S.D), BF16),
        gm=((4, S.D + S.DE, 128), BF16),
        gm_r=((3, S.D + S.DE, 128), BF16),
        work_m=((rows_m, 128), BF16),
        sum_mr=((rows_m, 128), BF16),
        sum_m=((rows_m, 128), BF16),
    )
    names = list(scratch) + ["send", "recv", "local"]
    shapes = [pltpu.VMEM(*v) for v in scratch.values()] + [
        pltpu.SemaphoreType.DMA((S.remote,)),
        pltpu.SemaphoreType.DMA((S.remote,)),
        pltpu.SemaphoreType.DMA((S.local,)),
    ]
    body = functools.partial(kernel_body, S, in_names, list(outs), names)
    body.__name__ = "layer"
    gains = ("gain_a", "gain_b", "gain_c")
    return pl.pallas_call(
        body,
        name="layer",
        out_shape=[jax.ShapeDtypeStruct(*v) for v in outs.values()],
        in_specs=[VMEM if n in gains else ANY for n in in_names],
        out_specs=[ANY] * len(outs),
        scratch_shapes=shapes,
        compiler_params=pltpu.CompilerParams(
            collective_id=0, has_side_effects=True, vmem_limit_bytes=62 * 1024 * 1024
        ),
    )


def unpack_body(S, names, *refs):
    A = SimpleNamespace(**dict(zip(names, refs, strict=True)))
    D, DE, RB = S.D, S.DE, S.RB
    count = [0]

    def copy(src, dst):
        c = pltpu.make_async_copy(src, dst, A.sems.at[count[0]])
        count[0] += 1
        c.start()
        return c

    part = RB // 4
    edge_loads = [
        copy(A.in_edges.at[pl.ds(part * i, part)], A.edges_l.at[pl.ds(part * i, part)])
        for i in range(4)
    ]
    pairs = (
        (A.in_e, A.e_l),
        (A.in_i, A.i_l),
        (A.in_o, A.o_l),
        (A.in_m, A.m_l),
        (A.in_nodes, A.nodes_l),
        (A.in_gains, A.gains_l),
    )
    loads = [copy(*p) for p in pairs]
    grads = [copy(A.in_edge_grad, A.eg_l), copy(A.in_node_grad, A.ng_l)]
    stores = []
    for i in range(4):
        edge_loads[i].wait()

        @pl.loop(0, part // 16)
        def _(k, i=i):
            at = pl.ds(pl.multiple_of(part * i + 16 * k, 16), 16)
            A.edges_f[at] = A.edges_l[at].astype(F32)

        at = pl.ds(part * i, part)
        stores.append(copy(A.edges_f.at[at], A.o1.at[at]))
    for c in (*grads, *loads):
        c.wait()
    stores += [copy(A.eg_l, A.o3), copy(A.ng_l, A.o2)]

    def widen(src, dst, out, rows):
        dst[...] = src[0:rows].astype(F32)
        stores.append(copy(dst, out))

    widen(A.i_l, A.i_f, A.o7, D)
    widen(A.o_l, A.o_f, A.o8, S.FL)
    widen(A.nodes_l, A.nodes_f, A.o0, RB)
    widen(A.m_l, A.m_f, A.o4, 2 * D + DE)
    for u in range(4):
        row = 2 * D + DE + 128 * u
        A.mo_f[:, 128 * u : 128 * u + 128] = A.m_l[row : row + 128].astype(F32)
    stores.append(copy(A.mo_f, A.o5))
    mixed = A.e_l[9 * DE : 10 * DE].astype(F32)
    for t in range(9):
        A.ei_f[:, 128 * t : 128 * t + 128] = A.e_l[DE * t : DE * t + DE].astype(F32)
    A.ei_f[:, 1152 : 1152 + 64] = mixed[:, 0:64]
    stores.append(copy(A.ei_f, A.o10))
    A.eo_f[:, 0:128] = A.e_l[10 * DE : 11 * DE].astype(F32)
    A.eo_f[:, 128:DE] = pltpu.roll(mixed, 64, 1)[:, 0:64]
    stores.append(copy(A.eo_f, A.o11))
    A.ga_f[...] = A.gains_l[0:1]
    A.gb_f[...] = A.gains_l[1:2]
    A.gc_f[...] = A.gains_l[2:3, 0:DE]
    for src, out in ((A.ga_f, A.o6), (A.gb_f, A.o9), (A.gc_f, A.o12)):
        stores.append(copy(src, out))
    for c in stores:
        c.wait()


def unpack(S, values):
    D, DE, RB, RQ, K, FL = S.D, S.DE, S.RB, S.RQ, S.K, S.FL
    ins = ["in_nodes", "in_edges", "in_node_grad", "in_edge_grad"]
    ins += ["in_e", "in_i", "in_o", "in_m", "in_gains"]
    shapes = [
        (RB, D),
        (RB, K * DE),
        (RQ, D),
        (RQ, K * DE),
        (2 * D + DE, S.HM // 4),
        (S.HM // 4, D),
        (1, D),
        (D, FL),
        (FL, D),
        (1, D),
        (S.HE // 4, 2 * D + DE),
        (S.HE // 4, DE),
        (1, DE),
    ]
    outs = ["o%d" % i for i in range(13)]
    scratch = dict(
        edges_l=((RB, K * DE), BF16),
        edges_f=((RB, K * DE), F32),
        e_l=(values[4].shape, BF16),
        i_l=((D, FL), BF16),
        o_l=((FL, D), BF16),
        m_l=(values[7].shape, BF16),
        nodes_l=((RB, D), BF16),
        gains_l=((8, D), F32),
        eg_l=((RQ, K * DE), F32),
        ng_l=((RQ, D), F32),
        i_f=((D, FL), F32),
        o_f=((FL, D), F32),
        nodes_f=((RB, D), F32),
        m_f=(shapes[4], F32),
        mo_f=(shapes[5], F32),
        ei_f=(shapes[10], F32),
        eo_f=(shapes[11], F32),
        ga_f=(shapes[6], F32),
        gb_f=(shapes[9], F32),
        gc_f=(shapes[12], F32),
    )
    names = ins + outs + list(scratch) + ["sems"]
    body = functools.partial(unpack_body, S, names)
    return list(
        pl.pallas_call(
            body,
            name="unpack",
            out_shape=[jax.ShapeDtypeStruct(x, F32) for x in shapes],
            in_specs=[ANY] * len(ins),
            out_specs=[ANY] * len(outs),
            scratch_shapes=[pltpu.VMEM(*v) for v in scratch.values()]
            + [pltpu.SemaphoreType.DMA((32,))],
            compiler_params=pltpu.CompilerParams(vmem_limit_bytes=62 * 1024 * 1024),
        )(*values)
    )


STOP = 0


def plans(bits):
    low = list(range(bits - 2))
    high = [bits - 2, bits - 1]
    return [low + [-1], low + high, high + low, low + [-1]]


def on_device(n_res, *args):
    nodes, edges, neighbours, _, _, _, _, ffn_in = args[:8]
    height = nodes.shape[0]
    degree = neighbours.shape[1]
    S = SimpleNamespace(
        n_res=n_res,
        bits=int(math.log2(n_res)),
        RB=height,
        RQ=height // 4,
        K=degree,
        D=nodes.shape[1],
        DE=edges.shape[1] // degree,
        HM=args[4].shape[1] * 4,
        HE=args[10].shape[1] * 4,
        FL=ffn_in.shape[1],
        grain=16 if n_res <= 16 else 8,
        remote=200,
        local=32,
        stop=STOP,
    )
    fixed = [a.reshape(1, -1) if a.ndim == 1 else a for a in args]
    for i in (2, 3, 10):
        fixed[i] = fixed[i].T
    out = unpack(S, build(S)(*fixed))
    for i in (6, 9, 12):
        out[i] = out[i].reshape(-1)
    out[10] = out[10].T
    return tuple(out)


def solution(mesh):
    in_specs = (
        P("res", None),
        P("res", None),
        P("res", None),
        P("res", None),
        P(None, "mp"),
        P("mp", None),
        P(),
        P(None, "mp"),
        P("mp", None),
        P(),
        P(None, "mp"),
        P("mp", None),
        P(),
        P("res", None),
        P("res", None),
    )
    out_specs = (
        P("res", None),
        P("res", None),
        P(("res", "mp"), None),
        P(("res", "mp"), None),
        P(None, "mp"),
        P("mp", None),
        P(),
        P(None, "mp"),
        P("mp", None),
        P(),
        P(None, "mp"),
        P("mp", None),
        P(),
    )
    return jax.shard_map(
        functools.partial(on_device, mesh.shape["res"]),
        mesh=mesh,
        in_specs=in_specs,
        out_specs=out_specs,
        check_vma=False,
    )
```
